32 devices in a mesh: dp: 8 (over z, x), seq: 4 (over y, core).
Axes of the slice: x: 2, y: 2, z: 4, core: 2. Of those that a mesh axis runs over, the one named last changes fastest.
Arguments:
- layer_input: bfloat16 [16384, 768], P(('dp', 'seq')), may hold values from -6 to 6
- query_weight: bfloat16 [768, 768], replicated, may hold values from -0.3125 to 0.3125
- query_bias: float32 [768], replicated, may hold values from -3 to 3
- key_weight: bfloat16 [768, 768], replicated, may hold values from -0.3125 to 0.3125
- value_weight: bfloat16 [768, 768], replicated, may hold values from -0.21875 to 0.21875
- value_bias: float32 [768], replicated, may hold values from -3 to 3
- output_weight: bfloat16 [768, 768], replicated, may hold values from -1.25 to 1.25
- output_bias: float32 [768], replicated, may hold values from -1.75 to 1.75
- first_gain: float32 [768], replicated, may hold values from 0.25 to 1.75
- first_shift: float32 [768], replicated, may hold values from -1.75 to 1.75
- up_weight: bfloat16 [768, 3072], replicated, may hold values from -0.21875 to 0.21875
- up_bias: float32 [3072], replicated, may hold values from -3 to 3
- down_weight: bfloat16 [3072, 768], replicated, may hold values from -0.109375 to 0.109375
- down_bias: float32 [768], replicated, may hold values from -1.75 to 1.75
- second_gain: float32 [768], replicated, may hold values from 0.25 to 1.75
- second_shift: float32 [768], replicated, may hold values from -1.75 to 1.75
- out_cotangent: bfloat16 [16384, 768], P(('dp', 'seq')), may hold values from -6 to 6
- passage_lengths: int32 [8, 8], P('dp'), may hold values from 1 to 512, 2048 in all within a row
Outputs:
- layer_output: bfloat16 [16384, 768], P(('dp', 'seq'))
- input_grad: bfloat16 [16384, 768], P(('dp', 'seq'))
- query_weight_grad: float32 [768, 768], P(('dp', 'seq'))
- query_bias_grad: float32 [768], P(('dp', 'seq'))
- key_weight_grad: float32 [768, 768], P(('dp', 'seq'))
- value_weight_grad: float32 [768, 768], P(('dp', 'seq'))
- value_bias_grad: float32 [768], P(('dp', 'seq'))
- output_weight_grad: float32 [768, 768], P(('dp', 'seq'))
- output_bias_grad: float32 [768], P(('dp', 'seq'))
- first_gain_grad: float32 [768], P(('dp', 'seq'))
- first_shift_grad: float32 [768], P(('dp', 'seq'))
- up_weight_grad: float32 [768, 3072], P(('dp', 'seq'))
- up_bias_grad: float32 [3072], P(('dp', 'seq'))
- down_weight_grad: float32 [3072, 768], P(('dp', 'seq'))
- down_bias_grad: float32 [768], P(('dp', 'seq'))
- second_gain_grad: float32 [768], P(('dp', 'seq'))
- second_shift_grad: float32 [768], P(('dp', 'seq'))
The draws below stay inside these ranges and needn't reach their ends.
Inputs may be any that keep to these rules, and one draw needn't show every extreme that they name: `passage_lengths`: each row lists the passages of one group in order; a row sums to 2048 and its longest passage has exactly 512 tokens.
All inputs are finite; a program needn't handle non-finite values.
Results may differ from the reference program's by a relative error of at most 0.015.
The reference program's roundings to bfloat16 on the way count: a program that leaves them out, or rounds other values in their place, can miss the bound.
Values may be sent and summed in bfloat16 or wider, within the bound.
A program may use at most 192 MiB of HBM per device.

```python
import math
import jax
import jax.numpy as jnp
import numpy as np
from jax import lax

D = 768
HEADS = 12
HEAD_DIM = 64
FF = 3072
MAXLEN = 512
GROUP = 2048
SLOTS = 8
GROUPS = 8
TOKENS = 16384


def strengthened(values, rng, source, target, parts, factor):
    def block_of(axis_at):
        return (jnp.arange(values.shape[axis_at]) // (values.shape[axis_at] // parts)).reshape((-1,) + (1,) * (values.ndim - 1 - axis_at))

    one_side = jax.random.permutation(rng, parts)[block_of(target)]
    other_side = (block_of(target) + parts // 2) % parts
    return jnp.where((block_of(source) == one_side) | (block_of(source) == other_side), factor * values, values)


def shard_levels(key, dims, shards, low, high):
    def one(position, blocks):
        draws = jax.random.uniform(jax.random.fold_in(jax.random.fold_in(key, 6), position), (blocks,), jnp.float32, low / len(shards), high / len(shards))
        return jnp.repeat(jnp.exp(draws), dims[position] // blocks).reshape((-1,) + (1,) * (len(dims) - position - 1))

    level = one(*shards[0])
    for cut in shards[1:]:
        level = level * one(*cut)
    return level


def profile(number_of, total, reach, skew):
    loads = [(1 << 20) // math.isqrt(standing ** skew) + 1 for standing in range(2, number_of + 1)]
    rest, given = total - reach - (number_of - 1), [1] * (number_of - 1)
    while rest > 0:
        free = [i for i in range(number_of - 1) if given[i] < reach]
        whole, left = sum([loads[i] for i in free]), rest
        for i in free:
            addition = min(reach - given[i], max(1, left * loads[i] // whole), rest)
            given[i] = given[i] + addition
            rest = rest - addition
    return np.array([reach] + given)


def uneven_parts(stream_key, count, total, limit, skew):
    if count == 2:
        one = jax.random.randint(stream_key, (), max(1, total - limit), min(limit, total - 1) + 1)
        return jnp.stack([one, total - one])
    sizes = jnp.asarray(profile(count, total, limit, skew), jnp.int32)
    couples = (count - 1) // 2
    giver, sink = sizes[1:1 + 2 * couples:2], sizes[2:2 + 2 * couples:2]
    margin = jnp.minimum(giver - 1, limit - sink)
    moved = jax.random.randint(jax.random.fold_in(stream_key, 1), (couples,), 0, 1 << 20) % (margin + 1)
    sizes = sizes.at[1:1 + 2 * couples:2].set(giver - moved).at[2:2 + 2 * couples:2].set(sink + moved)
    return sizes[jax.random.permutation(jax.random.fold_in(stream_key, 2), count)]


def scatter_about(key, extent, scale, bound, shards=(), held_as=jnp.bfloat16):
    entries = scale * jax.random.normal(key, extent, jnp.float32)
    if shards:
        entries = entries * shard_levels(key, extent, shards, -0.22, 0.18)
    return jnp.clip(entries, -bound, bound).astype(held_as)


def heavy_noise(own_key, shape, scale, reach, pieces, heavy, kind=jnp.bfloat16):
    values = scale * jax.random.normal(own_key, shape, jnp.float32)
    if pieces:
        values = values * shard_levels(own_key, shape, pieces, -0.22, 0.18)
    return jnp.clip(strengthened(values, jax.random.fold_in(own_key, 3), *heavy), -reach, reach).astype(kind)


def setup_inputs(seed: int = 0) -> dict:
    key_of = jax.random.split(jax.random.key(seed), 19)
    layer_input = heavy_noise(key_of[0], (TOKENS, D), 1.0, 6.0, ((0, 32),), (0, 1, 32, 2.75))
    query_weight = scatter_about(key_of[1], (D, D), (D // 2) ** -0.5, 0.3125)
    query_bias = scatter_about(key_of[2], (D,), 0.5, 3.0, (), jnp.float32)
    key_weight = scatter_about(key_of[3], (D, D), (D // 2) ** -0.5, 0.3125)
    value_weight = scatter_about(key_of[4], (D, D), D ** -0.5, 0.21875)
    value_bias = scatter_about(key_of[5], (D,), 0.5, 3.0, (), jnp.float32)
    output_weight = scatter_about(key_of[6], (D, D), (D // 32) ** -0.5, 1.25)
    output_bias = scatter_about(key_of[7], (D,), 0.3, 1.75, (), jnp.float32)
    first_gain = jnp.clip(1.0 + 0.15 * jax.random.normal(key_of[8], (D,), jnp.float32), 0.25, 1.75)
    first_shift = scatter_about(key_of[9], (D,), 0.3, 1.75, (), jnp.float32)
    up_weight = scatter_about(key_of[10], (D, FF), D ** -0.5, 0.21875)
    up_bias = scatter_about(key_of[11], (FF,), 0.5, 3.0, (), jnp.float32)
    down_weight = scatter_about(key_of[12], (FF, D), FF ** -0.5, 0.109375)
    down_bias = scatter_about(key_of[13], (D,), 0.3, 1.75, (), jnp.float32)
    second_gain = jnp.clip(1.0 + 0.15 * jax.random.normal(key_of[14], (D,), jnp.float32), 0.25, 1.75)
    second_shift = scatter_about(key_of[15], (D,), 0.3, 1.75, (), jnp.float32)
    out_cotangent = heavy_noise(key_of[16], (TOKENS, D), 1.0, 6.0, ((0, 32),), (0, 1, 32, 2.75))
    passage_lengths = jax.vmap(lambda own: uneven_parts(own, SLOTS, GROUP, MAXLEN, 2))(jax.random.split(key_of[17], GROUPS)).reshape((GROUPS, SLOTS)).astype(jnp.int32)
    return dict(layer_input=layer_input, query_weight=query_weight, query_bias=query_bias, key_weight=key_weight, value_weight=value_weight, value_bias=value_bias, output_weight=output_weight, output_bias=output_bias, first_gain=first_gain, first_shift=first_shift, up_weight=up_weight, up_bias=up_bias, down_weight=down_weight, down_bias=down_bias, second_gain=second_gain, second_shift=second_shift, out_cotangent=out_cotangent, passage_lengths=passage_lengths)


layer_eps = 1e-12
masked_score = -1000000000.0

@jax.custom_vjp
def low(v):
    return lax.optimization_barrier(v.astype(jnp.bfloat16)).astype(jnp.float32)

@jax.custom_vjp
def low_back(v):
    return v

def low_keep(v):
    return (low(v), None)

def low_pass(kept, grad):
    return (grad,)

def back_keep(v):
    return (v, None)

def back_low(kept, grad):
    return (low(grad),)
low.defvjp(low_keep, low_pass)
low_back.defvjp(back_keep, back_low)

def matmul(left, right):
    return jnp.dot(left, right, precision=lax.Precision.HIGHEST, preferred_element_type=jnp.float32)

def layer_norm(hidden, gain, shift):
    mean = lax.optimization_barrier(jnp.mean(hidden, axis=-1, keepdims=True))
    centred = hidden - mean
    variance = lax.optimization_barrier(jnp.mean(centred * centred, axis=-1, keepdims=True))
    return centred * lax.rsqrt(variance + layer_eps) * gain + shift

def segment_ids(lengths_row, count):
    ends = jnp.cumsum(lengths_row.astype(jnp.int32)).astype(jnp.int32)
    positions = jnp.arange(count, dtype=jnp.int32)
    return lax.optimization_barrier(jnp.sum((positions[:, None] >= ends[None, :]).astype(jnp.int32), axis=1)).astype(jnp.int32)

def attention(queries, key_rows, value_rows, segment):
    count = queries.shape[0]
    block = min(512, count)
    blocks = count // block
    scale = HEAD_DIM ** (-0.5)
    query_blocks = queries.reshape(blocks, block, HEADS, HEAD_DIM)
    seg_blocks = segment.reshape(blocks, block)

    def one_block(packed):
        query_block, seg_block = packed
        raw = jnp.einsum('qhd,khd->hqk', query_block, key_rows, precision=lax.Precision.HIGHEST)
        same = seg_block[:, None] == segment[None, :]
        scores = low_back(jnp.where(same[None], raw * scale, masked_score))
        probs = jax.nn.softmax(scores, axis=-1)
        return jnp.einsum('hqk,khd->qhd', low(probs), value_rows, precision=lax.Precision.HIGHEST)
    result = lax.map(jax.checkpoint(one_block), (query_blocks, seg_blocks))
    return result.reshape(count, HEADS * HEAD_DIM)

def layer(params, inputs, segment):
    query_weight, query_bias, key_weight, value_weight, value_bias, output_weight, output_bias, first_gain, first_shift, up_weight, up_bias, down_weight, down_bias, second_gain, second_shift = params
    count = inputs.shape[0]
    queries = low_back(low(matmul(inputs, query_weight) + query_bias))
    key_rows = low_back(low(matmul(inputs, key_weight)))
    value_rows = low_back(low(matmul(inputs, value_weight) + value_bias))
    context = attention(queries.reshape(count, HEADS, HEAD_DIM), key_rows.reshape(count, HEADS, HEAD_DIM), value_rows.reshape(count, HEADS, HEAD_DIM), segment)
    context = low_back(low(context))
    attended = low_back(matmul(context, output_weight) + output_bias)
    normed = layer_norm(inputs + attended, first_gain, first_shift)
    up_pre = low_back(matmul(low(normed), up_weight) + up_bias)
    hidden = low(jax.nn.gelu(up_pre, approximate=False))
    branch = low_back(matmul(hidden, down_weight) + down_bias)
    return layer_norm(normed + branch, second_gain, second_shift)

def reference(layer_input, query_weight, query_bias, key_weight, value_weight, value_bias, output_weight, output_bias, first_gain, first_shift, up_weight, up_bias, down_weight, down_bias, second_gain, second_shift, out_cotangent, passage_lengths):
    params = (query_weight.astype(jnp.float32), query_bias.astype(jnp.float32), key_weight.astype(jnp.float32), value_weight.astype(jnp.float32), value_bias.astype(jnp.float32), output_weight.astype(jnp.float32), output_bias.astype(jnp.float32), first_gain.astype(jnp.float32), first_shift.astype(jnp.float32), up_weight.astype(jnp.float32), up_bias.astype(jnp.float32), down_weight.astype(jnp.float32), down_bias.astype(jnp.float32), second_gain.astype(jnp.float32), second_shift.astype(jnp.float32))
    groups = passage_lengths.shape[0]
    count = layer_input.shape[0] // groups
    inputs = layer_input.astype(jnp.float32).reshape(groups, count, D)
    cotangents = out_cotangent.astype(jnp.float32).reshape(groups, count, D)

    def one_group(totals, packed):
        rows_in, rows_grad, lengths_row = packed
        segment = segment_ids(lengths_row, count)

        def apply(weights, values):
            return layer(weights, values, segment)
        result, pullback = jax.vjp(apply, params, rows_in)
        weight_grads, row_grads = pullback(rows_grad)
        totals = jax.tree.map(jnp.add, totals, weight_grads)
        return (totals, (result.astype(jnp.bfloat16), row_grads.astype(jnp.bfloat16)))
    zeros = jax.tree.map(jnp.zeros_like, params)
    totals, (outputs, grads) = lax.scan(one_group, zeros, (inputs, cotangents, passage_lengths))
    return (outputs.reshape(groups * count, D), grads.reshape(groups * count, D), totals[0], totals[1], totals[2], totals[3], totals[4], totals[5], totals[6], totals[7], totals[8], totals[9], totals[10], totals[11], totals[12], totals[13], totals[14])
```

```python
import functools

import jax
import jax.numpy as jnp
from jax import lax
from jax.experimental import pallas as pl
from jax.experimental.pallas import tpu as pltpu
from jax.sharding import PartitionSpec as P

HEAD_DIM = 64
PAIR = 2 * HEAD_DIM
AXES = ("dp", "seq")
NEG = -1e30
FLOOR = -3e38
BQ = 256
BK = 256
LEVELS = 5
layer_eps = 1e-12
F32 = jnp.float32
BF16 = jnp.bfloat16


def nn(a, b):
    return lax.dot_general(a, b, (((1,), (0,)), ((), ())), preferred_element_type=F32)


def nt(a, b):
    return lax.dot_general(a, b, (((1,), (1,)), ((), ())), preferred_element_type=F32)


def tn(a, b):
    return lax.dot_general(a, b, (((0,), (0,)), ((), ())), preferred_element_type=F32)


def cost(flops, nbytes, trans=0):
    return pl.CostEstimate(flops=int(flops), bytes_accessed=int(nbytes), transcendentals=int(trans))


def params(limit=56 << 20):
    return pltpu.CompilerParams(vmem_limit_bytes=limit)


def whole():
    return pl.BlockSpec(memory_space=pltpu.VMEM)


def hbm():
    return pl.BlockSpec(memory_space=pl.ANY)


def low_lanes():
    return lax.broadcasted_iota(jnp.int32, (1, PAIR), 1) < HEAD_DIM


def qkv_kernel(x_ref, wq, bq, wk, wv, bv, q_ref, k_ref, v_ref):
    x = x_ref[...]
    q_ref[...] = (nn(x, wq[...]) + bq[...]).astype(BF16)
    k_ref[...] = nn(x, wk[...]).astype(BF16)
    v_ref[...] = (nn(x, wv[...]) + bv[...]).astype(BF16)


def project_qkv(x, wq, bq, wk, wv, bv):
    rows, width = x.shape
    step = 256
    wide = pl.BlockSpec((width, width), lambda i: (0, 0))
    one = pl.BlockSpec((1, width), lambda i: (0, 0))
    tile = pl.BlockSpec((step, width), lambda i: (i, 0))
    out = jax.ShapeDtypeStruct((rows, width), BF16)
    return pl.pallas_call(
        qkv_kernel,
        grid=(rows // step,),
        in_specs=[tile, wide, one, wide, wide, one],
        out_specs=[tile] * 3,
        out_shape=[out] * 3,
        compiler_params=params(),
        cost_estimate=cost(6 * rows * width * width, 6 * width * width + 8 * rows * width),
        name="qkv",
    )(x, wq, bq, wk, wv, bv)


def forward_kernel(
    lo_ref, hi_ref, q_ref, kp, ko, kn, vp, vo, vn, onehot, qmask, ctx_ref, lse_ref, ka, kb, vt
):
    rows = q_ref.shape[0]
    low = low_lanes()
    for part, (kpart, vpart) in enumerate(((kp, vp), (ko, vo), (kn, vn))):
        at = slice(part * rows, (part + 1) * rows)
        key = kpart[...]
        hot = onehot[at, :]
        ka[at, :] = jnp.where(low, key, hot)
        kb[at, :] = jnp.where(low, hot, key)
        vt[:, at] = vpart[...].T
    for i in range(rows // BQ):
        block = rows // BQ + i
        at = slice(i * BQ, (i + 1) * BQ)
        query = q_ref[at, :] * BF16(HEAD_DIM**-0.5)
        mask = qmask[rows + i * BQ : rows + (i + 1) * BQ, :]
        qa = jnp.where(low, query, mask)
        qb = jnp.where(low, mask, query)

        def step(j, carry):
            base = pl.multiple_of(j * BK, BK)
            out = []
            for head, (keys, qh) in enumerate(((ka, qa), (kb, qb))):
                top, total, acc = carry[head]
                scores = nt(keys[pl.ds(base, BK), :], qh)
                new_top = jnp.maximum(top, jnp.max(scores, axis=0, keepdims=True))
                weights = jnp.exp(scores - new_top)
                alpha = jnp.exp(top - new_top)
                total = total * alpha + jnp.sum(weights, axis=0, keepdims=True)
                vals = vt[head * HEAD_DIM : (head + 1) * HEAD_DIM, pl.ds(base, BK)]
                acc = acc * alpha + nn(vals, weights.astype(BF16))
                out.append((new_top, total, acc))
            return tuple(out)

        init = (
            jnp.full((1, BQ), FLOOR, F32),
            jnp.zeros((1, BQ), F32),
            jnp.zeros((HEAD_DIM, BQ), F32),
        )
        result = lax.fori_loop(lo_ref[block], hi_ref[block], step, (init, init))
        parts = [acc / total for _, total, acc in result]
        ctx_ref[at, :] = jnp.concatenate(parts, axis=0).T
        for head, (top, total, _) in enumerate(result):
            lse_ref[0, head : head + 1, at] = top + jnp.log(total)


def attend_forward(lo, hi, q, k, v, kh, vh, onehot, qmask):
    rows, width = q.shape
    pairs = width // PAIR
    own = pl.BlockSpec((rows, PAIR), lambda p, *_: (0, p))
    nxt = pl.BlockSpec((rows, PAIR), lambda p, *_: (1, p))
    seg = pl.BlockSpec((3 * rows, PAIR), lambda p, *_: (0, 0))
    grid = pltpu.PrefetchScalarGridSpec(
        num_scalar_prefetch=2,
        grid=(pairs,),
        in_specs=[own, own, own, nxt, own, own, nxt, seg, seg],
        out_specs=[own, pl.BlockSpec((1, 2, rows), lambda p, *_: (p, 0, 0))],
        scratch_shapes=[
            pltpu.VMEM((3 * rows, PAIR), BF16),
            pltpu.VMEM((3 * rows, PAIR), BF16),
            pltpu.VMEM((PAIR, 3 * rows), BF16),
        ],
    )
    return pl.pallas_call(
        forward_kernel,
        grid_spec=grid,
        out_shape=[
            jax.ShapeDtypeStruct((rows, width), F32),
            jax.ShapeDtypeStruct((pairs, 2, rows), F32),
        ],
        compiler_params=params(),
        cost_estimate=cost(8 * rows * rows * width, 24 * rows * width),
        name="attend_forward",
    )(lo, hi, q, kh, k, kh, vh, v, vh, onehot, qmask)


def backward_kernel(
    lo_ref, hi_ref, qp, qo, qn, kp, ko, kn, vp, vo, vn, gp, go, gn, sp, so, sn, onehot, qmask,
    dq_ref, dk_ref, dv_ref, ka, kb, kt, vs, dk_acc, dv_acc,
):
    rows = qo.shape[0]
    per = rows // BQ
    low = low_lanes()
    zero = jnp.zeros((1, PAIR), BF16)
    for part, (kpart, vpart) in enumerate(((kp, vp), (ko, vo), (kn, vn))):
        at = slice(part * rows, (part + 1) * rows)
        key = kpart[...]
        hot = onehot[at, :]
        ka[at, :] = jnp.where(low, key, hot)
        kb[at, :] = jnp.where(low, hot, key)
        kt[:, at] = key.T
        vs[at, :] = vpart[...]
    dk_acc[...] = jnp.zeros_like(dk_acc)
    dv_acc[...] = jnp.zeros_like(dv_acc)
    for i in range(3 * per):
        part = i // per
        own_q = part == 1
        at = slice((i % per) * BQ, (i % per + 1) * BQ)
        stat = (sp, so, sn)[part]
        query = (qp, qo, qn)[part][at, :] * BF16(HEAD_DIM**-0.5)
        grad = (gp, go, gn)[part][at, :]
        mask = qmask[i * BQ : (i + 1) * BQ, :]
        qs = (jnp.where(low, query, mask), jnp.where(low, mask, query))
        qz = (jnp.where(low, query, zero), jnp.where(low, zero, query))
        gz = (jnp.where(low, grad, zero), jnp.where(low, zero, grad))
        lse = (stat[0, 0:1, at], stat[0, 1:2, at])
        delta = (stat[0, 2:3, at], stat[0, 3:4, at])

        def step(j, carry, own_k):
            base = pl.multiple_of(j * BK, BK)
            out = []
            dv = dk = None
            for head, keys in enumerate((ka, kb)):
                scores = nt(keys[pl.ds(base, BK), :], qs[head])
                probs = jnp.exp(scores - lse[head])
                prob_grad = nt(vs[pl.ds(base, BK), :], gz[head])
                score_grad = (probs * (prob_grad - delta[head])).astype(BF16)
                if own_k:
                    one = nn(probs.astype(BF16), gz[head])
                    two = nn(score_grad, qz[head])
                    dv = one if dv is None else dv + one
                    dk = two if dk is None else dk + two
                if own_q:
                    rows_t = kt[head * HEAD_DIM : (head + 1) * HEAD_DIM, pl.ds(base, BK)]
                    out.append(carry[head] + nn(rows_t, score_grad))
            if own_k:
                to = pl.ds(pl.multiple_of(base - rows, BK), BK)
                dv_acc[to, :] = dv_acc[to, :] + dv
                dk_acc[to, :] = dk_acc[to, :] + dk
            return tuple(out)

        lo, hi = lo_ref[i], hi_ref[i]
        first, last = rows // BK, 2 * rows // BK
        if own_q:
            init = (jnp.zeros((HEAD_DIM, BQ), F32),) * 2
            outer = functools.partial(step, own_k=False)
            inner = functools.partial(step, own_k=True)
            total = lax.fori_loop(lo, jnp.minimum(hi, first), outer, init)
            total = lax.fori_loop(jnp.maximum(lo, first), jnp.minimum(hi, last), inner, total)
            total = lax.fori_loop(jnp.maximum(lo, last), hi, outer, total)
            dq = jnp.concatenate(total, axis=0) * F32(HEAD_DIM**-0.5)
            dq_ref[at, :] = dq.T.astype(BF16)
        else:
            lax.fori_loop(lo, hi, functools.partial(step, own_k=True), ())
    dk_ref[...] = dk_acc[...].astype(BF16)
    dv_ref[...] = dv_acc[...].astype(BF16)


def attend_backward(lo, hi, q, k, v, qh, kh, vh, g, gp, gn, st, stp, stn, onehot, qmask):
    rows, width = q.shape
    pairs = width // PAIR
    own = pl.BlockSpec((rows, PAIR), lambda p, *_: (0, p))
    nxt = pl.BlockSpec((rows, PAIR), lambda p, *_: (1, p))
    seg = pl.BlockSpec((3 * rows, PAIR), lambda p, *_: (0, 0))
    sta = pl.BlockSpec((1, 4, rows), lambda p, *_: (p, 0, 0))
    out = jax.ShapeDtypeStruct((rows, width), BF16)
    grid = pltpu.PrefetchScalarGridSpec(
        num_scalar_prefetch=2,
        grid=(pairs,),
        in_specs=[own, own, nxt] * 3 + [own] * 3 + [sta] * 3 + [seg, seg],
        out_specs=[own] * 3,
        scratch_shapes=[
            pltpu.VMEM((3 * rows, PAIR), BF16),
            pltpu.VMEM((3 * rows, PAIR), BF16),
            pltpu.VMEM((PAIR, 3 * rows), BF16),
            pltpu.VMEM((3 * rows, PAIR), BF16),
            pltpu.VMEM((rows, PAIR), F32),
            pltpu.VMEM((rows, PAIR), F32),
        ],
    )
    return pl.pallas_call(
        backward_kernel,
        grid_spec=grid,
        out_shape=[out] * 3,
        compiler_params=params(),
        cost_estimate=cost(24 * rows * rows * width, 40 * rows * width),
        name="attend_backward",
    )(lo, hi, qh, q, qh, kh, k, kh, vh, v, vh, gp, g, gn, stp, st, stn, onehot, qmask)


def norm_forward(h):
    mean = jnp.mean(h, axis=-1, keepdims=True)
    centred = h - mean
    variance = jnp.mean(centred * centred, axis=-1, keepdims=True)
    inverse = lax.rsqrt(variance + layer_eps)
    return centred * inverse, inverse


def norm_backward(grad, gain, hat, inverse):
    g = grad * gain
    return inverse * (
        g - jnp.mean(g, axis=-1, keepdims=True) - hat * jnp.mean(g * hat, axis=-1, keepdims=True)
    )


def colsum(v):
    return jnp.sum(v, axis=0, keepdims=True)


def middle_kernel(
    x_ref, ctx_ref, ct_ref, wo, bo, g1, s1, wup_hbm, bup, wdn_hbm, bdn, g2, s2, lse_ref,
    result_ref, fg_ref, ag_ref, cg_ref, hid_ref, ug_ref, nl_ref, bg_ref, cl_ref, stat_ref,
    vec_ref, bup_ref,
    wup, wdn, slope, normed, hat, inv, acc, sems,
):
    rows, width = x_ref.shape
    ff = wup.shape[1]
    rc, fc = 256, 512
    chunks, tiles = rows // rc, ff // fc
    up_copy = pltpu.make_async_copy(wup_hbm, wup, sems.at[0])
    dn_copy = pltpu.make_async_copy(wdn_hbm, wdn, sems.at[1])
    up_copy.start()
    dn_copy.start()

    @pl.loop(0, chunks)
    def _(r):
        at = pl.ds(pl.multiple_of(r * rc, rc), rc)
        c_low = ctx_ref[at, :].astype(BF16)
        cl_ref[at, :] = c_low
        h = x_ref[at, :].astype(F32) + (nn(c_low, wo[...]) + bo[...])
        xhat, inverse = norm_forward(h)
        out = xhat * g1[...] + s1[...]
        hat[at, :] = xhat
        inv[at, :] = inverse
        normed[at, :] = out
        nl_ref[at, :] = out.astype(BF16)

    up_copy.wait()
    dn_copy.wait()
    acc[...] = jnp.zeros_like(acc)

    @pl.loop(0, tiles)
    def _(j):
        cols = pl.ds(pl.multiple_of(j * fc, fc), fc)
        for r in range(chunks):
            at = slice(r * rc, (r + 1) * rc)
            up = nn(nl_ref[at, :], wup[:, cols]) + bup[:, cols]
            cdf = 0.5 * (1.0 + lax.erf(up * F32(0.5**0.5)))
            density = jnp.exp(-0.5 * up * up) * F32(0.3989422804014327)
            slope[at, cols] = cdf + up * density
            act = (up * cdf).astype(BF16)
            hid_ref[at, cols] = act
            acc[at, :] = acc[at, :] + nn(act, wdn[cols, :])

    vec_ref[...] = jnp.zeros_like(vec_ref)

    @pl.loop(0, chunks)
    def _(r):
        at = pl.ds(pl.multiple_of(r * rc, rc), rc)
        xhat, inverse = norm_forward(normed[at, :] + (acc[at, :] + bdn[...]))
        result_ref[at, :] = (xhat * g2[...] + s2[...]).astype(BF16)
        ct = ct_ref[at, :].astype(F32)
        second = norm_backward(ct, g2[...], xhat, inverse)
        low = second.astype(BF16)
        bg_ref[at, :] = low
        acc[at, :] = second
        vec_ref[0:1, :] = vec_ref[0:1, :] + colsum(ct * xhat)
        vec_ref[1:2, :] = vec_ref[1:2, :] + colsum(ct)
        vec_ref[2:3, :] = vec_ref[2:3, :] + colsum(low.astype(F32))

    @pl.loop(0, tiles)
    def _(j):
        cols = pl.ds(pl.multiple_of(j * fc, fc), fc)
        sums = jnp.zeros((1, fc), F32)
        for r in range(chunks):
            at = slice(r * rc, (r + 1) * rc)
            ug = (nt(bg_ref[at, :], wdn[cols, :]) * slope[at, cols]).astype(BF16)
            ug_ref[at, cols] = ug
            sums = sums + colsum(ug.astype(F32))
            acc[at, :] = acc[at, :] + nt(ug, wup[:, cols])
        bup_ref[:, cols] = sums

    for r in range(chunks):
        at = slice(r * rc, (r + 1) * rc)
        total = acc[at, :]
        xhat = hat[at, :]
        first = norm_backward(total, g1[...], xhat, inv[at, :])
        fg_ref[at, :] = first
        low = first.astype(BF16)
        ag_ref[at, :] = low
        vec_ref[3:4, :] = vec_ref[3:4, :] + colsum(total * xhat)
        vec_ref[4:5, :] = vec_ref[4:5, :] + colsum(total)
        vec_ref[5:6, :] = vec_ref[5:6, :] + colsum(low.astype(F32))
        cg = nt(low, wo[...]).astype(BF16)
        cg_ref[at, :] = cg
        prod = cg.astype(F32) * ctx_ref[at, :]
        for p in range(width // PAIR):
            flip = prod[:, p * PAIR : (p + 1) * PAIR].T
            stat_ref[p, 2:3, at] = colsum(flip[:HEAD_DIM])
            stat_ref[p, 3:4, at] = colsum(flip[HEAD_DIM:])
    for p in range(width // PAIR):
        stat_ref[p, 0:2, :] = lse_ref[p]


def middle(x, ctx, ct, wo, bo, g1, s1, wup, bup, wdn, bdn, g2, s2, lse):
    rows, width = x.shape
    ff = wup.shape[1]
    pairs = width // PAIR

    def out(shape, dtype):
        return jax.ShapeDtypeStruct(shape, dtype)

    shapes = [
        out((rows, width), BF16),
        out((rows, width), F32),
        out((rows, width), BF16),
        out((rows, width), BF16),
        out((rows, ff), BF16),
        out((rows, ff), BF16),
        out((rows, width), BF16),
        out((rows, width), BF16),
        out((rows, width), BF16),
        out((pairs, 4, rows), F32),
        out((8, width), F32),
        out((1, ff), F32),
    ]
    return pl.pallas_call(
        middle_kernel,
        in_specs=[whole()] * 7 + [hbm(), whole(), hbm()] + [whole()] * 4,
        out_specs=[whole()] * 12,
        out_shape=shapes,
        scratch_shapes=[
            pltpu.VMEM((width, ff), BF16),
            pltpu.VMEM((ff, width), BF16),
            pltpu.VMEM((rows, ff), F32),
            pltpu.VMEM((rows, width), F32),
            pltpu.VMEM((rows, width), F32),
            pltpu.VMEM((rows, 1), F32),
            pltpu.VMEM((rows, width), F32),
            pltpu.SemaphoreType.DMA((2,)),
        ],
        compiler_params=params(),
        cost_estimate=cost(8 * rows * width * ff + 4 * rows * width * width, 30 << 20),
        name="middle",
    )(x, ctx, ct, wo, bo, g1, s1, wup, bup, wdn, bdn, g2, s2, lse)


def place_bits(me, order):
    bits = [(me // (1 << b)) % 2 for b in range(LEVELS)]

    def position(c):
        at = 0
        for k, b in enumerate(order):
            bit = bits[b]
            if (c >> b) & 1:
                bit = 1 - bit
            at = at + bit * (1 << (LEVELS - 1 - k))
        return at

    return position


def block_number(ndev, sizes):
    me = lax.axis_index("dp") * sizes + lax.axis_index("seq")
    return me // (ndev >> LEVELS)


def ff_grads_kernel(
    ndev, parts, orders, hid, bg, nl, ug, cl, ag, dn_out, up_out, wo_out, dn_s, up_s, wo_s, sems
):
    ff, width = hid.shape[1], bg.shape[1]
    nblk = 1 << LEVELS
    me = block_number(ndev, parts)
    pos = [place_bits(me, o) for o in orders]
    tall, short = ff // nblk, width // nblk
    tile = 4 * tall
    bgv = bg[...]

    @pl.loop(0, ff // tile)
    def _(j):
        grad = tn(hid[:, pl.ds(pl.multiple_of(j * tile, tile), tile)], bgv)
        dn_s[pl.ds(4 * j, 4)] = grad.reshape(4, tall, width).astype(BF16)

    for c in range(nblk):
        pltpu.make_async_copy(dn_s.at[c], dn_out.at[pos[0](c)], sems.at[0]).start()
    fc = 512

    @pl.loop(0, ff // fc)
    def _(j):
        cols = pl.ds(pl.multiple_of(j * fc, fc), fc)
        grad = tn(nl[...], ug[:, cols])
        up_s[:, :, cols] = grad.reshape(nblk, short, fc).astype(BF16)

    for c in range(nblk):
        pltpu.make_async_copy(up_s.at[c], up_out.at[pos[1](c)], sems.at[1]).start()
    wo_s[...] = tn(cl[...], ag[...]).reshape(nblk, short, width).astype(BF16)
    for c in range(nblk):
        pltpu.make_async_copy(wo_s.at[c], wo_out.at[pos[2](c)], sems.at[2]).start()
    pltpu.make_async_copy(dn_s, dn_out, sems.at[0]).wait()
    pltpu.make_async_copy(up_s, up_out, sems.at[1]).wait()
    pltpu.make_async_copy(wo_s, wo_out, sems.at[2]).wait()


def ff_grads(ndev, parts, orders, hid, bg, nl, ug, cl, ag):
    rows, ff = hid.shape
    width = bg.shape[1]
    nblk = 1 << LEVELS
    shapes = [(nblk, ff // nblk, width), (nblk, width // nblk, ff), (nblk, width // nblk, width)]
    return pl.pallas_call(
        functools.partial(ff_grads_kernel, ndev, parts, orders),
        in_specs=[whole()] * 6,
        out_specs=[hbm()] * 3,
        out_shape=[jax.ShapeDtypeStruct(s, BF16) for s in shapes],
        scratch_shapes=[pltpu.VMEM(s, BF16) for s in shapes] + [pltpu.SemaphoreType.DMA((3,))],
        compiler_params=params(),
        cost_estimate=cost(4 * rows * width * ff + 2 * rows * width * width, 20 << 20),
        name="ff_grads",
    )(hid, bg, nl, ug, cl, ag)


def input_kernel(
    ndev, parts, order, x, dq, dk, dv, wq, wk, wv, fg, ig_ref, out, vec_ref, scr, sem
):
    width = x.shape[1]
    nblk = 1 << LEVELS
    pos = place_bits(block_number(ndev, parts), order)
    xv = x[...]
    for n, grad in enumerate((dq, dk, dv)):
        scr[:, n] = tn(xv, grad[...]).reshape(nblk, width // nblk, width).astype(BF16)
    for c in range(nblk):
        pltpu.make_async_copy(scr.at[c], out.at[pos(c)], sem).start()
    ig_ref[...] = (
        nt(dq[...], wq[...]) + nt(dk[...], wk[...]) + nt(dv[...], wv[...]) + fg[...]
    ).astype(BF16)
    vec_ref[...] = jnp.zeros_like(vec_ref)
    vec_ref[0:1, :] = colsum(dq[...].astype(F32))
    vec_ref[1:2, :] = colsum(dv[...].astype(F32))
    pltpu.make_async_copy(scr, out, sem).wait()


def input_side(ndev, parts, order, x, dq, dk, dv, wq, wk, wv, fg):
    rows, width = x.shape
    nblk = 1 << LEVELS
    shape = (nblk, 3, width // nblk, width)
    return pl.pallas_call(
        functools.partial(input_kernel, ndev, parts, order),
        in_specs=[whole()] * 8,
        out_specs=[whole(), hbm(), whole()],
        out_shape=[
            jax.ShapeDtypeStruct((rows, width), BF16),
            jax.ShapeDtypeStruct(shape, BF16),
            jax.ShapeDtypeStruct((8, width), F32),
        ],
        scratch_shapes=[pltpu.VMEM(shape, BF16), pltpu.SemaphoreType.DMA(())],
        compiler_params=params(),
        cost_estimate=cost(12 * rows * width * width, 16 << 20),
        name="input_side",
    )(x, dq, dk, dv, wq, wk, wv, fg)


def halve(arr, order, ndev):
    shift = ndev >> LEVELS
    for k, b in enumerate(order):
        half = arr.shape[0] // 2
        flip = shift << b
        got = lax.ppermute(arr[half:], AXES, [(i, i ^ flip) for i in range(ndev)])
        arr = arr[:half].astype(F32) + got.astype(F32)
        if k < len(order) - 1:
            arr = arr.astype(BF16)
    return arr[0]


def finish(block, ndev):
    rest = ndev >> LEVELS
    if rest == 1:
        return block
    step = 1
    me = lax.axis_index("dp") * lax.axis_size("seq") + lax.axis_index("seq")
    arr = block.reshape(rest, block.shape[0] // rest, block.shape[1])
    flip = rest
    while flip > 1:
        flip //= 2
        bit = (me // flip) % 2
        half = arr.shape[0] // 2
        keep = lax.dynamic_slice_in_dim(arr, bit * half, half, 0)
        send = lax.dynamic_slice_in_dim(arr, (1 - bit) * half, half, 0)
        arr = keep + lax.ppermute(send, AXES, [(i, i ^ flip) for i in range(ndev)])
    return arr[0]


def shards(
    layer_input,
    query_weight,
    query_bias,
    key_weight,
    value_weight,
    value_bias,
    output_weight,
    output_bias,
    first_gain,
    first_shift,
    up_weight,
    up_bias,
    down_weight,
    down_bias,
    second_gain,
    second_shift,
    out_cotangent,
    passage_lengths,
):
    parts = lax.axis_size("seq")
    ndev = parts * lax.axis_size("dp")
    rows, width = layer_input.shape
    ff = up_weight.shape[1]
    count = rows * parts
    place = lax.axis_index("seq")
    ahead = [(i, i + 1) for i in range(parts - 1)]
    back = [(i + 1, i) for i in range(parts - 1)]

    def row(v):
        return v.reshape(1, -1)

    x_prev = lax.ppermute(layer_input, "seq", ahead)
    x_next = lax.ppermute(layer_input, "seq", back)
    q, k, v = project_qkv(
        layer_input, query_weight, row(query_bias), key_weight, value_weight, row(value_bias)
    )
    lengths = passage_lengths[0]
    slots = lengths.shape[0]
    upto = jnp.arange(slots)[:, None] >= jnp.arange(slots)[None, :]
    ends = jnp.sum(jnp.where(upto, lengths[None, :], 0), axis=1)
    start = (place - 1) * rows
    where = start + jnp.arange(3 * rows, dtype=jnp.int32)
    seg = jnp.sum((where[:, None] >= ends[None, :]).astype(jnp.int32), axis=1)
    valid = (where >= 0) & (where < count)
    seg = jnp.where(valid, seg, slots)
    lanes = jnp.arange(PAIR, dtype=jnp.int32) % HEAD_DIM
    match = seg[:, None] == lanes[None, :]
    onehot = jnp.where(match, 1.0, 0.0).astype(BF16)
    qmask = jnp.where(match, 0.0, NEG).astype(BF16)
    heads_at = start + jnp.arange(3 * rows // BQ, dtype=jnp.int32) * BQ
    inside = (heads_at >= 0) & (heads_at < count)
    first_end = jnp.where(ends[None, :] <= heads_at[:, None], ends[None, :], 0)
    lo = jnp.max(first_end, axis=1) - start
    far = heads_at + BQ - 1
    hi = jnp.min(jnp.where(ends[None, :] > far[:, None], ends[None, :], count), axis=1) - start
    own_block = (jnp.arange(3 * rows // BQ) * BQ // rows) == 1
    lo = jnp.where(own_block, jnp.maximum(lo, 0), jnp.maximum(lo, rows))
    hi = jnp.where(own_block, jnp.minimum(hi, 3 * rows), jnp.minimum(hi, 2 * rows))
    lo = (lo // BK).astype(jnp.int32)
    hi = jnp.where(inside, (hi + BK - 1) // BK, 0).astype(jnp.int32)

    qh, kh, vh = project_qkv(
        jnp.concatenate([x_prev, x_next], axis=0),
        query_weight, row(query_bias), key_weight, value_weight, row(value_bias),
    )
    ctx, lse = attend_forward(lo, hi, q, k, v, kh, vh, onehot, qmask)
    result, fg, ag, cg, hid, ug, nl, bg, cl, stat, vec, bup = middle(
        layer_input, ctx, out_cotangent, output_weight, row(output_bias), row(first_gain),
        row(first_shift), up_weight, row(up_bias), down_weight, row(down_bias), row(second_gain),
        row(second_shift), lse,
    )
    g_prev = lax.ppermute(cg, "seq", ahead)
    g_next = lax.ppermute(cg, "seq", back)
    s_prev = lax.ppermute(stat, "seq", ahead)
    s_next = lax.ppermute(stat, "seq", back)
    orders = ((0, 2, 1, 3, 4), (0, 1, 2, 3, 4), (0, 3, 4, 2, 1))
    dn_parts, up_parts, wo_parts = ff_grads(ndev, parts, orders, hid, bg, nl, ug, cl, ag)
    dq, dk, dv = attend_backward(
        lo, hi, q, k, v, qh, kh, vh, cg, g_prev, g_next, stat, s_prev, s_next, onehot, qmask
    )
    in_order = (0, 2, 1, 3, 4)
    input_grad, in_parts, vec_in = input_side(
        ndev, parts, in_order, layer_input, dq, dk, dv, query_weight, key_weight, value_weight, fg
    )
    dn_sum = finish(halve(dn_parts, orders[0], ndev), ndev)
    up_sum = finish(halve(up_parts, orders[1], ndev), ndev)
    wo_sum = finish(halve(wo_parts, orders[2], ndev), ndev)
    in_sum = halve(in_parts, in_order, ndev)
    in_sum = [finish(in_sum[n], ndev) for n in range(3)]

    vectors = [vec_in[0], vec_in[1], vec[5], vec[3], vec[4], bup[0], vec[2], vec[0], vec[1]]
    packed = jnp.concatenate([u.reshape(ndev, -1) for u in vectors], axis=1)
    shared = lax.all_to_all(packed, AXES, split_axis=0, concat_axis=0, tiled=True)
    summed = jnp.sum(shared, axis=0)
    sizes = [u.shape[0] // ndev for u in vectors]
    outs = []
    at = 0
    for size in sizes:
        outs.append(summed[at : at + size])
        at += size
    qb, vb, ob, g1g, s1g, ub, db, g2g, s2g = outs
    return (
        result, input_grad, in_sum[0], qb, in_sum[1], in_sum[2], vb, wo_sum, ob, g1g, s1g,
        up_sum, ub, dn_sum, db, g2g, s2g,
    )


def solution(mesh):
    split = P(AXES, None)
    part = P(AXES)
    in_specs = (split,) + (P(),) * 15 + (split, P("dp", None))
    out_specs = (
        split, split, split, part, split, split, part, split, part, part, part,
        split, part, split, part, part, part,
    )
    return jax.shard_map(shards, mesh=mesh, in_specs=in_specs, out_specs=out_specs, check_vma=False)
```

```python
import functools

import jax
import jax.numpy as jnp
from jax import lax
from jax.experimental import pallas as pl
from jax.experimental.pallas import tpu as pltpu
from jax.sharding import PartitionSpec as P

HEAD_DIM = 64
PAIR = 2 * HEAD_DIM
AXES = ("dp", "seq")
NEG = -1e30
FLOOR = -3e38
BQ = 256
BK = 256
LEVELS = 5
layer_eps = 1e-12
F32 = jnp.float32
BF16 = jnp.bfloat16


def nn(a, b):
    return lax.dot_general(a, b, (((1,), (0,)), ((), ())), preferred_element_type=F32)


def nt(a, b):
    return lax.dot_general(a, b, (((1,), (1,)), ((), ())), preferred_element_type=F32)


def tn(a, b):
    return lax.dot_general(a, b, (((0,), (0,)), ((), ())), preferred_element_type=F32)


def cost(flops, nbytes, trans=0):
    return pl.CostEstimate(flops=int(flops), bytes_accessed=int(nbytes), transcendentals=int(trans))


def params(limit=56 << 20):
    return pltpu.CompilerParams(vmem_limit_bytes=limit)


def whole():
    return pl.BlockSpec(memory_space=pltpu.VMEM)


def hbm():
    return pl.BlockSpec(memory_space=pl.ANY)


def low_lanes():
    return lax.broadcasted_iota(jnp.int32, (1, PAIR), 1) < HEAD_DIM


def line(ref):
    return ref[...].reshape(1, -1)


def qkv_kernel(x_ref, wq, bq, wk, wv, bv, q_ref, k_ref, v_ref):
    x = x_ref[...]
    q_ref[...] = (nn(x, wq[...]) + line(bq)).astype(BF16)
    k_ref[...] = nn(x, wk[...]).astype(BF16)
    v_ref[...] = (nn(x, wv[...]) + line(bv)).astype(BF16)


def project_qkv(x, wq, bq, wk, wv, bv):
    rows, width = x.shape
    step = 256
    wide = pl.BlockSpec((width, width), lambda i: (0, 0))
    one = pl.BlockSpec((width,), lambda i: (0,))
    tile = pl.BlockSpec((step, width), lambda i: (i, 0))
    out = jax.ShapeDtypeStruct((rows, width), BF16)
    return pl.pallas_call(
        qkv_kernel,
        grid=(rows // step,),
        in_specs=[tile, wide, one, wide, wide, one],
        out_specs=[tile] * 3,
        out_shape=[out] * 3,
        compiler_params=params(),
        cost_estimate=cost(6 * rows * width * width, 6 * width * width + 8 * rows * width),
        name="qkv",
    )(x, wq, bq, wk, wv, bv)


def forward_kernel(
    lo_ref, hi_ref, q_ref, kp, ko, kn, vp, vo, vn, onehot, qmask, ctx_ref, lse_ref, ka, kb, vt
):
    rows = q_ref.shape[0]
    low = low_lanes()
    for part, (kpart, vpart) in enumerate(((kp, vp), (ko, vo), (kn, vn))):
        at = slice(part * rows, (part + 1) * rows)
        key = kpart[...]
        hot = onehot[at, :]
        ka[at, :] = jnp.where(low, key, hot)
        kb[at, :] = jnp.where(low, hot, key)
        vt[:, at] = vpart[...].T
    for i in range(rows // BQ):
        block = rows // BQ + i
        at = slice(i * BQ, (i + 1) * BQ)
        query = q_ref[at, :] * BF16(HEAD_DIM**-0.5)
        mask = qmask[rows + i * BQ : rows + (i + 1) * BQ, :]
        qa = jnp.where(low, query, mask)
        qb = jnp.where(low, mask, query)

        def step(j, carry):
            base = pl.multiple_of(j * BK, BK)
            out = []
            for head, (keys, qh) in enumerate(((ka, qa), (kb, qb))):
                top, total, acc = carry[head]
                scores = nt(keys[pl.ds(base, BK), :], qh)
                new_top = jnp.maximum(top, jnp.max(scores, axis=0, keepdims=True))
                weights = jnp.exp(scores - new_top)
                alpha = jnp.exp(top - new_top)
                total = total * alpha + jnp.sum(weights, axis=0, keepdims=True)
                vals = vt[head * HEAD_DIM : (head + 1) * HEAD_DIM, pl.ds(base, BK)]
                acc = acc * alpha + nn(vals, weights.astype(BF16))
                out.append((new_top, total, acc))
            return tuple(out)

        init = (
            jnp.full((1, BQ), FLOOR, F32),
            jnp.zeros((1, BQ), F32),
            jnp.zeros((HEAD_DIM, BQ), F32),
        )
        result = lax.fori_loop(lo_ref[block], hi_ref[block], step, (init, init))
        parts = [acc / total for _, total, acc in result]
        ctx_ref[at, :] = jnp.concatenate(parts, axis=0).T
        for head, (top, total, _) in enumerate(result):
            lse_ref[0, head : head + 1, at] = top + jnp.log(total)


def attend_forward(lo, hi, q, k, v, kh, vh, onehot, qmask):
    rows, width = q.shape
    pairs = width // PAIR
    own = pl.BlockSpec((rows, PAIR), lambda p, *_: (0, p))
    nxt = pl.BlockSpec((rows, PAIR), lambda p, *_: (1, p))
    seg = pl.BlockSpec((3 * rows, PAIR), lambda p, *_: (0, 0))
    grid = pltpu.PrefetchScalarGridSpec(
        num_scalar_prefetch=2,
        grid=(pairs,),
        in_specs=[own, own, own, nxt, own, own, nxt, seg, seg],
        out_specs=[own, pl.BlockSpec((1, 2, rows), lambda p, *_: (p, 0, 0))],
        scratch_shapes=[
            pltpu.VMEM((3 * rows, PAIR), BF16),
            pltpu.VMEM((3 * rows, PAIR), BF16),
            pltpu.VMEM((PAIR, 3 * rows), BF16),
        ],
    )
    return pl.pallas_call(
        forward_kernel,
        grid_spec=grid,
        out_shape=[
            jax.ShapeDtypeStruct((rows, width), F32),
            jax.ShapeDtypeStruct((pairs, 2, rows), F32),
        ],
        compiler_params=params(),
        cost_estimate=cost(40e9, 24 * rows * width),
        name="attend_forward",
    )(lo, hi, q, kh, k, kh, vh, v, vh, onehot, qmask)


def backward_kernel(
    lo_ref, hi_ref, qp, qo, qn, kp, ko, kn, vp, vo, vn, gp, go, gn, sp, so, sn, onehot, qmask,
    dq_ref, dk_ref, dv_ref, ka, kb, kt, vs, dk_acc, dv_acc,
):
    rows = qo.shape[0]
    per = rows // BQ
    low = low_lanes()
    zero = jnp.zeros((1, PAIR), BF16)
    for part, (kpart, vpart) in enumerate(((kp, vp), (ko, vo), (kn, vn))):
        at = slice(part * rows, (part + 1) * rows)
        key = kpart[...]
        hot = onehot[at, :]
        ka[at, :] = jnp.where(low, key, hot)
        kb[at, :] = jnp.where(low, hot, key)
        kt[:, at] = key.T
        vs[at, :] = vpart[...]
    dk_acc[...] = jnp.zeros_like(dk_acc)
    dv_acc[...] = jnp.zeros_like(dv_acc)
    for i in range(3 * per):
        part = i // per
        own_q = part == 1
        at = slice((i % per) * BQ, (i % per + 1) * BQ)
        stat = (sp, so, sn)[part]
        query = (qp, qo, qn)[part][at, :] * BF16(HEAD_DIM**-0.5)
        grad = (gp, go, gn)[part][at, :]
        mask = qmask[i * BQ : (i + 1) * BQ, :]
        qs = (jnp.where(low, query, mask), jnp.where(low, mask, query))
        qz = (jnp.where(low, query, zero), jnp.where(low, zero, query))
        gz = (jnp.where(low, grad, zero), jnp.where(low, zero, grad))
        lse = (stat[0, 0:1, at], stat[0, 1:2, at])
        delta = (stat[0, 2:3, at], stat[0, 3:4, at])

        def step(j, carry, own_k):
            base = pl.multiple_of(j * BK, BK)
            out = []
            dv = dk = None
            for head, keys in enumerate((ka, kb)):
                scores = nt(keys[pl.ds(base, BK), :], qs[head])
                probs = jnp.exp(scores - lse[head])
                prob_grad = nt(vs[pl.ds(base, BK), :], gz[head])
                score_grad = (probs * (prob_grad - delta[head])).astype(BF16)
                if own_k:
                    one = nn(probs.astype(BF16), gz[head])
                    two = nn(score_grad, qz[head])
                    dv = one if dv is None else dv + one
                    dk = two if dk is None else dk + two
                if own_q:
                    rows_t = kt[head * HEAD_DIM : (head + 1) * HEAD_DIM, pl.ds(base, BK)]
                    out.append(carry[head] + nn(rows_t, score_grad))
            if own_k:
                to = pl.ds(pl.multiple_of(base - rows, BK), BK)
                dv_acc[to, :] = dv_acc[to, :] + dv
                dk_acc[to, :] = dk_acc[to, :] + dk
            return tuple(out)

        lo, hi = lo_ref[i], hi_ref[i]
        first, last = rows // BK, 2 * rows // BK
        if own_q:
            init = (jnp.zeros((HEAD_DIM, BQ), F32),) * 2
            outer = functools.partial(step, own_k=False)
            inner = functools.partial(step, own_k=True)
            total = lax.fori_loop(lo, jnp.minimum(hi, first), outer, init)
            total = lax.fori_loop(jnp.maximum(lo, first), jnp.minimum(hi, last), inner, total)
            total = lax.fori_loop(jnp.maximum(lo, last), hi, outer, total)
            dq = jnp.concatenate(total, axis=0) * F32(HEAD_DIM**-0.5)
            dq_ref[at, :] = dq.T.astype(BF16)
        else:
            lax.fori_loop(lo, hi, functools.partial(step, own_k=True), ())
    dk_ref[...] = dk_acc[...].astype(BF16)
    dv_ref[...] = dv_acc[...].astype(BF16)


def attend_backward(lo, hi, q, k, v, qh, kh, vh, g, gp, gn, st, stp, stn, onehot, qmask):
    rows, width = q.shape
    pairs = width // PAIR
    own = pl.BlockSpec((rows, PAIR), lambda p, *_: (0, p))
    nxt = pl.BlockSpec((rows, PAIR), lambda p, *_: (1, p))
    seg = pl.BlockSpec((3 * rows, PAIR), lambda p, *_: (0, 0))
    sta = pl.BlockSpec((1, 4, rows), lambda p, *_: (p, 0, 0))
    out = jax.ShapeDtypeStruct((rows, width), BF16)
    grid = pltpu.PrefetchScalarGridSpec(
        num_scalar_prefetch=2,
        grid=(pairs,),
        in_specs=[own, own, nxt] * 3 + [own] * 3 + [sta] * 3 + [seg, seg],
        out_specs=[own] * 3,
        scratch_shapes=[
            pltpu.VMEM((3 * rows, PAIR), BF16),
            pltpu.VMEM((3 * rows, PAIR), BF16),
            pltpu.VMEM((PAIR, 3 * rows), BF16),
            pltpu.VMEM((3 * rows, PAIR), BF16),
            pltpu.VMEM((rows, PAIR), F32),
            pltpu.VMEM((rows, PAIR), F32),
        ],
    )
    return pl.pallas_call(
        backward_kernel,
        grid_spec=grid,
        out_shape=[out] * 3,
        compiler_params=params(),
        cost_estimate=cost(50e9, 40 * rows * width),
        name="attend_backward",
    )(lo, hi, qh, q, qh, kh, k, kh, vh, v, vh, gp, g, gn, stp, st, stn, onehot, qmask)


def norm_forward(h):
    mean = jnp.mean(h, axis=-1, keepdims=True)
    centred = h - mean
    variance = jnp.mean(centred * centred, axis=-1, keepdims=True)
    inverse = lax.rsqrt(variance + layer_eps)
    return centred * inverse, inverse


def norm_backward(grad, gain, hat, inverse):
    g = grad * gain
    return inverse * (
        g - jnp.mean(g, axis=-1, keepdims=True) - hat * jnp.mean(g * hat, axis=-1, keepdims=True)
    )


def colsum(v):
    return jnp.sum(v, axis=0, keepdims=True)


def middle_kernel(
    x_ref, ctx_ref, ct_ref, wo, bo, g1, s1, wup_hbm, bup, wdn_hbm, bdn, g2, s2, lse_ref,
    result_ref, fg_ref, ag_ref, cg_ref, hid_ref, ug_ref, nl_ref, bg_ref, cl_ref, stat_ref,
    vec_ref, bup_ref,
    wup, wdn, slope, normed, hat, inv, acc, sems,
):
    rows, width = x_ref.shape
    ff = wup.shape[1]
    rc, fc = 256, 512
    chunks, tiles = rows // rc, ff // fc
    up_copy = pltpu.make_async_copy(wup_hbm, wup, sems.at[0])
    dn_copy = pltpu.make_async_copy(wdn_hbm, wdn, sems.at[1])
    up_copy.start()
    dn_copy.start()

    @pl.loop(0, chunks)
    def _(r):
        at = pl.ds(pl.multiple_of(r * rc, rc), rc)
        c_low = ctx_ref[at, :].astype(BF16)
        cl_ref[at, :] = c_low
        h = x_ref[at, :].astype(F32) + (nn(c_low, wo[...]) + line(bo))
        xhat, inverse = norm_forward(h)
        out = xhat * line(g1) + line(s1)
        hat[at, :] = xhat
        inv[at, :] = inverse
        normed[at, :] = out
        nl_ref[at, :] = out.astype(BF16)

    up_copy.wait()
    dn_copy.wait()
    acc[...] = jnp.zeros_like(acc)

    @pl.loop(0, tiles)
    def _(j):
        cols = pl.ds(pl.multiple_of(j * fc, fc), fc)
        for r in range(chunks):
            at = slice(r * rc, (r + 1) * rc)
            up = nn(nl_ref[at, :], wup[:, cols]) + bup[cols].reshape(1, fc)
            cdf = 0.5 * (1.0 + lax.erf(up * F32(0.5**0.5)))
            density = jnp.exp(-0.5 * up * up) * F32(0.3989422804014327)
            slope[at, cols] = cdf + up * density
            act = (up * cdf).astype(BF16)
            hid_ref[at, cols] = act
            acc[at, :] = acc[at, :] + nn(act, wdn[cols, :])

    vec_ref[...] = jnp.zeros_like(vec_ref)

    @pl.loop(0, chunks)
    def _(r):
        at = pl.ds(pl.multiple_of(r * rc, rc), rc)
        xhat, inverse = norm_forward(normed[at, :] + (acc[at, :] + line(bdn)))
        result_ref[at, :] = (xhat * line(g2) + line(s2)).astype(BF16)
        ct = ct_ref[at, :].astype(F32)
        second = norm_backward(ct, line(g2), xhat, inverse)
        low = second.astype(BF16)
        bg_ref[at, :] = low
        acc[at, :] = second
        vec_ref[0:1, :] = vec_ref[0:1, :] + colsum(ct * xhat)
        vec_ref[1:2, :] = vec_ref[1:2, :] + colsum(ct)
        vec_ref[2:3, :] = vec_ref[2:3, :] + colsum(low.astype(F32))

    @pl.loop(0, tiles)
    def _(j):
        cols = pl.ds(pl.multiple_of(j * fc, fc), fc)
        sums = jnp.zeros((1, fc), F32)
        for r in range(chunks):
            at = slice(r * rc, (r + 1) * rc)
            ug = (nt(bg_ref[at, :], wdn[cols, :]) * slope[at, cols]).astype(BF16)
            ug_ref[at, cols] = ug
            sums = sums + colsum(ug.astype(F32))
            acc[at, :] = acc[at, :] + nt(ug, wup[:, cols])
        bup_ref[:, cols] = sums

    for r in range(chunks):
        at = slice(r * rc, (r + 1) * rc)
        total = acc[at, :]
        xhat = hat[at, :]
        first = norm_backward(total, line(g1), xhat, inv[at, :])
        fg_ref[at, :] = first
        low = first.astype(BF16)
        ag_ref[at, :] = low
        vec_ref[3:4, :] = vec_ref[3:4, :] + colsum(total * xhat)
        vec_ref[4:5, :] = vec_ref[4:5, :] + colsum(total)
        vec_ref[5:6, :] = vec_ref[5:6, :] + colsum(low.astype(F32))
        cg = nt(low, wo[...]).astype(BF16)
        cg_ref[at, :] = cg
        prod = cg.astype(F32) * ctx_ref[at, :]
        for p in range(width // PAIR):
            flip = prod[:, p * PAIR : (p + 1) * PAIR].T
            stat_ref[p, 2:3, at] = colsum(flip[:HEAD_DIM])
            stat_ref[p, 3:4, at] = colsum(flip[HEAD_DIM:])
    for p in range(width // PAIR):
        stat_ref[p, 0:2, :] = lse_ref[p]


def middle(x, ctx, ct, wo, bo, g1, s1, wup, bup, wdn, bdn, g2, s2, lse):
    rows, width = x.shape
    ff = wup.shape[1]
    pairs = width // PAIR

    def out(shape, dtype):
        return jax.ShapeDtypeStruct(shape, dtype)

    shapes = [
        out((rows, width), BF16),
        out((rows, width), F32),
        out((rows, width), BF16),
        out((rows, width), BF16),
        out((rows, ff), BF16),
        out((rows, ff), BF16),
        out((rows, width), BF16),
        out((rows, width), BF16),
        out((rows, width), BF16),
        out((pairs, 4, rows), F32),
        out((8, width), F32),
        out((1, ff), F32),
    ]
    return pl.pallas_call(
        middle_kernel,
        in_specs=[whole()] * 7 + [hbm(), whole(), hbm()] + [whole()] * 4,
        out_specs=[whole()] * 12,
        out_shape=shapes,
        scratch_shapes=[
            pltpu.VMEM((width, ff), BF16),
            pltpu.VMEM((ff, width), BF16),
            pltpu.VMEM((rows, ff), F32),
            pltpu.VMEM((rows, width), F32),
            pltpu.VMEM((rows, width), F32),
            pltpu.VMEM((rows, 1), F32),
            pltpu.VMEM((rows, width), F32),
            pltpu.SemaphoreType.DMA((2,)),
        ],
        compiler_params=params(),
        cost_estimate=cost(8 * rows * width * ff + 4 * rows * width * width, 30 << 20),
        name="middle",
    )(x, ctx, ct, wo, bo, g1, s1, wup, bup, wdn, bdn, g2, s2, lse)


def place_bits(me, order):
    bits = [(me // (1 << b)) % 2 for b in range(LEVELS)]

    def position(c):
        at = 0
        for k, b in enumerate(order):
            bit = bits[b]
            if (c >> b) & 1:
                bit = 1 - bit
            at = at + bit * (1 << (LEVELS - 1 - k))
        return at

    return position


def block_number(ndev, sizes):
    me = lax.axis_index("dp") * sizes + lax.axis_index("seq")
    return me // (ndev >> LEVELS)


def ff_grads_kernel(
    ndev, parts, orders, hid, bg, nl, ug, cl, ag, dn_out, up_out, wo_out, dn_s, up_s, wo_s, sems
):
    ff, width = hid.shape[1], bg.shape[1]
    nblk = 1 << LEVELS
    me = block_number(ndev, parts)
    pos = [place_bits(me, o) for o in orders]
    tall, short = ff // nblk, width // nblk
    tile = 4 * tall
    bgv = bg[...]

    @pl.loop(0, ff // tile)
    def _(j):
        grad = tn(hid[:, pl.ds(pl.multiple_of(j * tile, tile), tile)], bgv)
        dn_s[pl.ds(4 * j, 4)] = grad.reshape(4, tall, width).astype(BF16)

    for c in range(nblk):
        pltpu.make_async_copy(dn_s.at[c], dn_out.at[pos[0](c)], sems.at[0]).start()
    fc = 512

    @pl.loop(0, ff // fc)
    def _(j):
        cols = pl.ds(pl.multiple_of(j * fc, fc), fc)
        grad = tn(nl[...], ug[:, cols])
        up_s[:, :, cols] = grad.reshape(nblk, short, fc).astype(BF16)

    for c in range(nblk):
        pltpu.make_async_copy(up_s.at[c], up_out.at[pos[1](c)], sems.at[1]).start()
    wo_s[...] = tn(cl[...], ag[...]).reshape(nblk, short, width).astype(BF16)
    pltpu.make_async_copy(wo_s, wo_out, sems.at[2]).start()
    pltpu.make_async_copy(dn_s, dn_out, sems.at[0]).wait()
    pltpu.make_async_copy(up_s, up_out, sems.at[1]).wait()
    pltpu.make_async_copy(wo_s, wo_out, sems.at[2]).wait()


def ff_grads(ndev, parts, orders, hid, bg, nl, ug, cl, ag):
    rows, ff = hid.shape
    width = bg.shape[1]
    nblk = 1 << LEVELS
    shapes = [(nblk, ff // nblk, width), (nblk, width // nblk, ff), (nblk, width // nblk, width)]
    return pl.pallas_call(
        functools.partial(ff_grads_kernel, ndev, parts, orders),
        in_specs=[whole()] * 6,
        out_specs=[hbm()] * 3,
        out_shape=[jax.ShapeDtypeStruct(s, BF16) for s in shapes],
        scratch_shapes=[pltpu.VMEM(s, BF16) for s in shapes] + [pltpu.SemaphoreType.DMA((3,))],
        compiler_params=params(),
        cost_estimate=cost(4 * rows * width * ff + 2 * rows * width * width, 20 << 20),
        name="ff_grads",
    )(hid, bg, nl, ug, cl, ag)


def split_place(me, order):
    def position(c):
        at = 0
        for k, b in enumerate(order):
            mine, its = (me // (1 << b)) % 2, (c // (1 << b)) % 2
            at = at + (mine + its - 2 * mine * its) * (1 << (LEVELS - 1 - k))
        return at

    return position


DN_ORDER = (0, 2, 1, 3, 4)
UP_ORDER = (0, 1, 2, 3, 4)
ONE_ORDER = (0, 2, 1, 3, 4)
TWO_ORDER = (0, 1, 2, 4, 3)
EARLY = 2


def tail_kernel(
    ndev, parts,
    x, dq, dk, dv, wq, wk, wv, fg, dn_keep, dn_got, up_keep, up_got, wo_parts, vec, bup,
    ig_ref, dn_out, up_out, wo_out, q_out, k_out, v_out, vec_out, bup_out,
    dn_s, up_s, one_s, two_s, grad_s, vec_s, bup_s,
    dn_r, up_r, one_r, two_r, vec_r, bup_r,
    load_sems, send_sems, recv_sems,
):
    width = x.shape[1]
    nblk = 1 << LEVELS
    short = width // nblk
    shift = ndev >> LEVELS
    me = lax.axis_index("dp") * parts + lax.axis_index("seq")
    block = me // shift

    def partner(flip):
        other = me + (1 - 2 * ((me // flip) % 2)) * flip
        return (other // parts, other % parts)

    flips = []
    flip = 1
    while flip < ndev:
        flips.append(flip)
        flip *= 2
    barrier = pltpu.get_barrier_semaphore()
    for flip in flips:
        pl.semaphore_signal(
            barrier, inc=1, device_id=partner(flip), device_id_type=pl.DeviceIdType.MESH
        )
    pl.semaphore_wait(barrier, len(flips))

    used = [0]

    def exchange(src, dst, flip):
        n = used[0]
        used[0] += 1
        copy = pltpu.make_async_remote_copy(
            src_ref=src, dst_ref=dst, send_sem=send_sems.at[n], recv_sem=recv_sems.at[n],
            device_id=partner(flip), device_id_type=pl.DeviceIdType.MESH,
        )
        copy.start()
        return copy

    started = []

    class Chain:
        def __init__(self, buf, recv, order, done):
            self.buf, self.recv, self.order, self.step = buf, recv, order, done
            self.base = 0
            self.copy = None

        def send(self):
            half = (1 << LEVELS) >> (self.step + 1)
            self.half = half
            self.copy = exchange(
                self.buf.at[pl.ds(half, half)],
                self.recv.at[pl.ds(self.base, half)],
                shift << self.order[self.step],
            )
            started.append(self.copy)

        def add(self):
            self.copy.wait_recv()
            half, base, buf, recv = self.half, self.base, self.buf, self.recv
            if half > 1:

                @pl.loop(0, half)
                def _(i):
                    buf[i] = (buf[i].astype(F32) + recv[base + i].astype(F32)).astype(BF16)

            self.base += half
            self.step += 1
            if half > 1:
                self.send()

        def last(self):
            at = self.base - 1
            return self.buf[0].astype(F32) + self.recv[at].astype(F32)

    dn = Chain(dn_s, dn_r, DN_ORDER, EARLY)
    up = Chain(up_s, up_r, UP_ORDER, EARLY)
    one = Chain(one_s, one_r, ONE_ORDER, 0)
    two = Chain(two_s, two_r, TWO_ORDER, 0)

    loads = [
        pltpu.make_async_copy(keep.at[pl.ds(0, chain.buf.shape[0])], chain.buf, load_sems.at[n])
        for n, (chain, keep) in enumerate(((dn, dn_keep), (up, up_keep)))
    ]
    for load in loads:
        load.start()

    def begin(chain, load, got):
        load.wait()

        @pl.loop(0, chain.buf.shape[0])
        def _(i):
            chain.buf[i] = (chain.buf[i].astype(F32) + got[i].astype(F32)).astype(BF16)

        chain.send()

    begin(dn, loads[0], dn_got)
    begin(up, loads[1], up_got)

    vec_s[0] = vec[...]
    vec_s[0, 6:7, :] = colsum(dq[...].astype(F32))
    vec_s[0, 7:8, :] = colsum(dv[...].astype(F32))
    bup_s[0] = bup[...]

    def vector_send(n):
        a = exchange(vec_s.at[n], vec_r.at[n], flips[n])
        b = exchange(bup_s.at[n], bup_r.at[n], flips[n])
        started.extend((a, b))
        return a, b

    def vector_add(n, copies):
        for c in copies:
            c.wait_recv()
        vec_s[n + 1] = vec_s[n] + vec_r[n]
        bup_s[n + 1] = bup_s[n] + bup_r[n]
        return vector_send(n + 1) if n + 1 < len(flips) else None

    vc = vector_send(0)
    xv = x[...]

    def place(chain, offset, order):
        pos = split_place(block, order)

        @pl.loop(0, nblk)
        def _(c):
            at = pl.ds(pl.multiple_of(c * short, short), short)
            chain.buf[pos(c), offset : offset + short, :] = grad_s[at, :].astype(BF16)

    pos_one = split_place(block, ONE_ORDER)

    @pl.loop(0, nblk)
    def _(c):
        one_s[pos_one(c), 0:short, :] = wo_parts[c]

    grad_s[...] = tn(xv, dq[...])
    place(one, short, ONE_ORDER)
    one.send()
    grad_s[...] = tn(xv, dk[...])
    place(two, 0, TWO_ORDER)
    grad_s[...] = tn(xv, dv[...])
    place(two, short, TWO_ORDER)
    two.send()
    vc = vector_add(0, vc)
    one.add()
    ig_ref[...] = (
        nt(dq[...], wq[...]) + nt(dk[...], wk[...]) + nt(dv[...], wv[...]) + fg[...]
    ).astype(BF16)
    two.add()
    vc = vector_add(1, vc)
    dn.add()
    up.add()
    one.add()
    two.add()
    vc = vector_add(2, vc)
    dn.add()
    up.add()
    one.add()
    two.add()
    vc = vector_add(3, vc)
    dn.add()
    up.add()
    dn_out[...] = dn.last()
    up_out[...] = up.last()
    one.add()
    two.add()
    for n in range(4, len(flips)):
        vc = vector_add(n, vc)
    one.add()
    two.add()
    both = one.last()
    wo_out[...] = both[:short]
    q_out[...] = both[short:]
    both = two.last()
    k_out[...] = both[:short]
    v_out[...] = both[short:]
    vec_out[...] = vec_s[len(flips)]
    bup_out[...] = bup_s[len(flips)]
    for c in started:
        c.wait_send()


def tail(ndev, parts, x, dq, dk, dv, wq, wk, wv, fg, dn, dn_got, up, up_got, wo_parts, vec, bup):
    rows, width = x.shape
    nblk = 1 << LEVELS
    short = width // nblk
    left = nblk >> EARLY
    tall, ff = dn.shape[1], up.shape[2]
    steps = ndev.bit_length() - 1

    def out(*shape):
        return jax.ShapeDtypeStruct(shape, F32)

    copies = 2 * (LEVELS - EARLY) + 2 * LEVELS + 2 * steps
    return pl.pallas_call(
        functools.partial(tail_kernel, ndev, parts),
        in_specs=[whole()] * 8
        + [hbm(), whole(), hbm(), whole()]
        + [whole()] * 3,
        out_specs=[whole()] * 9,
        out_shape=[
            jax.ShapeDtypeStruct((rows, width), BF16),
            out(tall, width), out(short, ff),
            out(short, width), out(short, width), out(short, width), out(short, width),
            out(8, width), out(1, ff),
        ],
        scratch_shapes=[
            pltpu.VMEM((left, tall, width), BF16),
            pltpu.VMEM((left, short, ff), BF16),
            pltpu.VMEM((nblk, 2 * short, width), BF16),
            pltpu.VMEM((nblk, 2 * short, width), BF16),
            pltpu.VMEM((width, width), F32),
            pltpu.VMEM((steps + 1, 8, width), F32),
            pltpu.VMEM((steps + 1, 1, ff), F32),
            pltpu.VMEM((left, tall, width), BF16),
            pltpu.VMEM((left, short, ff), BF16),
            pltpu.VMEM((nblk, 2 * short, width), BF16),
            pltpu.VMEM((nblk, 2 * short, width), BF16),
            pltpu.VMEM((steps, 8, width), F32),
            pltpu.VMEM((steps, 1, ff), F32),
            pltpu.SemaphoreType.DMA((2,)),
            pltpu.SemaphoreType.DMA((copies,)),
            pltpu.SemaphoreType.DMA((copies,)),
        ],
        compiler_params=pltpu.CompilerParams(
            vmem_limit_bytes=56 << 20, collective_id=0, has_side_effects=True
        ),
        cost_estimate=cost(60e9, 16 << 20),
        name="tail",
    )(x, dq, dk, dv, wq, wk, wv, fg, dn, dn_got, up, up_got, wo_parts, vec, bup)


def first_halves(arr, order, ndev):
    shift = ndev >> LEVELS
    for k in range(EARLY):
        half = arr.shape[0] // 2
        flip = shift << order[k]
        got = lax.ppermute(arr[half:], AXES, [(i, i ^ flip) for i in range(ndev)])
        if k + 1 == EARLY:
            return arr, got
        arr = (arr[:half].astype(F32) + got.astype(F32)).astype(BF16)


def finish(block, ndev):
    rest = ndev >> LEVELS
    if rest == 1:
        return block
    step = 1
    me = lax.axis_index("dp") * lax.axis_size("seq") + lax.axis_index("seq")
    arr = block.reshape(rest, block.shape[0] // rest, block.shape[1])
    flip = rest
    while flip > 1:
        flip //= 2
        bit = (me // flip) % 2
        half = arr.shape[0] // 2
        keep = lax.dynamic_slice_in_dim(arr, bit * half, half, 0)
        send = lax.dynamic_slice_in_dim(arr, (1 - bit) * half, half, 0)
        arr = keep + lax.ppermute(send, AXES, [(i, i ^ flip) for i in range(ndev)])
    return arr[0]


def shards(
    layer_input,
    query_weight,
    query_bias,
    key_weight,
    value_weight,
    value_bias,
    output_weight,
    output_bias,
    first_gain,
    first_shift,
    up_weight,
    up_bias,
    down_weight,
    down_bias,
    second_gain,
    second_shift,
    out_cotangent,
    passage_lengths,
):
    parts = lax.axis_size("seq")
    ndev = parts * lax.axis_size("dp")
    rows, width = layer_input.shape
    ff = up_weight.shape[1]
    count = rows * parts
    place = lax.axis_index("seq")
    ahead = [(i, i + 1) for i in range(parts - 1)]
    back = [(i + 1, i) for i in range(parts - 1)]

    x_prev = lax.ppermute(layer_input, "seq", ahead)
    x_next = lax.ppermute(layer_input, "seq", back)
    q, k, v = project_qkv(
        layer_input, query_weight, query_bias, key_weight, value_weight, value_bias
    )
    lengths = passage_lengths[0]
    slots = lengths.shape[0]
    upto = jnp.arange(slots)[:, None] >= jnp.arange(slots)[None, :]
    ends = jnp.sum(jnp.where(upto, lengths[None, :], 0), axis=1)
    start = (place - 1) * rows
    where = start + jnp.arange(3 * rows, dtype=jnp.int32)
    seg = jnp.sum((where[:, None] >= ends[None, :]).astype(jnp.int32), axis=1)
    valid = (where >= 0) & (where < count)
    seg = jnp.where(valid, seg, slots)
    lanes = jnp.arange(PAIR, dtype=jnp.int32) % HEAD_DIM
    match = seg[:, None] == lanes[None, :]
    onehot = jnp.where(match, 1.0, 0.0).astype(BF16)
    qmask = jnp.where(match, 0.0, NEG).astype(BF16)
    heads_at = start + jnp.arange(3 * rows // BQ, dtype=jnp.int32) * BQ
    inside = (heads_at >= 0) & (heads_at < count)
    first_end = jnp.where(ends[None, :] <= heads_at[:, None], ends[None, :], 0)
    lo = jnp.max(first_end, axis=1) - start
    far = heads_at + BQ - 1
    hi = jnp.min(jnp.where(ends[None, :] > far[:, None], ends[None, :], count), axis=1) - start
    own_block = (jnp.arange(3 * rows // BQ) * BQ // rows) == 1
    lo = jnp.where(own_block, jnp.maximum(lo, 0), jnp.maximum(lo, rows))
    hi = jnp.where(own_block, jnp.minimum(hi, 3 * rows), jnp.minimum(hi, 2 * rows))
    lo = (lo // BK).astype(jnp.int32)
    hi = jnp.where(inside, (hi + BK - 1) // BK, 0).astype(jnp.int32)

    qh, kh, vh = project_qkv(
        jnp.concatenate([x_prev, x_next], axis=0),
        query_weight, query_bias, key_weight, value_weight, value_bias,
    )
    ctx, lse = attend_forward(lo, hi, q, k, v, kh, vh, onehot, qmask)
    result, fg, ag, cg, hid, ug, nl, bg, cl, stat, vec, bup = middle(
        layer_input, ctx, out_cotangent, output_weight, output_bias, first_gain,
        first_shift, up_weight, up_bias, down_weight, down_bias, second_gain,
        second_shift, lse,
    )
    g_prev = lax.ppermute(cg, "seq", ahead)
    g_next = lax.ppermute(cg, "seq", back)
    s_prev = lax.ppermute(stat, "seq", ahead)
    s_next = lax.ppermute(stat, "seq", back)
    dn_parts, up_parts, wo_parts = ff_grads(
        ndev, parts, (DN_ORDER, UP_ORDER), hid, bg, nl, ug, cl, ag
    )
    dn_keep, dn_got = first_halves(dn_parts, DN_ORDER, ndev)
    up_keep, up_got = first_halves(up_parts, UP_ORDER, ndev)
    dq, dk, dv = attend_backward(
        lo, hi, q, k, v, qh, kh, vh, cg, g_prev, g_next, stat, s_prev, s_next, onehot, qmask
    )
    ig, dn_sum, up_sum, wo_sum, q_sum, k_sum, v_sum, vecs, bups = tail(
        ndev, parts, layer_input, dq, dk, dv, query_weight, key_weight, value_weight, fg,
        dn_keep, dn_got, up_keep, up_got, wo_parts, vec, bup,
    )
    dn_sum, up_sum, wo_sum, q_sum, k_sum, v_sum = (
        finish(u, ndev) for u in (dn_sum, up_sum, wo_sum, q_sum, k_sum, v_sum)
    )
    me = lax.axis_index("dp") * parts + place
    mine = width // ndev
    cut = lax.dynamic_slice(vecs, (0, me * mine), (8, mine))
    g2g, s2g, db, g1g, s1g, ob, qb, vb = (cut[n] for n in range(8))
    ub = lax.dynamic_slice(bups, (0, me * (ff // ndev)), (1, ff // ndev))[0]
    input_grad = ig
    in_sum = (q_sum, k_sum, v_sum)
    return (
        result, input_grad, in_sum[0], qb, in_sum[1], in_sum[2], vb, wo_sum, ob, g1g, s1g,
        up_sum, ub, dn_sum, db, g2g, s2g,
    )


def solution(mesh):
    split = P(AXES, None)
    part = P(AXES)
    in_specs = (split,) + (P(),) * 15 + (split, P("dp", None))
    out_specs = (
        split, split, split, part, split, split, part, split, part, part, part,
        split, part, split, part, part, part,
    )
    return jax.shard_map(shards, mesh=mesh, in_specs=in_specs, out_specs=out_specs, check_vma=False)
```

```python
import functools

import jax
import jax.numpy as jnp
from jax import lax
from jax.experimental import pallas as pl
from jax.experimental.pallas import tpu as pltpu
from jax.sharding import PartitionSpec as P

HEAD_DIM = 64
PAIR = 2 * HEAD_DIM
AXES = ("dp", "seq")
NEG = -1e30
FLOOR = -3e38
BQ = 256
BK = 128
LEVELS = 5
layer_eps = 1e-12
F32 = jnp.float32
BF16 = jnp.bfloat16


def nn(a, b):
    return lax.dot_general(a, b, (((1,), (0,)), ((), ())), preferred_element_type=F32)


def nt(a, b):
    return lax.dot_general(a, b, (((1,), (1,)), ((), ())), preferred_element_type=F32)


def tn(a, b):
    return lax.dot_general(a, b, (((0,), (0,)), ((), ())), preferred_element_type=F32)


def cost(flops, nbytes, trans=0):
    return pl.CostEstimate(flops=int(flops), bytes_accessed=int(nbytes), transcendentals=int(trans))


def params(limit=56 << 20):
    return pltpu.CompilerParams(vmem_limit_bytes=limit)


def whole():
    return pl.BlockSpec(memory_space=pltpu.VMEM)


def hbm():
    return pl.BlockSpec(memory_space=pl.ANY)


def low_lanes():
    return lax.broadcasted_iota(jnp.int32, (1, PAIR), 1) < HEAD_DIM


def line(ref):
    return ref[...].reshape(1, -1)


def remote_params(number):
    return pltpu.CompilerParams(
        vmem_limit_bytes=60 << 20, collective_id=number, has_side_effects=True
    )


class Links:
    def __init__(self, ndev, parts, send_sems, recv_sems):
        self.ndev, self.parts = ndev, parts
        self.place = lax.axis_index("seq")
        self.row = lax.axis_index("dp")
        self.me = self.row * parts + self.place
        self.shift = ndev >> LEVELS
        self.block = self.me // self.shift
        self.send_sems, self.recv_sems = send_sems, recv_sems
        self.used = 0
        self.started = []
        self.has_prev = self.place > 0
        self.has_next = self.place < parts - 1

    def partner(self, flip):
        other = self.me + (1 - 2 * ((self.me // flip) % 2)) * flip
        return (other // self.parts, other % self.parts)

    def greet(self, flips, neighbours):
        barrier = pltpu.get_barrier_semaphore()

        def signal(device):
            pl.semaphore_signal(
                barrier, inc=1, device_id=device, device_id_type=pl.DeviceIdType.MESH
            )

        for flip in flips:
            signal(self.partner(flip))
        if neighbours:

            @pl.when(self.has_prev)
            def _():
                signal((self.row, self.place - 1))

            @pl.when(self.has_next)
            def _():
                signal((self.row, self.place + 1))

        count = len(flips)
        if neighbours:
            count = count + jnp.minimum(self.place, 1)
            count = count + jnp.minimum(self.parts - 1 - self.place, 1)
        pl.semaphore_wait(barrier, count)

    def make(self, src, dst, device):
        n = self.used
        self.used += 1
        return pltpu.make_async_remote_copy(
            src_ref=src, dst_ref=dst, send_sem=self.send_sems.at[n],
            recv_sem=self.recv_sems.at[n], device_id=device,
            device_id_type=pl.DeviceIdType.MESH,
        )

    def exchange(self, src, dst, flip):
        copy = self.make(src, dst, self.partner(flip))
        copy.start()
        self.started.append(copy)
        return copy

    def finish(self):
        for copy in self.started:
            copy.wait_send()

    def neighbours(self, src, at_next, at_prev):
        ahead = self.make(src, at_next, (self.row, self.place + 1))
        back = self.make(src, at_prev, (self.row, self.place - 1))

        @pl.when(self.has_next)
        def _():
            ahead.start()

        @pl.when(self.has_prev)
        def _():
            back.start()

        return ahead, back

    def from_prev(self, pair):
        @pl.when(self.has_prev)
        def _():
            pair[0].wait_recv()

    def from_next(self, pair):
        @pl.when(self.has_next)
        def _():
            pair[1].wait_recv()

    def sent(self, pair):
        @pl.when(self.has_next)
        def _():
            pair[0].wait_send()

        @pl.when(self.has_prev)
        def _():
            pair[1].wait_send()


def both(a, b):
    return (a.astype(F32) + b.astype(F32)).astype(BF16)


class Chain:
    def __init__(self, links, buf, recv, order, step):
        self.links, self.buf, self.recv, self.order, self.step = links, buf, recv, order, step
        self.base = 0

    def position(self, c):
        at = 0
        for k, b in enumerate(self.order):
            mine, its = (self.links.block // (1 << b)) % 2, (c // (1 << b)) % 2
            at = at + (mine + its - 2 * mine * its) * (1 << (LEVELS - 1 - k))
        return at

    def send(self):
        self.half = (1 << LEVELS) >> (self.step + 1)
        self.copy = self.links.exchange(
            self.buf.at[pl.ds(self.half, self.half)],
            self.recv.at[pl.ds(self.base, self.half)],
            self.links.shift << self.order[self.step],
        )

    def receive(self):
        self.copy.wait_recv()
        self.base += self.half
        self.step += 1

    def add(self):
        base, half, buf, recv = self.base, self.half, self.buf, self.recv
        self.receive()
        if half > 1:

            @pl.loop(0, half)
            def _(i):
                buf[i] = both(buf[i], recv[base + i])

            self.send()

    def last(self):
        return self.buf[0].astype(F32) + self.recv[self.base - 1].astype(F32)


DN_ONE = (0, 2, 1, 3, 4)
DN_TWO = (0, 1, 2, 3, 4)
UP_ONE = (0, 2, 3, 1, 4)
UP_TWO = (0, 1, 3, 2, 4)
OUT_ORDER = (0, 2, 1, 3, 4)
Q_ORDER = (0, 2, 1, 3, 4)
K_ORDER = (0, 1, 2, 3, 4)
V_ORDER = (0, 1, 3, 2, 4)
BLOCKS = 1 << LEVELS


def first_kernel(
    ndev, parts, x_ref, lengths, wq_hbm, bq, wk_hbm, wv_hbm, bv,
    q_ref, k_ref, v_ref, onehot, qmask, bounds,
    halo, wq, wk, wv, load_sems, send_sems, recv_sems,
):
    rows, width = x_ref.shape
    count = rows * parts
    loads = [
        pltpu.make_async_copy(src, dst, load_sems.at[n])
        for n, (src, dst) in enumerate(((wq_hbm, wq), (wk_hbm, wk), (wv_hbm, wv)))
    ]
    for load in loads:
        load.start()
    links = Links(ndev, parts, send_sems, recv_sems)
    links.greet([], True)
    step = rows // 2
    pairs = [
        links.neighbours(
            x_ref.at[pl.ds(h * step, step)],
            halo.at[0, pl.ds(h * step, step)],
            halo.at[1, pl.ds(h * step, step)],
        )
        for h in range(2)
    ]

    @pl.when(jnp.logical_not(links.has_prev))
    def _():
        halo[0] = jnp.zeros((rows, width), BF16)

    @pl.when(jnp.logical_not(links.has_next))
    def _():
        halo[1] = jnp.zeros((rows, width), BF16)

    for load in loads:
        load.wait()

    def project(x, at):
        q_ref[at, :] = (nn(x, wq[...]) + line(bq)).astype(BF16)
        k_ref[at, :] = nn(x, wk[...]).astype(BF16)
        v_ref[at, :] = (nn(x, wv[...]) + line(bv)).astype(BF16)

    project(x_ref[...], slice(rows, 2 * rows))

    slots = lengths.shape[1]
    ends, total = [], jnp.int32(0)
    for n in range(slots):
        total = total + lengths[0, n]
        ends.append(total)
    start = (links.place - 1) * rows
    lane = lax.broadcasted_iota(jnp.int32, (BQ, PAIR), 1) % HEAD_DIM
    one, none, far = BF16(1.0), BF16(0.0), BF16(NEG)

    @pl.loop(0, 3 * rows // BQ)
    def _(i):
        at = start + i * BQ
        where = at + lax.broadcasted_iota(jnp.int32, (BQ, PAIR), 0)
        seg = jnp.zeros((BQ, PAIR), jnp.int32)
        for end in ends:
            seg = seg + (where >= end).astype(jnp.int32)
        outside = (where < 0) | (where >= count)
        seg = jnp.where(outside, slots, seg)
        match = (seg == lane).astype(F32)
        to = pl.ds(pl.multiple_of(i * BQ, BQ), BQ)
        onehot[to, :] = match.astype(BF16)
        qmask[to, :] = ((1.0 - match) * NEG).astype(BF16)

    for n in range(rows // BQ):
        near = links.place * rows + n * BQ
        far_row = near + BQ - 1
        lo, hi = jnp.int32(0), jnp.int32(count)
        for end in ends:
            lo = jnp.where(end <= near, jnp.maximum(lo, end), lo)
            hi = jnp.where(end > far_row, jnp.minimum(hi, end), hi)
        lo = jnp.maximum(lo - start, 0)
        hi = jnp.minimum(hi - start, 3 * rows)
        bounds[0, n] = lo // BK
        bounds[1, n] = (hi + BK - 1) // BK

    for h in range(2):
        links.from_prev(pairs[h])
        project(halo[0, h * step : (h + 1) * step, :], slice(h * step, (h + 1) * step))
        links.from_next(pairs[h])
        at = 2 * rows + h * step
        project(halo[1, h * step : (h + 1) * step, :], slice(at, at + step))
    for pair in pairs:
        links.sent(pair)


def first(ndev, parts, x, lengths, wq, bq, wk, wv, bv):
    rows, width = x.shape
    ext = jax.ShapeDtypeStruct((3 * rows, width), BF16)
    seg = jax.ShapeDtypeStruct((3 * rows, PAIR), BF16)
    smem = pl.BlockSpec(memory_space=pltpu.SMEM)
    return pl.pallas_call(
        functools.partial(first_kernel, ndev, parts),
        in_specs=[whole(), smem, hbm(), whole(), hbm(), hbm(), whole()],
        out_specs=[whole()] * 5 + [smem],
        out_shape=[ext] * 3 + [seg] * 2 + [jax.ShapeDtypeStruct((2, rows // BQ), jnp.int32)],
        scratch_shapes=[
            pltpu.VMEM((2, rows, width), BF16),
            pltpu.VMEM((width, width), BF16),
            pltpu.VMEM((width, width), BF16),
            pltpu.VMEM((width, width), BF16),
            pltpu.SemaphoreType.DMA((3,)),
            pltpu.SemaphoreType.DMA((4,)),
            pltpu.SemaphoreType.DMA((4,)),
        ],
        compiler_params=remote_params(0),
        cost_estimate=cost(15e9, 12 << 20),
        name="first",
    )(x, lengths, wq, bq, wk, wv, bv)


def lengths_of(rows):
    most = BQ // BK + 2 * -(-(rows - 1) // BK)
    return [n for n in range(2, most) if n <= 6 or n % 2 == 0] + [most]


def key_range(bounds, i, rows):
    lo, hi = bounds[0, i], bounds[1, i]
    sizes = lengths_of(rows)
    number = jnp.int32(sizes[-1])
    for n in reversed(sizes):
        number = jnp.where(hi - lo <= n, n, number)
    return jnp.minimum(lo, 3 * rows // BK - number), number


def forward_kernel(bounds, q_ref, k_ref, v_ref, onehot, qmask, ctx_ref, lse_ref, ka, kb):
    rows = ctx_ref.shape[0]
    low = low_lanes()
    key, hot = k_ref[...], onehot[...]
    ka[...] = jnp.where(low, key, hot).T
    kb[...] = jnp.where(low, hot, key).T

    @pl.loop(0, rows // BQ)
    def _(i):
        first_block, number = key_range(bounds, i, rows)
        base = pl.multiple_of(first_block * BK, BK)
        at = pl.ds(pl.multiple_of(i * BQ, BQ), BQ)
        own = pl.ds(pl.multiple_of(rows + i * BQ, BQ), BQ)
        for num in lengths_of(rows):

            @pl.when(number == num)
            def _():
                span = pl.ds(base, num * BK)
                query = q_ref[own, :] * BF16(HEAD_DIM**-0.5)
                mask = qmask[own, :]
                parts = []
                for head, keys in enumerate((ka, kb)):
                    pick = (query, mask) if head == 0 else (mask, query)
                    scores = nn(jnp.where(low, *pick), keys[:, span])
                    top = jnp.max(scores, axis=1, keepdims=True)
                    weights = jnp.exp(scores - top)
                    total = jnp.sum(weights, axis=1, keepdims=True)
                    acc = nn(weights.astype(BF16), v_ref[span, :])
                    parts.append((acc / total, top + jnp.log(total)))
                ctx_ref[at, :] = jnp.where(low, parts[0][0], parts[1][0])
                flip = jnp.where(low, parts[0][1], parts[1][1]).T
                lse_ref[0, 0:1, at] = flip[0:1]
                lse_ref[0, 1:2, at] = flip[HEAD_DIM : HEAD_DIM + 1]


def attend_forward(bounds, q, k, v, onehot, qmask):
    rows, width = q.shape[0] // 3, q.shape[1]
    pairs = width // PAIR
    ext = pl.BlockSpec((3 * rows, PAIR), lambda p, *_: (0, p))
    seg = pl.BlockSpec((3 * rows, PAIR), lambda p, *_: (0, 0))
    grid = pltpu.PrefetchScalarGridSpec(
        num_scalar_prefetch=1,
        grid=(pairs,),
        in_specs=[ext, ext, ext, seg, seg],
        out_specs=[
            pl.BlockSpec((rows, PAIR), lambda p, *_: (0, p)),
            pl.BlockSpec((1, 2, rows), lambda p, *_: (p, 0, 0)),
        ],
        scratch_shapes=[
            pltpu.VMEM((PAIR, 3 * rows), BF16),
            pltpu.VMEM((PAIR, 3 * rows), BF16),
        ],
    )
    return pl.pallas_call(
        forward_kernel,
        grid_spec=grid,
        out_shape=[
            jax.ShapeDtypeStruct((rows, width), F32),
            jax.ShapeDtypeStruct((pairs, 2, rows), F32),
        ],
        compiler_params=params(),
        cost_estimate=cost(20e9, 24 * rows * width),
        name="attend_forward",
    )(bounds, q, k, v, onehot, qmask)


def backward_kernel(
    bounds, q_ref, k_ref, v_ref, g_ref, stat_ref, onehot, qmask,
    dq_ref, dk_ref, dv_ref, ka, kb, vt, qa, qb, gt,
):
    rows = dq_ref.shape[0]
    low = low_lanes()
    zero = jnp.zeros((1, PAIR), BF16)
    scale = BF16(HEAD_DIM**-0.5)
    key, hot = k_ref[...], onehot[...]
    ka[...] = jnp.where(low, key, hot).T
    kb[...] = jnp.where(low, hot, key).T
    query, mask = q_ref[...] * scale, qmask[...]
    qa[...] = jnp.where(low, query, mask).T
    qb[...] = jnp.where(low, mask, query).T
    vt[...] = v_ref[...].T
    gt[...] = g_ref[...].T

    @pl.loop(0, rows // BQ)
    def _(i):
        first_block, number = key_range(bounds, i, rows)
        base = pl.multiple_of(first_block * BK, BK)
        at = pl.ds(pl.multiple_of(i * BQ, BQ), BQ)
        own = pl.ds(pl.multiple_of(rows + i * BQ, BQ), BQ)
        for num in lengths_of(rows):

            @pl.when(number == num)
            def _():
                span = pl.ds(base, num * BK)

                def pick(head, value, other):
                    return jnp.where(low, value, other) if head == 0 else jnp.where(
                        low, other, value
                    )

                columns = stat_ref[0, :, own]
                columns = jnp.concatenate([columns, columns], axis=0).T
                out = []
                for head, keys in enumerate((ka, kb)):
                    queries = pick(head, q_ref[own, :] * scale, qmask[own, :])
                    grads = pick(head, g_ref[own, :], zero)
                    scores = nn(queries, keys[:, span])
                    prob_grad = nn(grads, vt[:, span])
                    probs = jnp.exp(scores - columns[:, head : head + 1])
                    delta = columns[:, 2 + head : 3 + head]
                    score_grad = (probs * (prob_grad - delta)).astype(BF16)
                    out.append(nn(score_grad, k_ref[span, :]))
                dq = jnp.where(low, out[0], out[1]) * F32(HEAD_DIM**-0.5)
                dq_ref[at, :] = dq.astype(BF16)
                out = []
                for head, queries in enumerate((qa, qb)):
                    keys = pick(head, k_ref[own, :], onehot[own, :])
                    vals = pick(head, v_ref[own, :], zero)
                    scores = nn(keys, queries[:, span])
                    prob_grad = nn(vals, gt[:, span])
                    probs = jnp.exp(scores - stat_ref[0, head : head + 1, span])
                    delta = stat_ref[0, 2 + head : 3 + head, span]
                    score_grad = (probs * (prob_grad - delta)).astype(BF16)
                    out.append((
                        nn(score_grad, q_ref[span, :] * scale),
                        nn(probs.astype(BF16), g_ref[span, :]),
                    ))
                dk_ref[at, :] = jnp.where(low, out[0][0], out[1][0]).astype(BF16)
                dv_ref[at, :] = jnp.where(low, out[0][1], out[1][1]).astype(BF16)


def attend_backward(bounds, q, k, v, g, stat, onehot, qmask):
    rows, width = q.shape[0] // 3, q.shape[1]
    pairs = width // PAIR
    ext = pl.BlockSpec((3 * rows, PAIR), lambda p, *_: (0, p))
    own = pl.BlockSpec((rows, PAIR), lambda p, *_: (0, p))
    seg = pl.BlockSpec((3 * rows, PAIR), lambda p, *_: (0, 0))
    grid = pltpu.PrefetchScalarGridSpec(
        num_scalar_prefetch=1,
        grid=(pairs,),
        in_specs=[ext] * 4 + [pl.BlockSpec((1, 4, 3 * rows), lambda p, *_: (p, 0, 0)), seg, seg],
        out_specs=[own] * 3,
        scratch_shapes=[pltpu.VMEM((PAIR, 3 * rows), BF16)] * 6,
    )
    return pl.pallas_call(
        backward_kernel,
        grid_spec=grid,
        out_shape=[jax.ShapeDtypeStruct((rows, width), BF16)] * 3,
        compiler_params=params(),
        cost_estimate=cost(40e9, 40 * rows * width),
        name="attend_backward",
    )(bounds, q, k, v, g, stat, onehot, qmask)


def norm_forward(h):
    mean = jnp.mean(h, axis=-1, keepdims=True)
    centred = h - mean
    variance = jnp.mean(centred * centred, axis=-1, keepdims=True)
    inverse = lax.rsqrt(variance + layer_eps)
    return centred * inverse, inverse


def norm_backward(grad, gain, hat, inverse):
    g = grad * gain
    return inverse * (
        g - jnp.mean(g, axis=-1, keepdims=True) - hat * jnp.mean(g * hat, axis=-1, keepdims=True)
    )


def colsum(v):
    return jnp.sum(v, axis=0, keepdims=True)


def middle_kernel(
    ndev, parts,
    x_ref, ctx_ref, ct_ref, wo, bo, g1, s1, wup_hbm, bup, wdn_hbm, bdn, g2, s2, lse_ref,
    result_ref, fg_ref, g_ref, stat_ref, vec_ref, bup_ref,
    dn_one, dn_two_keep, dn_two_send, up_one_keep, up_one_send, up_two_keep, up_two_send, wo_ref,
    wup, wdn, hid, nl, bg, cl, ag, slope, normed, inv, acc, grad_s,
    one_s, one_r, two_s, two_r, upa_s, upa_r, upb_s, upb_r, wo_s, wo_r,
    load_sems, send_sems, recv_sems,
):
    rows, width = x_ref.shape
    ff = wup.shape[1]
    rc, fc = 256, 512
    chunks, tiles = rows // rc, ff // fc
    tall, short = ff // BLOCKS, width // BLOCKS
    up_copy = pltpu.make_async_copy(wup_hbm, wup, load_sems.at[0])
    dn_copy = pltpu.make_async_copy(wdn_hbm, wdn, load_sems.at[1])
    up_copy.start()
    dn_copy.start()
    links = Links(ndev, parts, send_sems, recv_sems)
    links.greet([links.shift << DN_ONE[0], links.shift << DN_ONE[1]], True)
    one = Chain(links, one_s, one_r, DN_ONE, 0)
    two = Chain(links, two_s, two_r, DN_TWO, 0)
    upa = Chain(links, upa_s, upa_r, UP_ONE, 0)
    upb = Chain(links, upb_s, upb_r, UP_TWO, 0)
    out = Chain(links, wo_s, wo_r, OUT_ORDER, 0)

    @pl.loop(0, chunks)
    def _(r):
        at = pl.ds(pl.multiple_of(r * rc, rc), rc)
        c_low = ctx_ref[at, :].astype(BF16)
        cl[at, :] = c_low
        h = x_ref[at, :].astype(F32) + (nn(c_low, wo[...]) + line(bo))
        xhat, inverse = norm_forward(h)
        res = xhat * line(g1) + line(s1)
        fg_ref[at, :] = xhat
        inv[at, :] = inverse
        normed[at, :] = res
        nl[at, :] = res.astype(BF16)

    up_copy.wait()
    dn_copy.wait()
    acc[...] = jnp.zeros_like(acc)

    @pl.loop(0, tiles)
    def _(j):
        cols = pl.ds(pl.multiple_of(j * fc, fc), fc)
        bias = bup[cols].reshape(1, fc)
        for r in range(chunks):
            at = slice(r * rc, (r + 1) * rc)
            up = nn(nl[at, :], wup[:, cols]) + bias
            cdf = 0.5 * (1.0 + lax.erf(up * F32(0.5**0.5)))
            density = jnp.exp(-0.5 * up * up) * F32(0.3989422804014327)
            slope[at, cols] = cdf + up * density
            act = (up * cdf).astype(BF16)
            hid[at, cols] = act
            acc[at, :] = acc[at, :] + nn(act, wdn[cols, :])

    vec_ref[...] = jnp.zeros_like(vec_ref)

    @pl.loop(0, chunks)
    def _(r):
        at = pl.ds(pl.multiple_of(r * rc, rc), rc)
        xhat, inverse = norm_forward(normed[at, :] + (acc[at, :] + line(bdn)))
        result_ref[at, :] = (xhat * line(g2) + line(s2)).astype(BF16)
        ct = ct_ref[at, :].astype(F32)
        second = norm_backward(ct, line(g2), xhat, inverse)
        low = second.astype(BF16)
        bg[at, :] = low
        acc[at, :] = second
        vec_ref[0:1, :] = vec_ref[0:1, :] + colsum(ct * xhat)
        vec_ref[1:2, :] = vec_ref[1:2, :] + colsum(ct)
        vec_ref[2:3, :] = vec_ref[2:3, :] + colsum(low.astype(F32))

    some = width // tall

    @pl.loop(0, ff // width)
    def _(j):
        grad_s[...] = tn(hid[:, pl.ds(pl.multiple_of(j * width, width), width)], bg[...])

        @pl.loop(0, some)
        def _(c):
            base = pl.multiple_of(c * tall, tall // 2)
            one_s[one.position(j * some + c)] = grad_s[pl.ds(base, tall // 2), :].astype(BF16)
            base = pl.multiple_of(c * tall + tall // 2, tall // 2)
            two_s[two.position(j * some + c)] = grad_s[pl.ds(base, tall // 2), :].astype(BF16)

    one.send()
    two.send()

    def back_tiles(lo, hi):
        @pl.loop(lo, hi)
        def _(j):
            cols = pl.ds(pl.multiple_of(j * fc, fc), fc)
            sums = jnp.zeros((1, fc), F32)
            for r in range(chunks):
                at = slice(r * rc, (r + 1) * rc)
                grad = (nt(bg[at, :], wdn[cols, :]) * slope[at, cols]).astype(BF16)
                hid[at, cols] = grad
                sums = sums + colsum(grad.astype(F32))
                acc[at, :] = acc[at, :] + nt(grad, wup[:, cols])
            bup_ref[:, cols] = sums

    back_tiles(0, tiles - 2)
    one.add()
    back_tiles(tiles - 2, tiles)

    @pl.when(jnp.logical_not(links.has_prev))
    def _():
        g_ref[0:rows, :] = jnp.zeros((rows, width), BF16)
        stat_ref[:, :, 0:rows] = jnp.zeros((width // PAIR, 4, rows), F32)

    @pl.when(jnp.logical_not(links.has_next))
    def _():
        g_ref[2 * rows : 3 * rows, :] = jnp.zeros((rows, width), BF16)
        stat_ref[:, :, 2 * rows : 3 * rows] = jnp.zeros((width // PAIR, 4, rows), F32)

    pairs = []
    for r in range(chunks):
        at = slice(r * rc, (r + 1) * rc)
        mid = slice(rows + r * rc, rows + (r + 1) * rc)
        total = acc[at, :]
        xhat = fg_ref[at, :]
        first_grad = norm_backward(total, line(g1), xhat, inv[at, :])
        fg_ref[at, :] = first_grad
        low = first_grad.astype(BF16)
        ag[at, :] = low
        vec_ref[3:4, :] = vec_ref[3:4, :] + colsum(total * xhat)
        vec_ref[4:5, :] = vec_ref[4:5, :] + colsum(total)
        vec_ref[5:6, :] = vec_ref[5:6, :] + colsum(low.astype(F32))
        cg = nt(low, wo[...]).astype(BF16)
        g_ref[mid, :] = cg
        pairs.append(links.neighbours(
            g_ref.at[pl.ds(rows + r * rc, rc)],
            g_ref.at[pl.ds(r * rc, rc)],
            g_ref.at[pl.ds(2 * rows + r * rc, rc)],
        ))
        prod = cg.astype(F32) * ctx_ref[at, :]
        for p in range(width // PAIR):
            flip = prod[:, p * PAIR : (p + 1) * PAIR].T
            stat_ref[p, 2:3, mid] = colsum(flip[:HEAD_DIM])
            stat_ref[p, 3:4, mid] = colsum(flip[HEAD_DIM:])
    for p in range(width // PAIR):
        stat_ref[p, 0:2, rows : 2 * rows] = lse_ref[p]
    pairs.append(links.neighbours(
        stat_ref.at[:, :, pl.ds(rows, rows)],
        stat_ref.at[:, :, pl.ds(0, rows)],
        stat_ref.at[:, :, pl.ds(2 * rows, rows)],
    ))

    for n in range(ff // width):
        chain = (upa, upb)[n // 2]
        grad_s[...] = tn(nl[...], hid[:, n * width : (n + 1) * width])
        to = slice((n % 2) * width, (n % 2 + 1) * width)

        @pl.loop(0, BLOCKS)
        def _(c):
            at = pl.ds(pl.multiple_of(c * short, short), short)
            chain.buf[chain.position(c), :, to] = grad_s[at, :].astype(BF16)

        if n % 2 == 1:
            chain.send()

    grad_s[...] = tn(cl[...], ag[...])

    @pl.loop(0, BLOCKS)
    def _(c):
        at = pl.ds(pl.multiple_of(c * short, short), short)
        wo_s[out.position(c)] = grad_s[at, :].astype(BF16)

    out.send()

    def settle(chain, keep, send):
        chain.receive()
        half = BLOCKS // 4

        @pl.loop(0, half)
        def _(i):
            keep[i] = both(chain.buf[i], chain.recv[i])
            send[i] = both(chain.buf[half + i], chain.recv[half + i])

    settle(two, dn_two_keep, dn_two_send)
    settle(upa, up_one_keep, up_one_send)
    settle(upb, up_two_keep, up_two_send)
    out.receive()

    @pl.loop(0, BLOCKS // 2)
    def _(i):
        wo_ref[i] = both(wo_s[i], wo_r[i])

    one.receive()

    @pl.loop(0, BLOCKS // 4)
    def _(i):
        dn_one[i] = both(one_s[i], one_r[BLOCKS // 2 + i])

    for pair in pairs:
        links.from_prev(pair)
        links.from_next(pair)
        links.sent(pair)
    links.finish()


def middle(ndev, parts, x, ctx, ct, wo, bo, g1, s1, wup, bup, wdn, bdn, g2, s2, lse):
    rows, width = x.shape
    ff = wup.shape[1]
    pairs = width // PAIR
    tall, short = ff // BLOCKS, width // BLOCKS
    left = BLOCKS // 4

    def out(*shape, dtype=BF16):
        return jax.ShapeDtypeStruct(shape, dtype)

    shapes = [
        out(rows, width),
        out(rows, width, dtype=F32),
        out(3 * rows, width),
        out(pairs, 4, 3 * rows, dtype=F32),
        out(8, width, dtype=F32),
        out(1, ff, dtype=F32),
        out(left, tall // 2, width),
        out(left, tall // 2, width),
        out(left, tall // 2, width),
        out(left, short, ff // 2),
        out(left, short, ff // 2),
        out(left, short, ff // 2),
        out(left, short, ff // 2),
        out(BLOCKS // 2, short, width),
    ]

    def chain(*shape):
        return [pltpu.VMEM((BLOCKS,) + shape, BF16), pltpu.VMEM((BLOCKS // 2,) + shape, BF16)]

    dn_one = chain(tall // 2, width)
    dn_one[1] = pltpu.VMEM((3 * BLOCKS // 4, tall // 2, width), BF16)
    copies = 6 + 6
    return pl.pallas_call(
        functools.partial(middle_kernel, ndev, parts),
        in_specs=[whole()] * 7 + [hbm(), whole(), hbm()] + [whole()] * 4,
        out_specs=[whole()] * len(shapes),
        out_shape=shapes,
        scratch_shapes=[
            pltpu.VMEM((width, ff), BF16),
            pltpu.VMEM((ff, width), BF16),
            pltpu.VMEM((rows, ff), BF16),
            pltpu.VMEM((rows, width), BF16),
            pltpu.VMEM((rows, width), BF16),
            pltpu.VMEM((rows, width), BF16),
            pltpu.VMEM((rows, width), BF16),
            pltpu.VMEM((rows, ff), F32),
            pltpu.VMEM((rows, width), F32),
            pltpu.VMEM((rows, 1), F32),
            pltpu.VMEM((rows, width), F32),
            pltpu.VMEM((width, width), F32),
        ]
        + dn_one + chain(tall // 2, width) + chain(short, ff // 2) * 2 + chain(short, width)
        + [
            pltpu.SemaphoreType.DMA((2,)),
            pltpu.SemaphoreType.DMA((copies,)),
            pltpu.SemaphoreType.DMA((copies,)),
        ],
        compiler_params=remote_params(1),
        cost_estimate=cost(50e9, 30 << 20),
        name="middle",
    )(x, ctx, ct, wo, bo, g1, s1, wup, bup, wdn, bdn, g2, s2, lse)


def tail_kernel(
    ndev, parts,
    x, dq, dk, dv, wq, wk, wv, fg, dn_one, dn_keep, dn_got, upa_keep, upa_got, upb_keep, upb_got,
    wo_in, vec, bup,
    ig_ref, dn1_out, dn2_out, up1_out, up2_out, wo_out, q_out, k_out, v_out, vec_out, bup_out,
    one_s, one_r, two_s, two_r, upa_s, upa_r, upb_s, upb_r, wo_s, wo_r, q_s, q_r, k_s, k_r,
    v_s, v_r, grad_s, vec_s, vec_r, bup_s, bup_r,
    load_sems, send_sems, recv_sems,
):
    width = x.shape[1]
    short = width // BLOCKS
    loads = [
        pltpu.make_async_copy(dn_one, one_s, load_sems.at[0]),
        pltpu.make_async_copy(wo_in, wo_s, load_sems.at[1]),
    ]
    for load in loads:
        load.start()
    links = Links(ndev, parts, send_sems, recv_sems)
    flips = [1 << n for n in range(ndev.bit_length() - 1)]
    links.greet(flips, False)
    one = Chain(links, one_s, one_r, DN_ONE, 2)
    two = Chain(links, two_s, two_r, DN_TWO, 2)
    upa = Chain(links, upa_s, upa_r, UP_ONE, 2)
    upb = Chain(links, upb_s, upb_r, UP_TWO, 2)
    out = Chain(links, wo_s, wo_r, OUT_ORDER, 1)
    qc = Chain(links, q_s, q_r, Q_ORDER, 0)
    kc = Chain(links, k_s, k_r, K_ORDER, 0)
    vc = Chain(links, v_s, v_r, V_ORDER, 0)

    def begin(chain, keep, got):
        @pl.loop(0, BLOCKS // 4)
        def _(i):
            chain.buf[i] = both(keep[i], got[i])

        chain.send()

    begin(two, dn_keep, dn_got)
    loads[0].wait()
    one.send()
    begin(upa, upa_keep, upa_got)
    begin(upb, upb_keep, upb_got)
    loads[1].wait()
    out.send()

    def weight(chain, grad):
        grad_s[...] = tn(x[...], grad[...])

        @pl.loop(0, BLOCKS)
        def _(c):
            at = pl.ds(pl.multiple_of(c * short, short), short)
            chain.buf[chain.position(c)] = grad_s[at, :].astype(BF16)

        chain.send()

    weight(qc, dq)
    weight(kc, dk)
    weight(vc, dv)
    vec_s[0] = vec[...]
    vec_s[0, 6:7, :] = colsum(dq[...].astype(F32))
    vec_s[0, 7:8, :] = colsum(dv[...].astype(F32))
    bup_s[0] = bup[...]

    def vectors(n):
        if n >= len(flips):
            return None
        return [
            links.exchange(vec_s.at[n], vec_r.at[n], flips[n]),
            links.exchange(bup_s.at[n], bup_r.at[n], flips[n]),
        ]

    def add_vectors(n, copies):
        for c in copies:
            c.wait_recv()
        vec_s[n + 1] = vec_s[n] + vec_r[n]
        bup_s[n + 1] = bup_s[n] + bup_r[n]
        return vectors(n + 1)

    pending = vectors(0)
    qc.add()
    kc.add()
    vc.add()
    ig_ref[...] = (
        nt(dq[...], wq[...]) + nt(dk[...], wk[...]) + nt(dv[...], wv[...]) + fg[...]
    ).astype(BF16)
    pending = add_vectors(0, pending)
    two.add()
    one.add()
    out.add()
    upa.add()
    upb.add()
    pending = add_vectors(1, pending)
    qc.add()
    kc.add()
    vc.add()
    two.add()
    one.add()
    out.add()
    upa.add()
    upb.add()
    pending = add_vectors(2, pending)
    qc.add()
    kc.add()
    vc.add()
    two.add()
    one.add()
    upa.add()
    upb.add()
    out.add()
    pending = add_vectors(3, pending)
    dn1_out[...] = one.last()
    dn2_out[...] = two.last()
    up1_out[...] = upa.last()
    up2_out[...] = upb.last()
    qc.add()
    kc.add()
    vc.add()
    out.add()
    wo_out[...] = out.last()
    for n in range(4, len(flips)):
        pending = add_vectors(n, pending)
    vec_out[...] = vec_s[len(flips)]
    bup_out[...] = bup_s[len(flips)]
    qc.add()
    kc.add()
    vc.add()
    q_out[...] = qc.last()
    k_out[...] = kc.last()
    v_out[...] = vc.last()
    links.finish()


def tail(ndev, parts, x, dq, dk, dv, wq, wk, wv, fg, one, two, upa, upb, wo, vec, bup):
    rows, width = x.shape
    short = width // BLOCKS
    tall, ff = one.shape[1] * 2, upa[0].shape[2] * 2
    steps = ndev.bit_length() - 1

    def out(*shape):
        return jax.ShapeDtypeStruct(shape, F32)

    def chain(step, *shape):
        return [pltpu.VMEM((BLOCKS >> step,) + shape, BF16)] * 2

    copies = 4 * 3 + 4 + 3 * 5 + 2 * steps
    return pl.pallas_call(
        functools.partial(tail_kernel, ndev, parts),
        in_specs=[whole()] * 8 + [hbm()] + [whole()] * 6 + [hbm(), whole(), whole()],
        out_specs=[whole()] * 11,
        out_shape=[
            jax.ShapeDtypeStruct((rows, width), BF16),
            out(tall // 2, width), out(tall // 2, width), out(short, ff // 2), out(short, ff // 2),
            out(short, width), out(short, width), out(short, width), out(short, width),
            out(8, width), out(1, ff),
        ],
        scratch_shapes=chain(2, tall // 2, width) * 2
        + chain(2, short, ff // 2) * 2
        + chain(1, short, width)
        + chain(0, short, width) * 3
        + [
            pltpu.VMEM((width, width), F32),
            pltpu.VMEM((steps + 1, 8, width), F32),
            pltpu.VMEM((steps, 8, width), F32),
            pltpu.VMEM((steps + 1, 1, ff), F32),
            pltpu.VMEM((steps, 1, ff), F32),
            pltpu.SemaphoreType.DMA((2,)),
            pltpu.SemaphoreType.DMA((copies,)),
            pltpu.SemaphoreType.DMA((copies,)),
        ],
        compiler_params=remote_params(2),
        cost_estimate=cost(60e9, 16 << 20),
        name="tail",
    )(x, dq, dk, dv, wq, wk, wv, fg, one, *two, *upa, *upb, wo, vec, bup)


def write_kernel(
    ndev, parts, ig, dn1, dn2, up1, up2, wo, q, k, v, vec, bup,
    ig_out, dn_out, up_out, wo_out, q_out, k_out, v_out,
    g2_out, s2_out, db_out, g1_out, s1_out, ob_out, qb_out, vb_out, ub_out,
    sem,
):
    copy = pltpu.make_async_copy(ig, ig_out, sem)
    copy.start()
    me = lax.axis_index("dp") * parts + lax.axis_index("seq")
    half = dn1.shape[0]
    dn_out[0:half, :] = dn1[...]
    dn_out[half : 2 * half, :] = dn2[...]
    half = up1.shape[1]
    up_out[:, 0:half] = up1[...]
    up_out[:, half : 2 * half] = up2[...]
    wo_out[...] = wo[...]
    q_out[...] = q[...]
    k_out[...] = k[...]
    v_out[...] = v[...]
    width, ff = vec.shape[1], bup.shape[1]
    mine = width // ndev
    mid = pltpu.roll(vec[...], lax.rem(width - me * mine, width), 1)[:, :128]
    for n, ref in enumerate((g2_out, s2_out, db_out, g1_out, s1_out, ob_out, qb_out, vb_out)):
        ref[...] = mid[n, :mine]
    wide = jnp.broadcast_to(bup[...], (8, ff))
    wide = pltpu.roll(wide, lax.rem(ff - me * (ff // ndev), ff), 1)[:, :128]
    ub_out[...] = wide[0, : ff // ndev]
    copy.wait()


def write(ndev, parts, ig, dn1, dn2, up1, up2, wo, q, k, v, vec, bup):
    width, ff = vec.shape[1], bup.shape[1]

    def out(*shape):
        return jax.ShapeDtypeStruct(shape, F32)

    shapes = [
        jax.ShapeDtypeStruct(ig.shape, BF16),
        out(2 * dn1.shape[0], width), out(up1.shape[0], ff), out(*wo.shape), out(*q.shape),
        out(*k.shape), out(*v.shape),
    ] + [out(width // ndev)] * 8 + [out(ff // ndev)]
    return pl.pallas_call(
        functools.partial(write_kernel, ndev, parts),
        in_specs=[hbm()] + [whole()] * 10,
        out_specs=[hbm()] + [whole()] * 15,
        out_shape=shapes,
        scratch_shapes=[pltpu.SemaphoreType.DMA(())],
        compiler_params=params(),
        name="write",
    )(ig, dn1, dn2, up1, up2, wo, q, k, v, vec, bup)


def finish(block, ndev):
    rest = ndev >> LEVELS
    if rest == 1:
        return block
    step = 1
    me = lax.axis_index("dp") * lax.axis_size("seq") + lax.axis_index("seq")
    arr = block.reshape(rest, block.shape[0] // rest, block.shape[1])
    flip = rest
    while flip > 1:
        flip //= 2
        bit = (me // flip) % 2
        half = arr.shape[0] // 2
        keep = lax.dynamic_slice_in_dim(arr, bit * half, half, 0)
        send = lax.dynamic_slice_in_dim(arr, (1 - bit) * half, half, 0)
        arr = keep + lax.ppermute(send, AXES, [(i, i ^ flip) for i in range(ndev)])
    return arr[0]


def shards(
    layer_input,
    query_weight,
    query_bias,
    key_weight,
    value_weight,
    value_bias,
    output_weight,
    output_bias,
    first_gain,
    first_shift,
    up_weight,
    up_bias,
    down_weight,
    down_bias,
    second_gain,
    second_shift,
    out_cotangent,
    passage_lengths,
):
    parts = lax.axis_size("seq")
    ndev = parts * lax.axis_size("dp")
    shift = ndev >> LEVELS
    q, k, v, onehot, qmask, bounds = first(
        ndev, parts, layer_input, passage_lengths, query_weight, query_bias, key_weight,
        value_weight, value_bias,
    )
    ctx, lse = attend_forward(bounds, q, k, v, onehot, qmask)
    (
        result, fg, grads, stat, vec, bup, one, two_keep, two_send, upa_keep, upa_send, upb_keep,
        upb_send, wo,
    ) = middle(
        ndev, parts, layer_input, ctx, out_cotangent, output_weight, output_bias, first_gain,
        first_shift, up_weight, up_bias, down_weight, down_bias, second_gain, second_shift, lse,
    )

    def second_step(send, order):
        flip = shift << order[1]
        return lax.ppermute(send, AXES, [(i, i ^ flip) for i in range(ndev)])

    two_got = second_step(two_send, DN_TWO)
    upa_got = second_step(upa_send, UP_ONE)
    upb_got = second_step(upb_send, UP_TWO)
    dq, dk, dv = attend_backward(bounds, q, k, v, grads, stat, onehot, qmask)
    sums = tail(
        ndev, parts, layer_input, dq, dk, dv, query_weight, key_weight, value_weight, fg, one,
        (two_keep, two_got), (upa_keep, upa_got), (upb_keep, upb_got), wo, vec, bup,
    )
    ig, dn, up, wo, qg, kg, vg, g2g, s2g, db, g1g, s1g, ob, qb, vb, ub = write(ndev, parts, *sums)
    dn, up, wo, qg, kg, vg = (finish(u, ndev) for u in (dn, up, wo, qg, kg, vg))
    return (
        result, ig, qg, qb, kg, vg, vb, wo, ob, g1g, s1g, up, ub, dn, db, g2g, s2g,
    )


def solution(mesh):
    split = P(AXES, None)
    part = P(AXES)
    in_specs = (split,) + (P(),) * 15 + (split, P("dp", None))
    out_specs = (
        split, split, split, part, split, split, part, split, part, part, part,
        split, part, split, part, part, part,
    )
    return jax.shard_map(shards, mesh=mesh, in_specs=in_specs, out_specs=out_specs, check_vma=False)
```

```python
import functools

import jax
import jax.numpy as jnp
from jax import lax
from jax.experimental import pallas as pl
from jax.experimental.pallas import tpu as pltpu
from jax.sharding import PartitionSpec as P

HEAD_DIM = 64
PAIR = 2 * HEAD_DIM
AXES = ("dp", "seq")
NEG = -1e30
FLOOR = -3e38
BQ = 256
BK = 128
LEVELS = 5
layer_eps = 1e-12
F32 = jnp.float32
BF16 = jnp.bfloat16


def nn(a, b):
    return lax.dot_general(a, b, (((1,), (0,)), ((), ())), preferred_element_type=F32)


def nt(a, b):
    return lax.dot_general(a, b, (((1,), (1,)), ((), ())), preferred_element_type=F32)


def tn(a, b):
    return lax.dot_general(a, b, (((0,), (0,)), ((), ())), preferred_element_type=F32)


def cost(flops, nbytes, trans=0):
    return pl.CostEstimate(flops=int(flops), bytes_accessed=int(nbytes), transcendentals=int(trans))


def params(limit=56 << 20):
    return pltpu.CompilerParams(vmem_limit_bytes=limit)


def whole():
    return pl.BlockSpec(memory_space=pltpu.VMEM)


def hbm():
    return pl.BlockSpec(memory_space=pl.ANY)


def low_lanes():
    return lax.broadcasted_iota(jnp.int32, (1, PAIR), 1) < HEAD_DIM


def line(ref):
    return ref[...].reshape(1, -1)


def remote_params(number):
    return pltpu.CompilerParams(
        vmem_limit_bytes=60 << 20, collective_id=number, has_side_effects=True
    )


class Links:
    def __init__(self, ndev, parts, send_sems, recv_sems):
        self.ndev, self.parts = ndev, parts
        self.place = lax.axis_index("seq")
        self.row = lax.axis_index("dp")
        self.me = self.row * parts + self.place
        self.shift = ndev >> LEVELS
        self.block = self.me // self.shift
        self.send_sems, self.recv_sems = send_sems, recv_sems
        self.used = 0
        self.started = []
        self.has_prev = self.place > 0
        self.has_next = self.place < parts - 1

    def partner(self, flip):
        other = self.me + (1 - 2 * ((self.me // flip) % 2)) * flip
        return (other // self.parts, other % self.parts)

    def greet(self, flips, neighbours):
        barrier = pltpu.get_barrier_semaphore()

        def signal(device):
            pl.semaphore_signal(
                barrier, inc=1, device_id=device, device_id_type=pl.DeviceIdType.MESH
            )

        for flip in flips:
            signal(self.partner(flip))
        if neighbours:

            @pl.when(self.has_prev)
            def _():
                signal((self.row, self.place - 1))

            @pl.when(self.has_next)
            def _():
                signal((self.row, self.place + 1))

        count = len(flips)
        if neighbours:
            count = count + jnp.minimum(self.place, 1)
            count = count + jnp.minimum(self.parts - 1 - self.place, 1)
        pl.semaphore_wait(barrier, count)

    def make(self, src, dst, device):
        n = self.used
        self.used += 1
        return pltpu.make_async_remote_copy(
            src_ref=src, dst_ref=dst, send_sem=self.send_sems.at[n],
            recv_sem=self.recv_sems.at[n], device_id=device,
            device_id_type=pl.DeviceIdType.MESH,
        )

    def exchange(self, src, dst, flip):
        copy = self.make(src, dst, self.partner(flip))
        copy.start()
        self.started.append(copy)
        return copy

    def finish(self):
        for copy in self.started:
            copy.wait_send()

    def neighbours(self, src, at_next, at_prev):
        ahead = self.make(src, at_next, (self.row, self.place + 1))
        back = self.make(src, at_prev, (self.row, self.place - 1))

        @pl.when(self.has_next)
        def _():
            ahead.start()

        @pl.when(self.has_prev)
        def _():
            back.start()

        return ahead, back

    def from_prev(self, pair):
        @pl.when(self.has_prev)
        def _():
            pair[0].wait_recv()

    def from_next(self, pair):
        @pl.when(self.has_next)
        def _():
            pair[1].wait_recv()

    def sent(self, pair):
        @pl.when(self.has_next)
        def _():
            pair[0].wait_send()

        @pl.when(self.has_prev)
        def _():
            pair[1].wait_send()


def both(a, b):
    return (a.astype(F32) + b.astype(F32)).astype(BF16)


class Chain:
    def __init__(self, links, buf, recv, order, step):
        self.links, self.buf, self.recv, self.order, self.step = links, buf, recv, order, step
        self.base = 0

    def position(self, c):
        at = 0
        for k, b in enumerate(self.order):
            mine, its = (self.links.block // (1 << b)) % 2, (c // (1 << b)) % 2
            at = at + (mine + its - 2 * mine * its) * (1 << (LEVELS - 1 - k))
        return at

    def send(self):
        self.half = (1 << LEVELS) >> (self.step + 1)
        self.copy = self.links.exchange(
            self.buf.at[pl.ds(self.half, self.half)],
            self.recv.at[pl.ds(self.base, self.half)],
            self.links.shift << self.order[self.step],
        )

    def receive(self):
        self.copy.wait_recv()
        self.base += self.half
        self.step += 1

    def add(self):
        base, half, buf, recv = self.base, self.half, self.buf, self.recv
        self.receive()
        if half > 1:

            @pl.loop(0, half)
            def _(i):
                buf[i] = both(buf[i], recv[base + i])

            self.send()

    def last(self):
        return self.buf[0].astype(F32) + self.recv[self.base - 1].astype(F32)


DN_ONE = (0, 2, 1, 3, 4)
DN_TWO = (0, 1, 2, 3, 4)
UP_ONE = (0, 2, 3, 1, 4)
UP_TWO = (0, 1, 3, 2, 4)
OUT_ORDER = (0, 2, 1, 3, 4)
Q_ORDER = (0, 2, 1, 3, 4)
K_ORDER = (0, 1, 2, 3, 4)
V_ORDER = (0, 1, 3, 2, 4)
BLOCKS = 1 << LEVELS


def first_kernel(
    ndev, parts, x_ref, lengths, wq_hbm, bq, wk_hbm, wv_hbm, bv,
    q_hbm, k_hbm, v_hbm, onehot, qmask, bounds,
    halo, wq, wk, wv, q_ref, k_ref, v_ref, load_sems, store_sems, send_sems, recv_sems,
):
    rows, width = x_ref.shape
    count = rows * parts
    loads = [
        pltpu.make_async_copy(src, dst, load_sems.at[n])
        for n, (src, dst) in enumerate(((wq_hbm, wq), (wk_hbm, wk), (wv_hbm, wv)))
    ]
    for load in loads:
        load.start()
    links = Links(ndev, parts, send_sems, recv_sems)
    links.greet([], True)
    step = rows // 2
    pairs = [
        links.neighbours(
            x_ref.at[pl.ds(h * step, step)],
            halo.at[0, pl.ds(h * step, step)],
            halo.at[1, pl.ds(h * step, step)],
        )
        for h in range(2)
    ]

    @pl.when(jnp.logical_not(links.has_prev))
    def _():
        halo[0] = jnp.zeros((rows, width), BF16)

    @pl.when(jnp.logical_not(links.has_next))
    def _():
        halo[1] = jnp.zeros((rows, width), BF16)

    for load in loads:
        load.wait()

    stores = []

    def project(x, at):
        q_ref[at, :] = (nn(x, wq[...]) + line(bq)).astype(BF16)
        k_ref[at, :] = nn(x, wk[...]).astype(BF16)
        v_ref[at, :] = (nn(x, wv[...]) + line(bv)).astype(BF16)
        for src, dst in ((q_ref, q_hbm), (k_ref, k_hbm), (v_ref, v_hbm)):
            part = pl.ds(at.start, at.stop - at.start)
            store = pltpu.make_async_copy(src.at[part], dst.at[part], store_sems.at[len(stores)])
            store.start()
            stores.append(store)

    project(x_ref[...], slice(rows, 2 * rows))

    slots = lengths.shape[1]
    ends, total = [], jnp.int32(0)
    for n in range(slots):
        total = total + lengths[0, n]
        ends.append(total)
    start = (links.place - 1) * rows
    lane = lax.broadcasted_iota(jnp.int32, (BQ, PAIR), 1) % HEAD_DIM
    one, none, far = BF16(1.0), BF16(0.0), BF16(NEG)

    @pl.loop(0, 3 * rows // BQ)
    def _(i):
        at = start + i * BQ
        where = at + lax.broadcasted_iota(jnp.int32, (BQ, PAIR), 0)
        seg = jnp.zeros((BQ, PAIR), jnp.int32)
        for end in ends:
            seg = seg + (where >= end).astype(jnp.int32)
        outside = (where < 0) | (where >= count)
        seg = jnp.where(outside, slots, seg)
        match = (seg == lane).astype(F32)
        to = pl.ds(pl.multiple_of(i * BQ, BQ), BQ)
        onehot[to, :] = match.astype(BF16)
        qmask[to, :] = ((1.0 - match) * NEG).astype(BF16)

    for n in range(rows // BQ):
        near = links.place * rows + n * BQ
        far_row = near + BQ - 1
        lo, hi = jnp.int32(0), jnp.int32(count)
        for end in ends:
            lo = jnp.where(end <= near, jnp.maximum(lo, end), lo)
            hi = jnp.where(end > far_row, jnp.minimum(hi, end), hi)
        lo = jnp.maximum(lo - start, 0)
        hi = jnp.minimum(hi - start, 3 * rows)
        bounds[0, n] = lo // BK
        bounds[1, n] = (hi + BK - 1) // BK

    for h in range(2):
        links.from_prev(pairs[h])
        project(halo[0, h * step : (h + 1) * step, :], slice(h * step, (h + 1) * step))
        links.from_next(pairs[h])
        at = 2 * rows + h * step
        project(halo[1, h * step : (h + 1) * step, :], slice(at, at + step))
    for pair in pairs:
        links.sent(pair)
    for store in stores:
        store.wait()


def first(ndev, parts, x, lengths, wq, bq, wk, wv, bv):
    rows, width = x.shape
    ext = jax.ShapeDtypeStruct((3 * rows, width), BF16)
    seg = jax.ShapeDtypeStruct((3 * rows, PAIR), BF16)
    smem = pl.BlockSpec(memory_space=pltpu.SMEM)
    return pl.pallas_call(
        functools.partial(first_kernel, ndev, parts),
        in_specs=[whole(), smem, hbm(), whole(), hbm(), hbm(), whole()],
        out_specs=[hbm()] * 3 + [whole()] * 2 + [smem],
        out_shape=[ext] * 3 + [seg] * 2 + [jax.ShapeDtypeStruct((2, rows // BQ), jnp.int32)],
        scratch_shapes=[
            pltpu.VMEM((2, rows, width), BF16),
            pltpu.VMEM((width, width), BF16),
            pltpu.VMEM((width, width), BF16),
            pltpu.VMEM((width, width), BF16),
            pltpu.VMEM((3 * rows, width), BF16),
            pltpu.VMEM((3 * rows, width), BF16),
            pltpu.VMEM((3 * rows, width), BF16),
            pltpu.SemaphoreType.DMA((3,)),
            pltpu.SemaphoreType.DMA((15,)),
            pltpu.SemaphoreType.DMA((4,)),
            pltpu.SemaphoreType.DMA((4,)),
        ],
        compiler_params=remote_params(0),
        cost_estimate=cost(15e9, 12 << 20),
        name="first",
    )(x, lengths, wq, bq, wk, wv, bv)


def lengths_of(rows):
    most = BQ // BK + 2 * -(-(rows - 1) // BK)
    return [n for n in range(2, most) if n <= 6 or n % 2 == 0] + [most]


def key_range(bounds, i, rows):
    lo, hi = bounds[0, i], bounds[1, i]
    sizes = lengths_of(rows)
    number = jnp.int32(sizes[-1])
    for n in reversed(sizes):
        number = jnp.where(hi - lo <= n, n, number)
    return jnp.minimum(lo, 3 * rows // BK - number), number


def forward_kernel(bounds, q_ref, k_ref, v_ref, onehot, qmask, ctx_ref, lse_ref, ka, kb):
    rows = ctx_ref.shape[0]
    low = low_lanes()
    key, hot = k_ref[...], onehot[...]
    ka[...] = jnp.where(low, key, hot).T
    kb[...] = jnp.where(low, hot, key).T

    @pl.loop(0, rows // BQ)
    def _(i):
        first_block, number = key_range(bounds, i, rows)
        base = pl.multiple_of(first_block * BK, BK)
        at = pl.ds(pl.multiple_of(i * BQ, BQ), BQ)
        own = pl.ds(pl.multiple_of(rows + i * BQ, BQ), BQ)
        for num in lengths_of(rows):

            @pl.when(number == num)
            def _():
                span = pl.ds(base, num * BK)
                query = q_ref[own, :] * BF16(HEAD_DIM**-0.5)
                mask = qmask[own, :]
                parts = []
                for head, keys in enumerate((ka, kb)):
                    pick = (query, mask) if head == 0 else (mask, query)
                    scores = nn(jnp.where(low, *pick), keys[:, span])
                    top = jnp.max(scores, axis=1, keepdims=True)
                    weights = jnp.exp(scores - top)
                    total = jnp.sum(weights, axis=1, keepdims=True)
                    acc = nn(weights.astype(BF16), v_ref[span, :])
                    parts.append((acc / total, top + jnp.log(total)))
                ctx_ref[at, :] = jnp.where(low, parts[0][0], parts[1][0])
                flip = jnp.where(low, parts[0][1], parts[1][1]).T
                lse_ref[0, 0:1, at] = flip[0:1]
                lse_ref[0, 1:2, at] = flip[HEAD_DIM : HEAD_DIM + 1]


def attend_forward(bounds, q, k, v, onehot, qmask):
    rows, width = q.shape[0] // 3, q.shape[1]
    pairs = width // PAIR
    ext = pl.BlockSpec((3 * rows, PAIR), lambda p, *_: (0, p))
    seg = pl.BlockSpec((3 * rows, PAIR), lambda p, *_: (0, 0))
    grid = pltpu.PrefetchScalarGridSpec(
        num_scalar_prefetch=1,
        grid=(pairs,),
        in_specs=[ext, ext, ext, seg, seg],
        out_specs=[
            pl.BlockSpec((rows, PAIR), lambda p, *_: (0, p)),
            pl.BlockSpec((1, 2, rows), lambda p, *_: (p, 0, 0)),
        ],
        scratch_shapes=[
            pltpu.VMEM((PAIR, 3 * rows), BF16),
            pltpu.VMEM((PAIR, 3 * rows), BF16),
        ],
    )
    return pl.pallas_call(
        forward_kernel,
        grid_spec=grid,
        out_shape=[
            jax.ShapeDtypeStruct((rows, width), F32),
            jax.ShapeDtypeStruct((pairs, 2, rows), F32),
        ],
        compiler_params=params(),
        cost_estimate=cost(20e9, 24 * rows * width),
        name="attend_forward",
    )(bounds, q, k, v, onehot, qmask)


def backward_kernel(
    bounds, q_ref, k_ref, v_ref, g_ref, stat_ref, onehot, qmask,
    dq_ref, dk_ref, dv_ref, ka, kb, vt, qa, qb, gt,
):
    rows = dq_ref.shape[0]
    low = low_lanes()
    zero = jnp.zeros((1, PAIR), BF16)
    scale = BF16(HEAD_DIM**-0.5)
    key, hot = k_ref[...], onehot[...]
    ka[...] = jnp.where(low, key, hot).T
    kb[...] = jnp.where(low, hot, key).T
    query, mask = q_ref[...] * scale, qmask[...]
    qa[...] = jnp.where(low, query, mask).T
    qb[...] = jnp.where(low, mask, query).T
    vt[...] = v_ref[...].T
    gt[...] = g_ref[...].T

    @pl.loop(0, rows // BQ)
    def _(i):
        first_block, number = key_range(bounds, i, rows)
        base = pl.multiple_of(first_block * BK, BK)
        at = pl.ds(pl.multiple_of(i * BQ, BQ), BQ)
        own = pl.ds(pl.multiple_of(rows + i * BQ, BQ), BQ)
        for num in lengths_of(rows):

            @pl.when(number == num)
            def _():
                span = pl.ds(base, num * BK)

                def pick(head, value, other):
                    return jnp.where(low, value, other) if head == 0 else jnp.where(
                        low, other, value
                    )

                columns = stat_ref[0, :, own]
                columns = jnp.concatenate([columns, columns], axis=0).T
                out = []
                for head, keys in enumerate((ka, kb)):
                    queries = pick(head, q_ref[own, :] * scale, qmask[own, :])
                    grads = pick(head, g_ref[own, :], zero)
                    scores = nn(queries, keys[:, span])
                    prob_grad = nn(grads, vt[:, span])
                    probs = jnp.exp(scores - columns[:, head : head + 1])
                    delta = columns[:, 2 + head : 3 + head]
                    score_grad = (probs * (prob_grad - delta)).astype(BF16)
                    out.append(nn(score_grad, k_ref[span, :]))
                dq = jnp.where(low, out[0], out[1]) * F32(HEAD_DIM**-0.5)
                dq_ref[at, :] = dq.astype(BF16)
                out = []
                for head, queries in enumerate((qa, qb)):
                    keys = pick(head, k_ref[own, :], onehot[own, :])
                    vals = pick(head, v_ref[own, :], zero)
                    scores = nn(keys, queries[:, span])
                    prob_grad = nn(vals, gt[:, span])
                    probs = jnp.exp(scores - stat_ref[0, head : head + 1, span])
                    delta = stat_ref[0, 2 + head : 3 + head, span]
                    score_grad = (probs * (prob_grad - delta)).astype(BF16)
                    out.append((
                        nn(score_grad, q_ref[span, :] * scale),
                        nn(probs.astype(BF16), g_ref[span, :]),
                    ))
                dk_ref[at, :] = jnp.where(low, out[0][0], out[1][0]).astype(BF16)
                dv_ref[at, :] = jnp.where(low, out[0][1], out[1][1]).astype(BF16)


def attend_backward(bounds, q, k, v, g, stat, onehot, qmask):
    rows, width = q.shape[0] // 3, q.shape[1]
    pairs = width // PAIR
    ext = pl.BlockSpec((3 * rows, PAIR), lambda p, *_: (0, p))
    own = pl.BlockSpec((rows, PAIR), lambda p, *_: (0, p))
    seg = pl.BlockSpec((3 * rows, PAIR), lambda p, *_: (0, 0))
    grid = pltpu.PrefetchScalarGridSpec(
        num_scalar_prefetch=1,
        grid=(pairs,),
        in_specs=[ext] * 4 + [pl.BlockSpec((1, 4, 3 * rows), lambda p, *_: (p, 0, 0)), seg, seg],
        out_specs=[own] * 3,
        scratch_shapes=[pltpu.VMEM((PAIR, 3 * rows), BF16)] * 6,
    )
    return pl.pallas_call(
        backward_kernel,
        grid_spec=grid,
        out_shape=[jax.ShapeDtypeStruct((rows, width), BF16)] * 3,
        compiler_params=params(),
        cost_estimate=cost(40e9, 40 * rows * width),
        name="attend_backward",
    )(bounds, q, k, v, g, stat, onehot, qmask)


def norm_forward(h):
    mean = jnp.mean(h, axis=-1, keepdims=True)
    centred = h - mean
    variance = jnp.mean(centred * centred, axis=-1, keepdims=True)
    inverse = lax.rsqrt(variance + layer_eps)
    return centred * inverse, inverse


def norm_backward(grad, gain, hat, inverse):
    g = grad * gain
    return inverse * (
        g - jnp.mean(g, axis=-1, keepdims=True) - hat * jnp.mean(g * hat, axis=-1, keepdims=True)
    )


def colsum(v):
    return jnp.sum(v, axis=0, keepdims=True)


def middle_kernel(
    ndev, parts,
    x_ref, ctx_ref, ct_ref, wo, bo, g1, s1, wup_hbm, bup, wdn_hbm, bdn, g2, s2, lse_ref,
    result_hbm, fg_hbm, g_hbm, stat_ref, vec_ref, bup_ref,
    dn_one_hbm, two_keep_hbm, two_send_hbm, upa_keep_hbm, upa_send_hbm, upb_keep_hbm,
    upb_send_hbm, wo_hbm,
    wup, wdn, hid, nl, bg, cl, ag, slope, normed, inv, acc, grad_s,
    result_ref, fg_ref, g_ref,
    one_s, one_r, two_s, two_r, upa_s, upa_r, upb_s, upb_r, wo_s, wo_r,
    load_sems, store_sems, send_sems, recv_sems,
):
    stores = []

    def store(src, dst):
        copy = pltpu.make_async_copy(src, dst, store_sems.at[len(stores)])
        copy.start()
        stores.append(copy)

    rows, width = x_ref.shape
    ff = wup.shape[1]
    rc, fc = 256, 512
    chunks, tiles = rows // rc, ff // fc
    tall, short = ff // BLOCKS, width // BLOCKS
    up_copy = pltpu.make_async_copy(wup_hbm, wup, load_sems.at[0])
    dn_copy = pltpu.make_async_copy(wdn_hbm, wdn, load_sems.at[1])
    up_copy.start()
    dn_copy.start()
    links = Links(ndev, parts, send_sems, recv_sems)
    links.greet([links.shift << DN_ONE[0], links.shift << DN_ONE[1]], True)
    one = Chain(links, one_s, one_r, DN_ONE, 0)
    two = Chain(links, two_s, two_r, DN_TWO, 0)
    upa = Chain(links, upa_s, upa_r, UP_ONE, 0)
    upb = Chain(links, upb_s, upb_r, UP_TWO, 0)
    out = Chain(links, wo_s, wo_r, OUT_ORDER, 0)

    @pl.loop(0, chunks)
    def _(r):
        at = pl.ds(pl.multiple_of(r * rc, rc), rc)
        c_low = ctx_ref[at, :].astype(BF16)
        cl[at, :] = c_low
        h = x_ref[at, :].astype(F32) + (nn(c_low, wo[...]) + line(bo))
        xhat, inverse = norm_forward(h)
        res = xhat * line(g1) + line(s1)
        fg_ref[at, :] = xhat
        inv[at, :] = inverse
        normed[at, :] = res
        nl[at, :] = res.astype(BF16)

    up_copy.wait()
    dn_copy.wait()
    acc[...] = jnp.zeros_like(acc)

    @pl.loop(0, tiles)
    def _(j):
        cols = pl.ds(pl.multiple_of(j * fc, fc), fc)
        bias = bup[cols].reshape(1, fc)
        for r in range(chunks):
            at = slice(r * rc, (r + 1) * rc)
            up = nn(nl[at, :], wup[:, cols]) + bias
            cdf = 0.5 * (1.0 + lax.erf(up * F32(0.5**0.5)))
            density = jnp.exp(-0.5 * up * up) * F32(0.3989422804014327)
            slope[at, cols] = cdf + up * density
            act = (up * cdf).astype(BF16)
            hid[at, cols] = act
            acc[at, :] = acc[at, :] + nn(act, wdn[cols, :])

    vec_ref[...] = jnp.zeros_like(vec_ref)

    @pl.loop(0, chunks)
    def _(r):
        at = pl.ds(pl.multiple_of(r * rc, rc), rc)
        xhat, inverse = norm_forward(normed[at, :] + (acc[at, :] + line(bdn)))
        result_ref[at, :] = (xhat * line(g2) + line(s2)).astype(BF16)
        ct = ct_ref[at, :].astype(F32)
        second = norm_backward(ct, line(g2), xhat, inverse)
        low = second.astype(BF16)
        bg[at, :] = low
        acc[at, :] = second
        vec_ref[0:1, :] = vec_ref[0:1, :] + colsum(ct * xhat)
        vec_ref[1:2, :] = vec_ref[1:2, :] + colsum(ct)
        vec_ref[2:3, :] = vec_ref[2:3, :] + colsum(low.astype(F32))

    store(result_ref, result_hbm)

    some = width // tall

    @pl.loop(0, ff // width)
    def _(j):
        grad_s[...] = tn(hid[:, pl.ds(pl.multiple_of(j * width, width), width)], bg[...])

        @pl.loop(0, some)
        def _(c):
            base = pl.multiple_of(c * tall, tall // 2)
            one_s[one.position(j * some + c)] = grad_s[pl.ds(base, tall // 2), :].astype(BF16)
            base = pl.multiple_of(c * tall + tall // 2, tall // 2)
            two_s[two.position(j * some + c)] = grad_s[pl.ds(base, tall // 2), :].astype(BF16)

    one.send()
    two.send()

    def back_tiles(lo, hi):
        @pl.loop(lo, hi)
        def _(j):
            cols = pl.ds(pl.multiple_of(j * fc, fc), fc)
            sums = jnp.zeros((1, fc), F32)
            for r in range(chunks):
                at = slice(r * rc, (r + 1) * rc)
                grad = (nt(bg[at, :], wdn[cols, :]) * slope[at, cols]).astype(BF16)
                hid[at, cols] = grad
                sums = sums + colsum(grad.astype(F32))
                acc[at, :] = acc[at, :] + nt(grad, wup[:, cols])
            bup_ref[:, cols] = sums

    back_tiles(0, tiles - 2)
    one.add()
    back_tiles(tiles - 2, tiles)

    zero_prev = pltpu.make_async_copy(
        result_ref, g_hbm.at[pl.ds(0, rows)], store_sems.at[store_sems.shape[0] - 2]
    )
    zero_next = pltpu.make_async_copy(
        result_ref, g_hbm.at[pl.ds(2 * rows, rows)], store_sems.at[store_sems.shape[0] - 1]
    )
    stores.pop().wait()
    result_ref[...] = jnp.zeros_like(result_ref)

    @pl.when(jnp.logical_not(links.has_prev))
    def _():
        zero_prev.start()
        stat_ref[:, :, 0:rows] = jnp.zeros((width // PAIR, 4, rows), F32)

    @pl.when(jnp.logical_not(links.has_next))
    def _():
        zero_next.start()
        stat_ref[:, :, 2 * rows : 3 * rows] = jnp.zeros((width // PAIR, 4, rows), F32)

    pairs = []
    for r in range(chunks):
        at = slice(r * rc, (r + 1) * rc)
        mid = slice(rows + r * rc, rows + (r + 1) * rc)
        total = acc[at, :]
        xhat = fg_ref[at, :]
        first_grad = norm_backward(total, line(g1), xhat, inv[at, :])
        fg_ref[at, :] = first_grad
        low = first_grad.astype(BF16)
        ag[at, :] = low
        vec_ref[3:4, :] = vec_ref[3:4, :] + colsum(total * xhat)
        vec_ref[4:5, :] = vec_ref[4:5, :] + colsum(total)
        vec_ref[5:6, :] = vec_ref[5:6, :] + colsum(low.astype(F32))
        cg = nt(low, wo[...]).astype(BF16)
        g_ref[at, :] = cg
        pairs.append(links.neighbours(
            g_ref.at[pl.ds(r * rc, rc)],
            g_hbm.at[pl.ds(r * rc, rc)],
            g_hbm.at[pl.ds(2 * rows + r * rc, rc)],
        ))
        prod = cg.astype(F32) * ctx_ref[at, :]
        for p in range(width // PAIR):
            flip = prod[:, p * PAIR : (p + 1) * PAIR].T
            stat_ref[p, 2:3, mid] = colsum(flip[:HEAD_DIM])
            stat_ref[p, 3:4, mid] = colsum(flip[HEAD_DIM:])
    store(g_ref, g_hbm.at[pl.ds(rows, rows)])
    store(fg_ref, fg_hbm)
    for p in range(width // PAIR):
        stat_ref[p, 0:2, rows : 2 * rows] = lse_ref[p]
    pairs.append(links.neighbours(
        stat_ref.at[:, :, pl.ds(rows, rows)],
        stat_ref.at[:, :, pl.ds(0, rows)],
        stat_ref.at[:, :, pl.ds(2 * rows, rows)],
    ))

    for n in range(ff // width):
        chain = (upa, upb)[n // 2]
        grad_s[...] = tn(nl[...], hid[:, n * width : (n + 1) * width])
        to = slice((n % 2) * width, (n % 2 + 1) * width)

        @pl.loop(0, BLOCKS)
        def _(c):
            at = pl.ds(pl.multiple_of(c * short, short), short)
            chain.buf[chain.position(c), :, to] = grad_s[at, :].astype(BF16)

        if n % 2 == 1:
            chain.send()

    grad_s[...] = tn(cl[...], ag[...])

    @pl.loop(0, BLOCKS)
    def _(c):
        at = pl.ds(pl.multiple_of(c * short, short), short)
        wo_s[out.position(c)] = grad_s[at, :].astype(BF16)

    out.send()

    def settle(chain, keep, send):
        chain.receive()
        half, quarter = BLOCKS // 2, BLOCKS // 4

        @pl.loop(0, half)
        def _(i):
            chain.recv[i] = both(chain.buf[i], chain.recv[i])

        store(chain.recv.at[pl.ds(0, quarter)], keep)
        store(chain.recv.at[pl.ds(quarter, quarter)], send)

    settle(two, two_keep_hbm, two_send_hbm)
    settle(upa, upa_keep_hbm, upa_send_hbm)
    settle(upb, upb_keep_hbm, upb_send_hbm)
    out.receive()

    @pl.loop(0, BLOCKS // 2)
    def _(i):
        wo_r[i] = both(wo_s[i], wo_r[i])

    store(wo_r, wo_hbm)
    one.receive()

    @pl.loop(0, BLOCKS // 4)
    def _(i):
        one_s[i] = both(one_s[i], one_r[BLOCKS // 2 + i])

    store(one_s.at[pl.ds(0, BLOCKS // 4)], dn_one_hbm)
    for copy in stores:
        copy.wait()

    @pl.when(jnp.logical_not(links.has_prev))
    def _():
        zero_prev.wait()

    @pl.when(jnp.logical_not(links.has_next))
    def _():
        zero_next.wait()

    for pair in pairs:
        links.from_prev(pair)
        links.from_next(pair)
        links.sent(pair)
    links.finish()


def middle(ndev, parts, x, ctx, ct, wo, bo, g1, s1, wup, bup, wdn, bdn, g2, s2, lse):
    rows, width = x.shape
    ff = wup.shape[1]
    pairs = width // PAIR
    tall, short = ff // BLOCKS, width // BLOCKS
    left = BLOCKS // 4

    def out(*shape, dtype=BF16):
        return jax.ShapeDtypeStruct(shape, dtype)

    shapes = [
        out(rows, width),
        out(rows, width, dtype=F32),
        out(3 * rows, width),
        out(pairs, 4, 3 * rows, dtype=F32),
        out(8, width, dtype=F32),
        out(1, ff, dtype=F32),
        out(left, tall // 2, width),
        out(left, tall // 2, width),
        out(left, tall // 2, width),
        out(left, short, ff // 2),
        out(left, short, ff // 2),
        out(left, short, ff // 2),
        out(left, short, ff // 2),
        out(BLOCKS // 2, short, width),
    ]

    def chain(*shape):
        return [pltpu.VMEM((BLOCKS,) + shape, BF16), pltpu.VMEM((BLOCKS // 2,) + shape, BF16)]

    dn_one = chain(tall // 2, width)
    dn_one[1] = pltpu.VMEM((3 * BLOCKS // 4, tall // 2, width), BF16)
    copies = 6 + 6
    return pl.pallas_call(
        functools.partial(middle_kernel, ndev, parts),
        in_specs=[whole()] * 7 + [hbm(), whole(), hbm()] + [whole()] * 4,
        out_specs=[hbm()] * 3 + [whole()] * 3 + [hbm()] * 8,
        out_shape=shapes,
        scratch_shapes=[
            pltpu.VMEM((width, ff), BF16),
            pltpu.VMEM((ff, width), BF16),
            pltpu.VMEM((rows, ff), BF16),
            pltpu.VMEM((rows, width), BF16),
            pltpu.VMEM((rows, width), BF16),
            pltpu.VMEM((rows, width), BF16),
            pltpu.VMEM((rows, width), BF16),
            pltpu.VMEM((rows, ff), F32),
            pltpu.VMEM((rows, width), F32),
            pltpu.VMEM((rows, 1), F32),
            pltpu.VMEM((rows, width), F32),
            pltpu.VMEM((width, width), F32),
            pltpu.VMEM((rows, width), BF16),
            pltpu.VMEM((rows, width), F32),
            pltpu.VMEM((rows, width), BF16),
        ]
        + dn_one + chain(tall // 2, width) + chain(short, ff // 2) * 2 + chain(short, width)
        + [
            pltpu.SemaphoreType.DMA((2,)),
            pltpu.SemaphoreType.DMA((13,)),
            pltpu.SemaphoreType.DMA((copies,)),
            pltpu.SemaphoreType.DMA((copies,)),
        ],
        compiler_params=remote_params(1),
        cost_estimate=cost(50e9, 30 << 20),
        name="middle",
    )(x, ctx, ct, wo, bo, g1, s1, wup, bup, wdn, bdn, g2, s2, lse)


def tail_kernel(
    ndev, parts,
    x, dq, dk, dv, wq, wk, wv, fg, dn_one, dn_keep, dn_got, upa_keep, upa_got, upb_keep, upb_got,
    wo_in, vec, bup,
    ig_ref, dn1_out, dn2_out, up1_out, up2_out, wo_out, q_out, k_out, v_out, vec_out, bup_out,
    one_s, one_r, two_s, two_r, upa_s, upa_r, upb_s, upb_r, wo_s, wo_r, q_s, q_r, k_s, k_r,
    v_s, v_r, grad_s, vec_s, vec_r, bup_s, bup_r,
    load_sems, send_sems, recv_sems,
):
    width = x.shape[1]
    short = width // BLOCKS
    loads = [
        pltpu.make_async_copy(dn_one, one_s, load_sems.at[0]),
        pltpu.make_async_copy(wo_in, wo_s, load_sems.at[1]),
    ]
    for load in loads:
        load.start()
    links = Links(ndev, parts, send_sems, recv_sems)
    flips = [1 << n for n in range(ndev.bit_length() - 1)]
    links.greet(flips, False)
    one = Chain(links, one_s, one_r, DN_ONE, 2)
    two = Chain(links, two_s, two_r, DN_TWO, 2)
    upa = Chain(links, upa_s, upa_r, UP_ONE, 2)
    upb = Chain(links, upb_s, upb_r, UP_TWO, 2)
    out = Chain(links, wo_s, wo_r, OUT_ORDER, 1)
    qc = Chain(links, q_s, q_r, Q_ORDER, 0)
    kc = Chain(links, k_s, k_r, K_ORDER, 0)
    vc = Chain(links, v_s, v_r, V_ORDER, 0)

    def begin(chain, keep, got):
        @pl.loop(0, BLOCKS // 4)
        def _(i):
            chain.buf[i] = both(keep[i], got[i])

        chain.send()

    begin(two, dn_keep, dn_got)
    loads[0].wait()
    one.send()
    begin(upa, upa_keep, upa_got)
    begin(upb, upb_keep, upb_got)
    loads[1].wait()
    out.send()

    def weight(chain, grad):
        grad_s[...] = tn(x[...], grad[...])

        @pl.loop(0, BLOCKS)
        def _(c):
            at = pl.ds(pl.multiple_of(c * short, short), short)
            chain.buf[chain.position(c)] = grad_s[at, :].astype(BF16)

        chain.send()

    weight(qc, dq)
    weight(kc, dk)
    weight(vc, dv)
    vec_s[0] = vec[...]
    vec_s[0, 6:7, :] = colsum(dq[...].astype(F32))
    vec_s[0, 7:8, :] = colsum(dv[...].astype(F32))
    bup_s[0] = bup[...]

    def vectors(n):
        if n >= len(flips):
            return None
        return [
            links.exchange(vec_s.at[n], vec_r.at[n], flips[n]),
            links.exchange(bup_s.at[n], bup_r.at[n], flips[n]),
        ]

    def add_vectors(n, copies):
        for c in copies:
            c.wait_recv()
        vec_s[n + 1] = vec_s[n] + vec_r[n]
        bup_s[n + 1] = bup_s[n] + bup_r[n]
        return vectors(n + 1)

    pending = vectors(0)
    qc.add()
    kc.add()
    vc.add()
    ig_ref[...] = (
        nt(dq[...], wq[...]) + nt(dk[...], wk[...]) + nt(dv[...], wv[...]) + fg[...]
    ).astype(BF16)
    pending = add_vectors(0, pending)
    two.add()
    one.add()
    out.add()
    upa.add()
    upb.add()
    pending = add_vectors(1, pending)
    qc.add()
    kc.add()
    vc.add()
    two.add()
    one.add()
    out.add()
    upa.add()
    upb.add()
    pending = add_vectors(2, pending)
    qc.add()
    kc.add()
    vc.add()
    two.add()
    one.add()
    upa.add()
    upb.add()
    out.add()
    pending = add_vectors(3, pending)
    dn1_out[...] = one.last()
    dn2_out[...] = two.last()
    up1_out[...] = upa.last()
    up2_out[...] = upb.last()
    qc.add()
    kc.add()
    vc.add()
    out.add()
    wo_out[...] = out.last()
    for n in range(4, len(flips)):
        pending = add_vectors(n, pending)
    vec_out[...] = vec_s[len(flips)]
    bup_out[...] = bup_s[len(flips)]
    qc.add()
    kc.add()
    vc.add()
    q_out[...] = qc.last()
    k_out[...] = kc.last()
    v_out[...] = vc.last()
    links.finish()


def tail(ndev, parts, x, dq, dk, dv, wq, wk, wv, fg, one, two, upa, upb, wo, vec, bup):
    rows, width = x.shape
    short = width // BLOCKS
    tall, ff = one.shape[1] * 2, upa[0].shape[2] * 2
    steps = ndev.bit_length() - 1

    def out(*shape):
        return jax.ShapeDtypeStruct(shape, F32)

    def chain(step, *shape):
        return [pltpu.VMEM((BLOCKS >> step,) + shape, BF16)] * 2

    copies = 4 * 3 + 4 + 3 * 5 + 2 * steps
    return pl.pallas_call(
        functools.partial(tail_kernel, ndev, parts),
        in_specs=[whole()] * 8 + [hbm()] + [whole()] * 6 + [hbm(), whole(), whole()],
        out_specs=[whole()] * 11,
        out_shape=[
            jax.ShapeDtypeStruct((rows, width), BF16),
            out(tall // 2, width), out(tall // 2, width), out(short, ff // 2), out(short, ff // 2),
            out(short, width), out(short, width), out(short, width), out(short, width),
            out(8, width), out(1, ff),
        ],
        scratch_shapes=chain(2, tall // 2, width) * 2
        + chain(2, short, ff // 2) * 2
        + chain(1, short, width)
        + chain(0, short, width) * 3
        + [
            pltpu.VMEM((width, width), F32),
            pltpu.VMEM((steps + 1, 8, width), F32),
            pltpu.VMEM((steps, 8, width), F32),
            pltpu.VMEM((steps + 1, 1, ff), F32),
            pltpu.VMEM((steps, 1, ff), F32),
            pltpu.SemaphoreType.DMA((2,)),
            pltpu.SemaphoreType.DMA((copies,)),
            pltpu.SemaphoreType.DMA((copies,)),
        ],
        compiler_params=remote_params(2),
        cost_estimate=cost(60e9, 16 << 20),
        name="tail",
    )(x, dq, dk, dv, wq, wk, wv, fg, one, *two, *upa, *upb, wo, vec, bup)


def write_kernel(
    ndev, parts, ig, dn1, dn2, up1, up2, wo, q, k, v, vec, bup,
    ig_out, dn_out, up_out, wo_out, q_out, k_out, v_out,
    g2_out, s2_out, db_out, g1_out, s1_out, ob_out, qb_out, vb_out, ub_out,
):
    ig_out[...] = ig[...]
    me = lax.axis_index("dp") * parts + lax.axis_index("seq")
    half = dn1.shape[0]
    dn_out[0:half, :] = dn1[...]
    dn_out[half : 2 * half, :] = dn2[...]
    half = up1.shape[1]
    up_out[:, 0:half] = up1[...]
    up_out[:, half : 2 * half] = up2[...]
    wo_out[...] = wo[...]
    q_out[...] = q[...]
    k_out[...] = k[...]
    v_out[...] = v[...]
    width, ff = vec.shape[1], bup.shape[1]
    mine = width // ndev
    mid = pltpu.roll(vec[...], lax.rem(width - me * mine, width), 1)[:, :128]
    for n, ref in enumerate((g2_out, s2_out, db_out, g1_out, s1_out, ob_out, qb_out, vb_out)):
        ref[...] = mid[n, :mine]
    wide = jnp.broadcast_to(bup[...], (8, ff))
    wide = pltpu.roll(wide, lax.rem(ff - me * (ff // ndev), ff), 1)[:, :128]
    ub_out[...] = wide[0, : ff // ndev]


def write(ndev, parts, ig, dn1, dn2, up1, up2, wo, q, k, v, vec, bup):
    width, ff = vec.shape[1], bup.shape[1]

    def out(*shape):
        return jax.ShapeDtypeStruct(shape, F32)

    shapes = [
        jax.ShapeDtypeStruct(ig.shape, BF16),
        out(2 * dn1.shape[0], width), out(up1.shape[0], ff), out(*wo.shape), out(*q.shape),
        out(*k.shape), out(*v.shape),
    ] + [out(width // ndev)] * 8 + [out(ff // ndev)]
    return pl.pallas_call(
        functools.partial(write_kernel, ndev, parts),
        in_specs=[whole()] * 11,
        out_specs=[whole()] * 16,
        out_shape=shapes,
        compiler_params=params(),
        name="write",
    )(ig, dn1, dn2, up1, up2, wo, q, k, v, vec, bup)


def finish(block, ndev):
    rest = ndev >> LEVELS
    if rest == 1:
        return block
    step = 1
    me = lax.axis_index("dp") * lax.axis_size("seq") + lax.axis_index("seq")
    arr = block.reshape(rest, block.shape[0] // rest, block.shape[1])
    flip = rest
    while flip > 1:
        flip //= 2
        bit = (me // flip) % 2
        half = arr.shape[0] // 2
        keep = lax.dynamic_slice_in_dim(arr, bit * half, half, 0)
        send = lax.dynamic_slice_in_dim(arr, (1 - bit) * half, half, 0)
        arr = keep + lax.ppermute(send, AXES, [(i, i ^ flip) for i in range(ndev)])
    return arr[0]


def shards(
    layer_input,
    query_weight,
    query_bias,
    key_weight,
    value_weight,
    value_bias,
    output_weight,
    output_bias,
    first_gain,
    first_shift,
    up_weight,
    up_bias,
    down_weight,
    down_bias,
    second_gain,
    second_shift,
    out_cotangent,
    passage_lengths,
):
    parts = lax.axis_size("seq")
    ndev = parts * lax.axis_size("dp")
    shift = ndev >> LEVELS
    q, k, v, onehot, qmask, bounds = first(
        ndev, parts, layer_input, passage_lengths, query_weight, query_bias, key_weight,
        value_weight, value_bias,
    )
    ctx, lse = attend_forward(bounds, q, k, v, onehot, qmask)
    (
        result, fg, grads, stat, vec, bup, one, two_keep, two_send, upa_keep, upa_send, upb_keep,
        upb_send, wo,
    ) = middle(
        ndev, parts, layer_input, ctx, out_cotangent, output_weight, output_bias, first_gain,
        first_shift, up_weight, up_bias, down_weight, down_bias, second_gain, second_shift, lse,
    )

    def second_step(send, order):
        flip = shift << order[1]
        return lax.ppermute(send, AXES, [(i, i ^ flip) for i in range(ndev)])

    two_got = second_step(two_send, DN_TWO)
    upa_got = second_step(upa_send, UP_ONE)
    upb_got = second_step(upb_send, UP_TWO)
    dq, dk, dv = attend_backward(bounds, q, k, v, grads, stat, onehot, qmask)
    sums = tail(
        ndev, parts, layer_input, dq, dk, dv, query_weight, key_weight, value_weight, fg, one,
        (two_keep, two_got), (upa_keep, upa_got), (upb_keep, upb_got), wo, vec, bup,
    )
    ig, dn, up, wo, qg, kg, vg, g2g, s2g, db, g1g, s1g, ob, qb, vb, ub = write(ndev, parts, *sums)
    dn, up, wo, qg, kg, vg = (finish(u, ndev) for u in (dn, up, wo, qg, kg, vg))
    return (
        result, ig, qg, qb, kg, vg, vb, wo, ob, g1g, s1g, up, ub, dn, db, g2g, s2g,
    )


def solution(mesh):
    split = P(AXES, None)
    part = P(AXES)
    in_specs = (split,) + (P(),) * 15 + (split, P("dp", None))
    out_specs = (
        split, split, split, part, split, split, part, split, part, part, part,
        split, part, split, part, part, part,
    )
    return jax.shard_map(shards, mesh=mesh, in_specs=in_specs, out_specs=out_specs, check_vma=False)
```

```python
import functools

import jax
import jax.numpy as jnp
from jax import lax
from jax.experimental import pallas as pl
from jax.experimental.pallas import tpu as pltpu
from jax.sharding import PartitionSpec as P

HEAD_DIM = 64
PAIR = 2 * HEAD_DIM
AXES = ("dp", "seq")
NEG = -1e30
FLOOR = -3e38
BQ = 256
BK = 128
LEVELS = 5
layer_eps = 1e-12
F32 = jnp.float32
BF16 = jnp.bfloat16


def nn(a, b):
    return lax.dot_general(a, b, (((1,), (0,)), ((), ())), preferred_element_type=F32)


def nt(a, b):
    return lax.dot_general(a, b, (((1,), (1,)), ((), ())), preferred_element_type=F32)


def tn(a, b):
    return lax.dot_general(a, b, (((0,), (0,)), ((), ())), preferred_element_type=F32)


def cost(flops, nbytes, trans=0):
    return pl.CostEstimate(flops=int(flops), bytes_accessed=int(nbytes), transcendentals=int(trans))


def params(limit=56 << 20):
    return pltpu.CompilerParams(vmem_limit_bytes=limit)


def whole():
    return pl.BlockSpec(memory_space=pltpu.VMEM)


def hbm():
    return pl.BlockSpec(memory_space=pl.ANY)


def low_lanes():
    return lax.broadcasted_iota(jnp.int32, (1, PAIR), 1) < HEAD_DIM


def line(ref):
    return ref[...].reshape(1, -1)


def remote_params(number):
    return pltpu.CompilerParams(
        vmem_limit_bytes=60 << 20, collective_id=number, has_side_effects=True
    )


class Links:
    def __init__(self, ndev, parts, send_sems, recv_sems):
        self.ndev, self.parts = ndev, parts
        self.place = lax.axis_index("seq")
        self.row = lax.axis_index("dp")
        self.me = self.row * parts + self.place
        self.shift = ndev >> LEVELS
        self.block = self.me // self.shift
        self.send_sems, self.recv_sems = send_sems, recv_sems
        self.used = 0
        self.started = []
        self.has_prev = self.place > 0
        self.has_next = self.place < parts - 1

    def partner(self, *flips):
        other = self.me
        for flip in flips:
            other = other + (1 - 2 * ((self.me // flip) % 2)) * flip
        return (other // self.parts, other % self.parts)

    def greet(self, flips, neighbours):
        barrier = pltpu.get_barrier_semaphore()

        def signal(device):
            pl.semaphore_signal(
                barrier, inc=1, device_id=device, device_id_type=pl.DeviceIdType.MESH
            )

        for flip in flips:
            signal(self.partner(*(flip if isinstance(flip, tuple) else (flip,))))
        if neighbours:

            @pl.when(self.has_prev)
            def _():
                signal((self.row, self.place - 1))

            @pl.when(self.has_next)
            def _():
                signal((self.row, self.place + 1))

        count = len(flips)
        if neighbours:
            count = count + jnp.minimum(self.place, 1)
            count = count + jnp.minimum(self.parts - 1 - self.place, 1)
        pl.semaphore_wait(barrier, count)

    def make(self, src, dst, device):
        n = self.used
        self.used += 1
        return pltpu.make_async_remote_copy(
            src_ref=src, dst_ref=dst, send_sem=self.send_sems.at[n],
            recv_sem=self.recv_sems.at[n], device_id=device,
            device_id_type=pl.DeviceIdType.MESH,
        )

    def exchange(self, src, dst, *flips):
        copy = self.make(src, dst, self.partner(*flips))
        copy.start()
        self.started.append(copy)
        return copy

    def finish(self):
        for copy in self.started:
            copy.wait_send()

    def neighbours(self, src, at_next, at_prev):
        ahead = self.make(src, at_next, (self.row, self.place + 1))
        back = self.make(src, at_prev, (self.row, self.place - 1))

        @pl.when(self.has_next)
        def _():
            ahead.start()

        @pl.when(self.has_prev)
        def _():
            back.start()

        return ahead, back

    def from_prev(self, pair):
        @pl.when(self.has_prev)
        def _():
            pair[0].wait_recv()

    def from_next(self, pair):
        @pl.when(self.has_next)
        def _():
            pair[1].wait_recv()

    def sent(self, pair):
        @pl.when(self.has_next)
        def _():
            pair[0].wait_send()

        @pl.when(self.has_prev)
        def _():
            pair[1].wait_send()


def both(a, b):
    return (a.astype(F32) + b.astype(F32)).astype(BF16)


class Chain:
    def __init__(self, links, buf, recv, order, step):
        self.links, self.buf, self.recv, self.order, self.step = links, buf, recv, order, step
        self.base = 0

    def position(self, c):
        at = 0
        for k, b in enumerate(self.order):
            mine, its = (self.links.block // (1 << b)) % 2, (c // (1 << b)) % 2
            at = at + (mine + its - 2 * mine * its) * (1 << (LEVELS - 1 - k))
        return at

    def send(self):
        self.half = (1 << LEVELS) >> (self.step + 1)
        self.copy = self.links.exchange(
            self.buf.at[pl.ds(self.half, self.half)],
            self.recv.at[pl.ds(self.base, self.half)],
            self.links.shift << self.order[self.step],
        )

    def receive(self):
        self.copy.wait_recv()
        self.base += self.half
        self.step += 1

    def add(self):
        base, half, buf, recv = self.base, self.half, self.buf, self.recv
        self.receive()
        if half > 1:

            @pl.loop(0, half)
            def _(i):
                buf[i] = both(buf[i], recv[base + i])

            self.send()

    def last(self):
        return self.buf[0].astype(F32) + self.recv[self.base - 1].astype(F32)


class Flat:
    def __init__(self, links, buf, recvs, bits, order, step, cols=None):
        self.links, self.buf, self.recvs = links, buf, list(recvs)
        self.bits, self.order, self.step = bits, order, step
        self.at = [slice(None)] * len(bits)
        self.rows = buf.shape[len(bits)]
        self.cols = slice(None) if cols is None else cols

    def view(self, lead, start, size):
        index = tuple(i if isinstance(i, int) else slice(None) for i in lead)
        return self.buf.at[index + (pl.ds(start, size), self.cols)]

    def send(self):
        bit = self.order[self.step]
        shift = self.links.shift
        self.recv = self.recvs.pop(0)
        if isinstance(bit, tuple):
            self.rows //= 4
            self.copies = [
                self.links.exchange(
                    self.view(self.at, n * self.rows, self.rows),
                    self.recv.at[n - 1],
                    *(shift << b for k, b in enumerate(bit) if (n >> (1 - k)) & 1),
                )
                for n in (1, 2, 3)
            ]
            return
        if bit in self.bits:
            lead = list(self.at)
            lead[self.bits.index(bit)] = 1
            src = self.view(lead, 0, self.rows)
            self.at[self.bits.index(bit)] = 0
        else:
            self.rows //= 2
            src = self.view(self.at, self.rows, self.rows)
        self.copies = [self.links.exchange(src, self.recv, shift << bit)]

    def add(self):
        for copy in self.copies:
            copy.wait_recv()
        self.step += 1
        if self.step == len(self.order):
            return
        leads = [()]
        for i in self.at:
            leads = [a + (b,) for a in leads for b in ((0, 1) if i != 0 else (0,))]
        free = [n for n, i in enumerate(self.at) if i != 0]
        buf, recv, cols = self.buf, self.recv, self.cols

        @pl.loop(0, self.rows // 16)
        def _(i):
            at = pl.ds(pl.multiple_of(i * 16, 16), 16)
            for lead in leads:
                from_ = tuple(lead[n] for n in free)
                to = lead + (at, cols)
                buf[to] = both(buf[to], recv[from_ + (at,)])

        self.send()

    def last(self):
        lead = (0,) * len(self.bits)
        total = self.buf[lead + (slice(0, self.rows), self.cols)].astype(F32)
        if isinstance(self.order[-1], tuple):
            for n in range(3):
                total = total + self.recv[n].astype(F32)
            return total
        return total + self.recv[...].astype(F32)


def flat_recvs(bits, order, step, cols, blocks_rows):
    lead, rows = len(bits), blocks_rows
    shapes = []
    for bit in order[step:]:
        if isinstance(bit, tuple):
            shapes.append((3, rows // 4, cols))
            continue
        if bit in bits:
            lead -= 1
        else:
            rows //= 2
        shapes.append((2,) * lead + (rows, cols))
    return shapes


def shuffle(links, width):
    short = width // BLOCKS
    col = lax.broadcasted_iota(jnp.int32, (8, width), 1)
    source = col
    for p in range(BLOCKS):
        c = 0
        for k, b in enumerate(FLAT):
            mine, its = (links.block // (1 << b)) % 2, (p >> (LEVELS - 1 - k)) & 1
            c = c + (mine + its - 2 * mine * its) * (1 << b)
        source = jnp.where(col >= p * short, col + (c - p) * short, source)
    row = lax.broadcasted_iota(jnp.int32, (width, width), 0)
    return (row == source[0:1]).astype(F32).astype(BF16)


FLAT = (0, 2, 1, 3, 4)
DN_ONE = (0, 2, 1, 3, 4)
DN_TWO = (0, 1, 2, 3, 4)
UP_ONE = (0, 2, 1, 3, 4)
UP_TWO = (0, 3, 2, 1, 4)
OUT_ORDER = (0, 2, 1, 3, 4)
LEFT_ORDER = (0, 2, 1, (3, 4))
RIGHT_ORDER = (0, 1, 2, (3, 4))
BLOCKS = 1 << LEVELS


def first_kernel(
    ndev, parts, x_ref, lengths, wq_hbm, bq, wk_hbm, wv_hbm, bv,
    q_hbm, k_hbm, v_hbm, onehot, qmask, bounds, mix, xp,
    halo, wq, wk, wv, q_ref, k_ref, v_ref, load_sems, store_sems, send_sems, recv_sems,
):
    rows, width = x_ref.shape
    count = rows * parts
    loads = [
        pltpu.make_async_copy(src, dst, load_sems.at[n])
        for n, (src, dst) in enumerate(((wq_hbm, wq), (wk_hbm, wk), (wv_hbm, wv)))
    ]
    for load in loads:
        load.start()
    links = Links(ndev, parts, send_sems, recv_sems)
    links.greet([], True)
    step = rows // 2
    pairs = [
        links.neighbours(
            x_ref.at[pl.ds(h * step, step)],
            halo.at[pl.ds(h * step, step)],
            halo.at[pl.ds(2 * rows + h * step, step)],
        )
        for h in range(2)
    ]

    @pl.when(jnp.logical_not(links.has_prev))
    def _():
        halo[0:rows, :] = jnp.zeros((rows, width), BF16)

    @pl.when(jnp.logical_not(links.has_next))
    def _():
        halo[2 * rows : 3 * rows, :] = jnp.zeros((rows, width), BF16)

    halo[rows : 2 * rows, :] = x_ref[...]

    for load in loads:
        load.wait()

    def stores(at, n):
        part = pl.ds(at, step)
        return [
            pltpu.make_async_copy(src.at[part], dst.at[part], store_sems.at[n, m])
            for m, (src, dst) in enumerate(((q_ref, q_hbm), (k_ref, k_hbm), (v_ref, v_hbm)))
        ]

    def chunk(t):
        return jnp.where(t < 2, 2 + t, (t % 2) * 4 + t // 2 - 1)

    def project(t):
        at = pl.multiple_of(chunk(t) * step, step)
        rows_at = pl.ds(at, step)
        x = halo[rows_at, :]
        q_ref[rows_at, :] = (nn(x, wq[...]) + line(bq)).astype(BF16)
        k_ref[rows_at, :] = nn(x, wk[...]).astype(BF16)
        v_ref[rows_at, :] = (nn(x, wv[...]) + line(bv)).astype(BF16)
        for copy in stores(at, t):
            copy.start()

    pl.loop(0, 2)(project)

    slots = lengths.shape[1]
    ends, total = [], jnp.int32(0)
    for n in range(slots):
        total = total + lengths[0, n]
        ends.append(total)
    start = (links.place - 1) * rows
    lane = lax.broadcasted_iota(jnp.int32, (BQ, PAIR), 1) % HEAD_DIM
    one, none, far = BF16(1.0), BF16(0.0), BF16(NEG)

    @pl.loop(0, 3 * rows // BQ)
    def _(i):
        at = start + i * BQ
        where = at + lax.broadcasted_iota(jnp.int32, (BQ, PAIR), 0)
        seg = jnp.zeros((BQ, PAIR), jnp.int32)
        for end in ends:
            seg = seg + (where >= end).astype(jnp.int32)
        outside = (where < 0) | (where >= count)
        seg = jnp.where(outside, slots, seg)
        match = (seg == lane).astype(F32)
        to = pl.ds(pl.multiple_of(i * BQ, BQ), BQ)
        onehot[to, :] = match.astype(BF16)
        qmask[to, :] = ((1.0 - match) * NEG).astype(BF16)

    mix[...] = shuffle(links, width)
    xp[...] = nn(x_ref[...], mix[...]).astype(BF16)

    for n in range(rows // BQ):
        near = links.place * rows + n * BQ
        far_row = near + BQ - 1
        lo, hi = jnp.int32(0), jnp.int32(count)
        for end in ends:
            lo = jnp.where(end <= near, jnp.maximum(lo, end), lo)
            hi = jnp.where(end > far_row, jnp.minimum(hi, end), hi)
        lo = jnp.maximum(lo - start, 0)
        hi = jnp.minimum(hi - start, 3 * rows)
        bounds[0, n] = lo // BK
        bounds[1, n] = (hi + BK - 1) // BK

    @pl.loop(2, 6)
    def _(t):
        for h in range(2):

            @pl.when(t == 2 + 2 * h)
            def _():
                links.from_prev(pairs[h])

            @pl.when(t == 3 + 2 * h)
            def _():
                links.from_next(pairs[h])

        project(t)

    for pair in pairs:
        links.sent(pair)

    @pl.loop(0, 6)
    def _(t):
        for copy in stores(pl.multiple_of(chunk(t) * step, step), t):
            copy.wait()


def first(ndev, parts, x, lengths, wq, bq, wk, wv, bv):
    rows, width = x.shape
    ext = jax.ShapeDtypeStruct((3 * rows, width), BF16)
    seg = jax.ShapeDtypeStruct((3 * rows, PAIR), BF16)
    smem = pl.BlockSpec(memory_space=pltpu.SMEM)
    return pl.pallas_call(
        functools.partial(first_kernel, ndev, parts),
        in_specs=[whole(), smem, hbm(), whole(), hbm(), hbm(), whole()],
        out_specs=[hbm()] * 3 + [whole()] * 2 + [smem] + [whole()] * 2,
        out_shape=[ext] * 3
        + [seg] * 2
        + [
            jax.ShapeDtypeStruct((2, rows // BQ), jnp.int32),
            jax.ShapeDtypeStruct((width, width), BF16),
            jax.ShapeDtypeStruct((rows, width), BF16),
        ],
        scratch_shapes=[
            pltpu.VMEM((3 * rows, width), BF16),
            pltpu.VMEM((width, width), BF16),
            pltpu.VMEM((width, width), BF16),
            pltpu.VMEM((width, width), BF16),
            pltpu.VMEM((3 * rows, width), BF16),
            pltpu.VMEM((3 * rows, width), BF16),
            pltpu.VMEM((3 * rows, width), BF16),
            pltpu.SemaphoreType.DMA((3,)),
            pltpu.SemaphoreType.DMA((6, 3)),
            pltpu.SemaphoreType.DMA((4,)),
            pltpu.SemaphoreType.DMA((4,)),
        ],
        compiler_params=remote_params(0),
        cost_estimate=cost(15e9, 12 << 20),
        name="first",
    )(x, lengths, wq, bq, wk, wv, bv)


def lengths_of(rows):
    most = BQ // BK + 2 * -(-(rows - 1) // BK)
    return [n for n in range(3, most) if n <= 6 or n % 2 == 0] + [most]


def key_range(bounds, i, rows):
    lo, hi = bounds[0, i], bounds[1, i]
    sizes = lengths_of(rows)
    number = jnp.int32(sizes[-1])
    for n in reversed(sizes):
        number = jnp.where(hi - lo <= n, n, number)
    return jnp.minimum(lo, 3 * rows // BK - number), number


def forward_kernel(bounds, q_ref, k_ref, v_ref, onehot, qmask, ctx_ref, lse_ref, ka, kb):
    rows = ctx_ref.shape[0]
    low = low_lanes()
    key, hot = k_ref[...], onehot[...]
    ka[...] = jnp.where(low, key, hot)
    kb[...] = jnp.where(low, hot, key)

    @pl.loop(0, rows // BQ)
    def _(i):
        first_block, number = key_range(bounds, i, rows)
        base = pl.multiple_of(first_block * BK, BK)
        at = pl.ds(pl.multiple_of(i * BQ, BQ), BQ)
        own = pl.ds(pl.multiple_of(rows + i * BQ, BQ), BQ)
        for num in lengths_of(rows):

            @pl.when(number == num)
            def _():
                span = pl.ds(base, num * BK)
                query = q_ref[own, :] * BF16(HEAD_DIM**-0.5)
                mask = qmask[own, :]
                parts = []
                for head, keys in enumerate((ka, kb)):
                    pick = (query, mask) if head == 0 else (mask, query)
                    scores = nt(jnp.where(low, *pick), keys[span, :])
                    top = jnp.max(scores, axis=1, keepdims=True)
                    weights = jnp.exp(scores - top)
                    total = jnp.sum(weights, axis=1, keepdims=True)
                    acc = nn(weights.astype(BF16), v_ref[span, :])
                    parts.append((acc / total, top + jnp.log(total)))
                ctx_ref[at, :] = jnp.where(low, parts[0][0], parts[1][0])
                flip = jnp.where(low, parts[0][1], parts[1][1]).T
                lse_ref[0, 0:1, at] = flip[0:1]
                lse_ref[0, 1:2, at] = flip[HEAD_DIM : HEAD_DIM + 1]


def attend_forward(bounds, q, k, v, onehot, qmask):
    rows, width = q.shape[0] // 3, q.shape[1]
    pairs = width // PAIR
    ext = pl.BlockSpec((3 * rows, PAIR), lambda p, *_: (0, p))
    seg = pl.BlockSpec((3 * rows, PAIR), lambda p, *_: (0, 0))
    grid = pltpu.PrefetchScalarGridSpec(
        num_scalar_prefetch=1,
        grid=(pairs,),
        in_specs=[ext, ext, ext, seg, seg],
        out_specs=[
            pl.BlockSpec((rows, PAIR), lambda p, *_: (0, p)),
            pl.BlockSpec((1, 2, rows), lambda p, *_: (p, 0, 0)),
        ],
        scratch_shapes=[pltpu.VMEM((3 * rows, PAIR), BF16)] * 2,
    )
    return pl.pallas_call(
        forward_kernel,
        grid_spec=grid,
        out_shape=[
            jax.ShapeDtypeStruct((rows, width), F32),
            jax.ShapeDtypeStruct((pairs, 2, rows), F32),
        ],
        compiler_params=params(),
        cost_estimate=cost(20e9, 24 * rows * width),
        name="attend_forward",
    )(bounds, q, k, v, onehot, qmask)


def backward_kernel(
    bounds, q_ref, k_ref, v_ref, g_ref, stat_ref, onehot, qmask,
    dq_ref, dk_ref, dv_ref, ka, kb, qa, qb, qs,
):
    rows = dq_ref.shape[0]
    low = low_lanes()
    zero = jnp.zeros((1, PAIR), BF16)
    scale = BF16(HEAD_DIM**-0.5)
    key, hot = k_ref[...], onehot[...]
    ka[...] = jnp.where(low, key, hot)
    kb[...] = jnp.where(low, hot, key)
    query, mask = q_ref[...] * scale, qmask[...]
    qa[...] = jnp.where(low, query, mask)
    qb[...] = jnp.where(low, mask, query)
    qs[...] = query

    @pl.loop(0, rows // BQ)
    def _(i):
        first_block, number = key_range(bounds, i, rows)
        base = pl.multiple_of(first_block * BK, BK)
        at = pl.ds(pl.multiple_of(i * BQ, BQ), BQ)
        own = pl.ds(pl.multiple_of(rows + i * BQ, BQ), BQ)
        for num in lengths_of(rows):

            @pl.when(number == num)
            def _():
                span = pl.ds(base, num * BK)

                def pick(head, value, other):
                    return jnp.where(low, value, other) if head == 0 else jnp.where(
                        low, other, value
                    )

                columns = stat_ref[0, :, own]
                columns = jnp.concatenate([columns, columns], axis=0).T
                out = []
                for head, keys in enumerate((ka, kb)):
                    queries = (qa, qb)[head][own, :]
                    grads = pick(head, g_ref[own, :], zero)
                    scores = nt(queries, keys[span, :])
                    prob_grad = nt(grads, v_ref[span, :])
                    probs = jnp.exp(scores - columns[:, head : head + 1])
                    delta = columns[:, 2 + head : 3 + head]
                    score_grad = (probs * (prob_grad - delta)).astype(BF16)
                    out.append(nn(score_grad, k_ref[span, :]))
                dq = jnp.where(low, out[0], out[1]) * F32(HEAD_DIM**-0.5)
                dq_ref[at, :] = dq.astype(BF16)
                out = []
                for head, queries in enumerate((qa, qb)):
                    keys = (ka, kb)[head][own, :]
                    vals = pick(head, v_ref[own, :], zero)
                    scores = nt(keys, queries[span, :])
                    prob_grad = nt(vals, g_ref[span, :])
                    probs = jnp.exp(scores - stat_ref[0, head : head + 1, span])
                    delta = stat_ref[0, 2 + head : 3 + head, span]
                    score_grad = (probs * (prob_grad - delta)).astype(BF16)
                    out.append((
                        nn(score_grad, qs[span, :]),
                        nn(probs.astype(BF16), g_ref[span, :]),
                    ))
                dk_ref[at, :] = jnp.where(low, out[0][0], out[1][0]).astype(BF16)
                dv_ref[at, :] = jnp.where(low, out[0][1], out[1][1]).astype(BF16)


def attend_backward(bounds, q, k, v, g, stat, onehot, qmask):
    rows, width = q.shape[0] // 3, q.shape[1]
    pairs = width // PAIR
    ext = pl.BlockSpec((3 * rows, PAIR), lambda p, *_: (0, p))
    own = pl.BlockSpec((rows, PAIR), lambda p, *_: (0, p))
    seg = pl.BlockSpec((3 * rows, PAIR), lambda p, *_: (0, 0))
    grid = pltpu.PrefetchScalarGridSpec(
        num_scalar_prefetch=1,
        grid=(pairs,),
        in_specs=[ext] * 4 + [pl.BlockSpec((1, 4, 3 * rows), lambda p, *_: (p, 0, 0)), seg, seg],
        out_specs=[own] * 3,
        scratch_shapes=[pltpu.VMEM((3 * rows, PAIR), BF16)] * 5,
    )
    return pl.pallas_call(
        backward_kernel,
        grid_spec=grid,
        out_shape=[jax.ShapeDtypeStruct((rows, width), BF16)] * 3,
        compiler_params=params(),
        cost_estimate=cost(40e9, 40 * rows * width),
        name="attend_backward",
    )(bounds, q, k, v, g, stat, onehot, qmask)


def norm_forward(h):
    mean = jnp.mean(h, axis=-1, keepdims=True)
    centred = h - mean
    variance = jnp.mean(centred * centred, axis=-1, keepdims=True)
    inverse = lax.rsqrt(variance + layer_eps)
    return centred * inverse, inverse


def norm_backward(grad, gain, hat, inverse):
    g = grad * gain
    return inverse * (
        g - jnp.mean(g, axis=-1, keepdims=True) - hat * jnp.mean(g * hat, axis=-1, keepdims=True)
    )


def colsum(v):
    return jnp.sum(v, axis=0, keepdims=True)


def middle_kernel(
    ndev, parts,
    x_ref, ctx_ref, ct_ref, wo, bo, g1, s1, wup_hbm, bup, wdn_hbm, bdn, g2, s2, lse_ref, mix,
    result_hbm, fg_hbm, g_hbm, stat_ref, vec_ref, bup_ref,
    one_keep_hbm, one_send_hbm, two_keep_hbm, two_send_hbm, upa_keep_hbm, upa_send_hbm, upb_keep_hbm,
    upb_send_hbm, wo_keep_hbm, wo_send_hbm,
    wup, wdn, hid, nl, nlp, bg, cl, ag, slope, normed, inv, acc, grad_s,
    result_ref, fg_ref, g_ref,
    one_s, one_r, two_s, two_r, up_s, up_r, wo_s, wo_r,
    load_sems, store_sems, send_sems, recv_sems,
):
    stores = []

    def store(src, dst):
        copy = pltpu.make_async_copy(src, dst, store_sems.at[len(stores)])
        copy.start()
        stores.append(copy)

    rows, width = x_ref.shape
    ff = wup.shape[1]
    rc, fc = 256, 1024
    chunks, tiles = rows // rc, ff // fc
    tall, short = ff // BLOCKS, width // BLOCKS
    up_copy = pltpu.make_async_copy(wup_hbm, wup, load_sems.at[0])
    dn_copy = pltpu.make_async_copy(wdn_hbm, wdn, load_sems.at[1])
    up_copy.start()
    dn_copy.start()
    links = Links(ndev, parts, send_sems, recv_sems)
    links.greet([links.shift << DN_ONE[0], links.shift << DN_ONE[1]], True)
    one = Chain(links, one_s, one_r, DN_ONE, 0)
    two = Chain(links, two_s, two_r, DN_TWO, 0)
    @pl.loop(0, chunks)
    def _(r):
        at = pl.ds(pl.multiple_of(r * rc, rc), rc)
        c_low = ctx_ref[at, :].astype(BF16)
        cl[at, :] = nn(c_low, mix[...]).astype(BF16)
        h = x_ref[at, :].astype(F32) + (nn(c_low, wo[...]) + line(bo))
        xhat, inverse = norm_forward(h)
        res = xhat * line(g1) + line(s1)
        fg_ref[at, :] = xhat
        inv[at, :] = inverse
        normed[at, :] = res
        low = res.astype(BF16)
        nl[at, :] = low
        nlp[at, :] = nn(low, mix[...]).astype(BF16)

    up_copy.wait()
    dn_copy.wait()
    acc[...] = jnp.zeros_like(acc)

    @pl.loop(0, tiles)
    def _(j):
        cols = pl.ds(pl.multiple_of(j * fc, fc), fc)
        bias = bup[cols].reshape(1, fc)

        @pl.loop(0, chunks)
        def _(r):
            at = pl.ds(pl.multiple_of(r * rc, rc), rc)
            up = nn(nl[at, :], wup[:, cols]) + bias
            cdf = 0.5 * (1.0 + lax.erf(up * F32(0.5**0.5)))
            density = jnp.exp(-0.5 * up * up) * F32(0.3989422804014327)
            slope[at, cols] = cdf + up * density
            act = (up * cdf).astype(BF16)
            hid[at, cols] = act
            acc[at, :] = acc[at, :] + nn(act, wdn[cols, :])

    vec_ref[...] = jnp.zeros_like(vec_ref)

    @pl.loop(0, chunks)
    def _(r):
        at = pl.ds(pl.multiple_of(r * rc, rc), rc)
        xhat, inverse = norm_forward(normed[at, :] + (acc[at, :] + line(bdn)))
        result_ref[at, :] = (xhat * line(g2) + line(s2)).astype(BF16)
        ct = ct_ref[at, :].astype(F32)
        second = norm_backward(ct, line(g2), xhat, inverse)
        low = second.astype(BF16)
        bg[at, :] = low
        acc[at, :] = second
        vec_ref[0:1, :] = vec_ref[0:1, :] + colsum(ct * xhat)
        vec_ref[1:2, :] = vec_ref[1:2, :] + colsum(ct)
        vec_ref[2:3, :] = vec_ref[2:3, :] + colsum(low.astype(F32))

    store(result_ref, result_hbm)

    some = width // tall

    @pl.loop(0, ff // width)
    def _(j):
        grad_s[...] = tn(hid[:, pl.ds(pl.multiple_of(j * width, width), width)], bg[...])

        @pl.loop(0, some)
        def _(c):
            base = pl.multiple_of(c * tall, tall // 2)
            one_s[one.position(j * some + c)] = grad_s[pl.ds(base, tall // 2), :].astype(BF16)
            base = pl.multiple_of(c * tall + tall // 2, tall // 2)
            two_s[two.position(j * some + c)] = grad_s[pl.ds(base, tall // 2), :].astype(BF16)

    one.send()
    two.send()

    def back_tiles(lo, hi):
        @pl.loop(lo, hi)
        def _(j):
            cols = pl.ds(pl.multiple_of(j * fc, fc), fc)
            bup_ref[:, cols] = jnp.zeros((1, fc), F32)

            @pl.loop(0, chunks)
            def _(r):
                at = pl.ds(pl.multiple_of(r * rc, rc), rc)
                grad = (nt(bg[at, :], wdn[cols, :]) * slope[at, cols]).astype(BF16)
                hid[at, cols] = grad
                bup_ref[:, cols] = bup_ref[:, cols] + colsum(grad.astype(F32))
                acc[at, :] = acc[at, :] + nt(grad, wup[:, cols])

    back_tiles(0, tiles - 1)
    one.add()
    back_tiles(tiles - 1, tiles)

    zero_prev = pltpu.make_async_copy(
        result_ref, g_hbm.at[pl.ds(0, rows)], store_sems.at[store_sems.shape[0] - 2]
    )
    zero_next = pltpu.make_async_copy(
        result_ref, g_hbm.at[pl.ds(2 * rows, rows)], store_sems.at[store_sems.shape[0] - 1]
    )
    stores.pop().wait()
    result_ref[...] = jnp.zeros_like(result_ref)

    @pl.when(jnp.logical_not(links.has_prev))
    def _():
        zero_prev.start()
        stat_ref[:, :, 0:rows] = jnp.zeros((width // PAIR, 4, rows), F32)

    @pl.when(jnp.logical_not(links.has_next))
    def _():
        zero_next.start()
        stat_ref[:, :, 2 * rows : 3 * rows] = jnp.zeros((width // PAIR, 4, rows), F32)

    pairs = []
    for r in range(chunks):
        at = slice(r * rc, (r + 1) * rc)
        mid = slice(rows + r * rc, rows + (r + 1) * rc)
        total = acc[at, :]
        xhat = fg_ref[at, :]
        first_grad = norm_backward(total, line(g1), xhat, inv[at, :])
        fg_ref[at, :] = first_grad
        low = first_grad.astype(BF16)
        ag[at, :] = low
        vec_ref[3:4, :] = vec_ref[3:4, :] + colsum(total * xhat)
        vec_ref[4:5, :] = vec_ref[4:5, :] + colsum(total)
        vec_ref[5:6, :] = vec_ref[5:6, :] + colsum(low.astype(F32))
        cg = nt(low, wo[...]).astype(BF16)
        g_ref[at, :] = cg
        pairs.append(links.neighbours(
            g_ref.at[pl.ds(r * rc, rc)],
            g_hbm.at[pl.ds(r * rc, rc)],
            g_hbm.at[pl.ds(2 * rows + r * rc, rc)],
        ))
        prod = cg.astype(F32) * ctx_ref[at, :]
        for p in range(width // PAIR):
            flip = prod[:, p * PAIR : (p + 1) * PAIR].T
            stat_ref[p, 2:3, mid] = colsum(flip[:HEAD_DIM])
            stat_ref[p, 3:4, mid] = colsum(flip[HEAD_DIM:])
    store(g_ref, g_hbm.at[pl.ds(rows, rows)])
    store(fg_ref, fg_hbm)
    for p in range(width // PAIR):
        stat_ref[p, 0:2, rows : 2 * rows] = lse_ref[p]
    pairs.append(links.neighbours(
        stat_ref.at[:, :, pl.ds(rows, rows)],
        stat_ref.at[:, :, pl.ds(0, rows)],
        stat_ref.at[:, :, pl.ds(2 * rows, rows)],
    ))

    quarter = width // 8
    ups = []
    for n in range(2):

        @pl.loop(0, 2)
        def _(t):
            cols = pl.ds(pl.multiple_of(n * (ff // 2) + t * width, width), width)
            grad = tn(nlp[...], hid[:, cols])
            up_s[:, :, :, :, cols] = grad.astype(BF16).reshape(2, 2, 2, quarter, width)

        cols = pl.ds(n * (ff // 2), ff // 2)
        ups.append(links.exchange(
            up_s.at[1, :, :, :, cols], up_r.at[:, :, :, cols], links.shift << FLAT[0]
        ))

    wo_s[...] = tn(cl[...], ag[...]).astype(BF16).reshape(2, 2, 2, quarter, width)
    out = links.exchange(wo_s.at[1], wo_r, links.shift << FLAT[0])

    def settle(chain, keep, send):
        chain.receive()
        half, quarter = BLOCKS // 2, BLOCKS // 4

        @pl.loop(0, half)
        def _(i):
            chain.recv[i] = both(chain.buf[i], chain.recv[i])

        store(chain.recv.at[pl.ds(0, quarter)], keep)
        store(chain.recv.at[pl.ds(quarter, quarter)], send)

    settle(two, two_keep_hbm, two_send_hbm)

    def settle_flat(copy, mine, got, cols):
        copy.wait_recv()

        @pl.loop(0, quarter // 16)
        def _(i):
            at = pl.ds(pl.multiple_of(i * 16, 16), 16)
            for x_bit in range(2):
                for y_bit in range(2):
                    index = (x_bit, y_bit, at, cols)
                    got[index] = both(mine[(0,) + index], got[index])

    left, right = pl.ds(0, ff // 2), pl.ds(ff // 2, ff // 2)
    settle_flat(ups[0], up_s, up_r, left)
    store(up_r.at[0, :, :, left], upa_keep_hbm)
    store(up_r.at[1, :, :, left], upa_send_hbm)
    settle_flat(ups[1], up_s, up_r, right)
    store(up_r.at[:, :, pl.ds(0, quarter // 2), right], upb_keep_hbm)
    store(up_r.at[:, :, pl.ds(quarter // 2, quarter // 2), right], upb_send_hbm)
    settle_flat(out, wo_s, wo_r, slice(None))
    store(wo_r.at[0], wo_keep_hbm)
    store(wo_r.at[1], wo_send_hbm)
    one.receive()

    @pl.loop(0, BLOCKS // 4)
    def _(i):
        one_s[i] = both(one_s[i], one_r[BLOCKS // 2 + i])

    store(one_s.at[pl.ds(0, BLOCKS // 8)], one_keep_hbm)
    store(one_s.at[pl.ds(BLOCKS // 8, BLOCKS // 8)], one_send_hbm)
    for copy in stores:
        copy.wait()

    @pl.when(jnp.logical_not(links.has_prev))
    def _():
        zero_prev.wait()

    @pl.when(jnp.logical_not(links.has_next))
    def _():
        zero_next.wait()

    for pair in pairs:
        links.from_prev(pair)
        links.from_next(pair)
        links.sent(pair)
    links.finish()


def middle(ndev, parts, x, ctx, ct, wo, bo, g1, s1, wup, bup, wdn, bdn, g2, s2, lse, mix):
    rows, width = x.shape
    ff = wup.shape[1]
    pairs = width // PAIR
    tall, short = ff // BLOCKS, width // BLOCKS
    left = BLOCKS // 4

    def out(*shape, dtype=BF16):
        return jax.ShapeDtypeStruct(shape, dtype)

    shapes = [
        out(rows, width),
        out(rows, width, dtype=F32),
        out(3 * rows, width),
        out(pairs, 4, 3 * rows, dtype=F32),
        out(8, width, dtype=F32),
        out(1, ff, dtype=F32),
        out(left // 2, tall // 2, width),
        out(left // 2, tall // 2, width),
        out(left, tall // 2, width),
        out(left, tall // 2, width),
        out(2, width // 8, ff // 2),
        out(2, width // 8, ff // 2),
        out(2, 2, width // 16, ff // 2),
        out(2, 2, width // 16, ff // 2),
        out(2, width // 8, width),
        out(2, width // 8, width),
    ]

    def chain(*shape):
        return [pltpu.VMEM((BLOCKS,) + shape, BF16), pltpu.VMEM((BLOCKS // 2,) + shape, BF16)]

    dn_one = chain(tall // 2, width)
    dn_one[1] = pltpu.VMEM((3 * BLOCKS // 4, tall // 2, width), BF16)
    copies = 6 + 6
    return pl.pallas_call(
        functools.partial(middle_kernel, ndev, parts),
        in_specs=[whole()] * 7 + [hbm(), whole(), hbm()] + [whole()] * 5,
        out_specs=[hbm()] * 3 + [whole()] * 3 + [hbm()] * 10,
        out_shape=shapes,
        scratch_shapes=[
            pltpu.VMEM((width, ff), BF16),
            pltpu.VMEM((ff, width), BF16),
            pltpu.VMEM((rows, ff), BF16),
            pltpu.VMEM((rows, width), BF16),
            pltpu.VMEM((rows, width), BF16),
            pltpu.VMEM((rows, width), BF16),
            pltpu.VMEM((rows, width), BF16),
            pltpu.VMEM((rows, width), BF16),
            pltpu.VMEM((rows, ff), F32),
            pltpu.VMEM((rows, width), F32),
            pltpu.VMEM((rows, 1), F32),
            pltpu.VMEM((rows, width), F32),
            pltpu.VMEM((width, width), F32),
            pltpu.VMEM((rows, width), BF16),
            pltpu.VMEM((rows, width), F32),
            pltpu.VMEM((rows, width), BF16),
        ]
        + dn_one + chain(tall // 2, width)
        + [
            pltpu.VMEM((2, 2, 2, width // 8, ff), BF16),
            pltpu.VMEM((2, 2, width // 8, ff), BF16),
            pltpu.VMEM((2, 2, 2, width // 8, width), BF16),
            pltpu.VMEM((2, 2, width // 8, width), BF16),
        ]
        + [
            pltpu.SemaphoreType.DMA((2,)),
            pltpu.SemaphoreType.DMA((15,)),
            pltpu.SemaphoreType.DMA((copies,)),
            pltpu.SemaphoreType.DMA((copies,)),
        ],
        compiler_params=remote_params(1),
        cost_estimate=cost(50e9, 30 << 20),
        name="middle",
    )(x, ctx, ct, wo, bo, g1, s1, wup, bup, wdn, bdn, g2, s2, lse, mix)


def tail_kernel(
    ndev, parts,
    xp, dq_hbm, dk_hbm, dv_hbm, wq, wk, wv, fg, one_keep, one_got, two_keep, two_got,
    upa_keep, upa_got, upb_keep, upb_got, wo_keep, wo_got, vec, bup,
    ig_ref, dn1_out, dn2_out, up1_out, up2_out, wo_out, q_out, k_out, v_out, vec_out, bup_out,
    one_s, one_r, two_s, two_r, grads, vec_s, vec_r, bup_s, bup_r,
    load_sems, send_sems, recv_sems, upa_s, upb_s, wo_s, qkv_s, *recvs,
):
    rows, width = xp.shape
    loads = []
    for n, src in enumerate((dq_hbm, dk_hbm, dv_hbm)):
        to = grads.at[:, pl.ds(n * width, width)]
        loads.append(pltpu.make_async_copy(src, to, load_sems.at[n]))
    for load in loads:
        load.start()
    links = Links(ndev, parts, send_sems, recv_sems)
    flips = [1 << n for n in range(ndev.bit_length() - 1)]
    links.greet(flips + [(links.shift << 3, links.shift << 4)], False)
    one = Chain(links, one_s, one_r, DN_ONE, 3)
    two = Chain(links, two_s, two_r, DN_TWO, 2)
    recvs = iter(recvs)
    half = 3 * width // 2

    def chain(n, buf, cols=None):
        _, bits, order, step, _, _ = FLATS[n]
        return Flat(links, buf, [next(recvs) for _ in order[step:]], bits, order, step, cols)

    upa, upb, out = (chain(n, buf) for n, buf in enumerate((upa_s, upb_s, wo_s)))
    left = chain(3, qkv_s, slice(0, half))
    right = chain(4, qkv_s, slice(half, 2 * half))

    def begin(chain, keep, got):
        @pl.loop(0, keep.shape[0])
        def _(i):
            chain.buf[i] = both(keep[i], got[i])

        chain.send()

    def begin_flat(chain, keep, got):
        leads = [()]
        for size in keep.shape[:-2]:
            leads = [a + (b,) for a in leads for b in range(size)]

        @pl.loop(0, keep.shape[-2] // 16)
        def _(i):
            at = pl.ds(pl.multiple_of(i * 16, 16), 16)
            for lead in leads:
                index = lead + (at, slice(None))
                chain.buf[index] = both(keep[index], got[index])

        chain.send()

    begin(two, two_keep, two_got)
    begin_flat(upa, upa_keep, upa_got)
    for load in loads:
        load.wait()
    tile = width // 2

    def weights(chain, first_tile):
        @pl.loop(first_tile, first_tile + 3)
        def _(n):
            cols = pl.ds(pl.multiple_of(n * tile, tile), tile)
            part = tn(xp[...], grads[:, cols])
            qkv_s[:, :, :, :, cols] = part.astype(BF16).reshape(2, 2, 2, width // 8, tile)

        chain.send()

    weights(left, 0)
    weights(right, 3)
    begin_flat(upb, upb_keep, upb_got)
    begin_flat(out, wo_keep, wo_got)
    begin(one, one_keep, one_got)
    vec_s[0] = vec[...]
    vec_s[0, 6:7, :] = colsum(grads[:, 0:width].astype(F32))
    vec_s[0, 7:8, :] = colsum(grads[:, 2 * width : 3 * width].astype(F32))
    bup_s[0] = bup[...]

    def vectors(n):
        if n >= len(flips):
            return None
        return [
            links.exchange(vec_s.at[n], vec_r.at[n], flips[n]),
            links.exchange(bup_s.at[n], bup_r.at[n], flips[n]),
        ]

    def add_vectors(n, copies):
        for c in copies:
            c.wait_recv()
        vec_s[n + 1] = vec_s[n] + vec_r[n]
        bup_s[n + 1] = bup_s[n] + bup_r[n]
        return vectors(n + 1)

    pending = vectors(0)
    left.add()
    right.add()

    @pl.loop(0, 2)
    def _(r):
        at = pl.ds(pl.multiple_of(r * (rows // 2), rows // 2), rows // 2)
        total = nt(grads[at, 0:width], wq[...]) + nt(grads[at, width : 2 * width], wk[...])
        total = total + nt(grads[at, 2 * width : 3 * width], wv[...])
        ig_ref[at, :] = (total + fg[at, :]).astype(BF16)

    pending = add_vectors(0, pending)
    two.add()
    upa.add()
    upb.add()
    out.add()
    one.add()
    pending = add_vectors(1, pending)
    left.add()
    right.add()
    pending = add_vectors(2, pending)
    two.add()
    upa.add()
    upb.add()
    out.add()
    one.add()
    left.add()
    right.add()
    pending = add_vectors(3, pending)
    two.add()
    upa.add()
    upb.add()
    out.add()
    dn1_out[...] = one.last()
    dn2_out[...] = two.last()
    up1_out[...] = upa.last()
    up2_out[...] = upb.last()
    wo_out[...] = out.last()
    for n in range(4, len(flips)):
        pending = add_vectors(n, pending)
    vec_out[...] = vec_s[len(flips)]
    bup_out[...] = bup_s[len(flips)]
    left.add()
    right.add()
    mine = left.last()
    q_out[...] = mine[:, 0:width]
    k_out[:, 0:tile] = mine[:, width:]
    mine = right.last()
    k_out[:, tile:] = mine[:, 0:tile]
    v_out[...] = mine[:, tile:]
    links.finish()


FLATS = (
    ("upa", (1,), UP_ONE, 2, 4, 1),
    ("upb", (2, 1), UP_TWO, 2, 4, 2),
    ("out", (1,), OUT_ORDER, 2, 2, 1),
    ("left", (0, 2, 1), LEFT_ORDER, 0, 3, 1),
    ("right", (0, 2, 1), RIGHT_ORDER, 0, 3, 1),
)


def tail(ndev, parts, xp, dq, dk, dv, wq, wk, wv, fg, one, two, upa, upb, wo, vec, bup):
    rows, width = xp.shape
    short = width // BLOCKS
    tall, ff = one[0].shape[1] * 2, upa[0].shape[2] * 2
    steps = ndev.bit_length() - 1

    def out(*shape):
        return jax.ShapeDtypeStruct(shape, F32)

    def chain(step, *shape):
        return [pltpu.VMEM((BLOCKS >> step,) + shape, BF16)] * 2

    flat, received = [], []
    for _, bits, order, step, wide, cut in FLATS:
        cols, tops = wide * width // 2, width // 8 // cut
        flat.append(pltpu.VMEM((2,) * len(bits) + (tops, cols), BF16))
        received += [pltpu.VMEM(u, BF16) for u in flat_recvs(bits, order, step, cols, tops)]
    flat = flat[:3] + [pltpu.VMEM((2, 2, 2, width // 8, 3 * width), BF16)]
    copies = 2 + 3 + 3 * 3 + 2 * 6 + 2 * steps
    return pl.pallas_call(
        functools.partial(tail_kernel, ndev, parts),
        in_specs=[whole()] + [hbm()] * 3 + [whole()] * 16,
        out_specs=[whole()] * 11,
        out_shape=[
            jax.ShapeDtypeStruct((rows, width), BF16),
            out(tall // 2, width), out(tall // 2, width), out(short, ff // 2), out(short, ff // 2),
            out(short, width), out(short, width), out(short, width), out(short, width),
            out(8, width), out(1, ff),
        ],
        scratch_shapes=chain(3, tall // 2, width)
        + chain(2, tall // 2, width)
        + [
            pltpu.VMEM((rows, 3 * width), BF16),
            pltpu.VMEM((steps + 1, 8, width), F32),
            pltpu.VMEM((steps, 8, width), F32),
            pltpu.VMEM((steps + 1, 1, ff), F32),
            pltpu.VMEM((steps, 1, ff), F32),
            pltpu.SemaphoreType.DMA((3,)),
            pltpu.SemaphoreType.DMA((copies,)),
            pltpu.SemaphoreType.DMA((copies,)),
        ] + flat + received,
        compiler_params=remote_params(2),
        cost_estimate=cost(40e9, 16 << 20),
        name="tail",
    )(xp, dq, dk, dv, wq, wk, wv, fg, *one, *two, *upa, *upb, *wo, vec, bup)


def write_kernel(
    ndev, parts, ig, dn1, dn2, up1, up2, wo, q, k, v, vec, bup,
    ig_out, dn_out, up_out, wo_out, q_out, k_out, v_out,
    g2_out, s2_out, db_out, g1_out, s1_out, ob_out, qb_out, vb_out, ub_out,
):
    ig_out[...] = ig[...]
    me = lax.axis_index("dp") * parts + lax.axis_index("seq")
    half = dn1.shape[0]
    dn_out[0:half, :] = dn1[...]
    dn_out[half : 2 * half, :] = dn2[...]
    half = up1.shape[1]
    up_out[:, 0:half] = up1[...]
    up_out[:, half : 2 * half] = up2[...]
    wo_out[...] = wo[...]
    q_out[...] = q[...]
    k_out[...] = k[...]
    v_out[...] = v[...]
    width, ff = vec.shape[1], bup.shape[1]
    mine = width // ndev
    mid = pltpu.roll(vec[...], lax.rem(width - me * mine, width), 1)[:, :128]
    for n, ref in enumerate((g2_out, s2_out, db_out, g1_out, s1_out, ob_out, qb_out, vb_out)):
        ref[...] = mid[n, :mine]
    wide = jnp.broadcast_to(bup[...], (8, ff))
    wide = pltpu.roll(wide, lax.rem(ff - me * (ff // ndev), ff), 1)[:, :128]
    ub_out[...] = wide[0, : ff // ndev]


def write(ndev, parts, ig, dn1, dn2, up1, up2, wo, q, k, v, vec, bup):
    width, ff = vec.shape[1], bup.shape[1]

    def out(*shape):
        return jax.ShapeDtypeStruct(shape, F32)

    shapes = [
        jax.ShapeDtypeStruct(ig.shape, BF16),
        out(2 * dn1.shape[0], width), out(up1.shape[0], ff), out(*wo.shape), out(*q.shape),
        out(*k.shape), out(*v.shape),
    ] + [out(width // ndev)] * 8 + [out(ff // ndev)]
    return pl.pallas_call(
        functools.partial(write_kernel, ndev, parts),
        in_specs=[whole()] * 11,
        out_specs=[whole()] * 16,
        out_shape=shapes,
        compiler_params=params(),
        name="write",
    )(ig, dn1, dn2, up1, up2, wo, q, k, v, vec, bup)


def finish(block, ndev):
    rest = ndev >> LEVELS
    if rest == 1:
        return block
    step = 1
    me = lax.axis_index("dp") * lax.axis_size("seq") + lax.axis_index("seq")
    arr = block.reshape(rest, block.shape[0] // rest, block.shape[1])
    flip = rest
    while flip > 1:
        flip //= 2
        bit = (me // flip) % 2
        half = arr.shape[0] // 2
        keep = lax.dynamic_slice_in_dim(arr, bit * half, half, 0)
        send = lax.dynamic_slice_in_dim(arr, (1 - bit) * half, half, 0)
        arr = keep + lax.ppermute(send, AXES, [(i, i ^ flip) for i in range(ndev)])
    return arr[0]


def shards(
    layer_input,
    query_weight,
    query_bias,
    key_weight,
    value_weight,
    value_bias,
    output_weight,
    output_bias,
    first_gain,
    first_shift,
    up_weight,
    up_bias,
    down_weight,
    down_bias,
    second_gain,
    second_shift,
    out_cotangent,
    passage_lengths,
):
    parts = lax.axis_size("seq")
    ndev = parts * lax.axis_size("dp")
    shift = ndev >> LEVELS
    q, k, v, onehot, qmask, bounds, mix, xp = first(
        ndev, parts, layer_input, passage_lengths, query_weight, query_bias, key_weight,
        value_weight, value_bias,
    )
    ctx, lse = attend_forward(bounds, q, k, v, onehot, qmask)
    (
        result, fg, grads, stat, vec, bup, one_keep, one_send, two_keep, two_send, upa_keep,
        upa_send, upb_keep, upb_send, wo_keep, wo_send,
    ) = middle(
        ndev, parts, layer_input, ctx, out_cotangent, output_weight, output_bias, first_gain,
        first_shift, up_weight, up_bias, down_weight, down_bias, second_gain, second_shift, lse, mix,
    )

    def swap(send, bit):
        flip = shift << bit
        return lax.ppermute(send, AXES, [(i, i ^ flip) for i in range(ndev)])

    two = (two_keep, swap(two_send, DN_TWO[1]))
    upa = (upa_keep, swap(upa_send, UP_ONE[1]))
    upb = (upb_keep, swap(upb_send, UP_TWO[1]))
    one = (one_keep, swap(one_send, DN_ONE[2]))
    wo = (wo_keep, swap(wo_send, OUT_ORDER[1]))
    dq, dk, dv = attend_backward(bounds, q, k, v, grads, stat, onehot, qmask)
    sums = tail(
        ndev, parts, xp, dq, dk, dv, query_weight, key_weight, value_weight, fg, one, two, upa,
        upb, wo, vec, bup,
    )
    ig, dn, up, wo, qg, kg, vg, g2g, s2g, db, g1g, s1g, ob, qb, vb, ub = write(ndev, parts, *sums)
    dn, up, wo, qg, kg, vg = (finish(u, ndev) for u in (dn, up, wo, qg, kg, vg))
    return (
        result, ig, qg, qb, kg, vg, vb, wo, ob, g1g, s1g, up, ub, dn, db, g2g, s2g,
    )


def solution(mesh):
    split = P(AXES, None)
    part = P(AXES)
    in_specs = (split,) + (P(),) * 15 + (split, P("dp", None))
    out_specs = (
        split, split, split, part, split, split, part, split, part, part, part,
        split, part, split, part, part, part,
    )
    return jax.shard_map(shards, mesh=mesh, in_specs=in_specs, out_specs=out_specs, check_vma=False)
```

```python
import functools

import jax
import jax.numpy as jnp
from jax import lax
from jax.experimental import pallas as pl
from jax.experimental.pallas import tpu as pltpu
from jax.sharding import PartitionSpec as P

HEAD_DIM = 64
PAIR = 2 * HEAD_DIM
AXES = ("dp", "seq")
NEG = -1e30
FLOOR = -3e38
BQ = 256
BK = 128
LEVELS = 5
layer_eps = 1e-12
F32 = jnp.float32
BF16 = jnp.bfloat16


def nn(a, b):
    return lax.dot_general(a, b, (((1,), (0,)), ((), ())), preferred_element_type=F32)


def nt(a, b):
    return lax.dot_general(a, b, (((1,), (1,)), ((), ())), preferred_element_type=F32)


def tn(a, b):
    return lax.dot_general(a, b, (((0,), (0,)), ((), ())), preferred_element_type=F32)


def cost(flops, nbytes, trans=0):
    return pl.CostEstimate(flops=int(flops), bytes_accessed=int(nbytes), transcendentals=int(trans))


def params(limit=56 << 20):
    return pltpu.CompilerParams(vmem_limit_bytes=limit)


def whole():
    return pl.BlockSpec(memory_space=pltpu.VMEM)


def hbm():
    return pl.BlockSpec(memory_space=pl.ANY)


def low_lanes():
    return lax.broadcasted_iota(jnp.int32, (1, PAIR), 1) < HEAD_DIM


def line(ref):
    return ref[...].reshape(1, -1)


def remote_params(number, mib):
    return pltpu.CompilerParams(
        vmem_limit_bytes=mib << 20, collective_id=number, has_side_effects=True
    )


class Links:
    def __init__(self, ndev, parts, send_sems, recv_sems):
        self.ndev, self.parts = ndev, parts
        self.place = lax.axis_index("seq")
        self.row = lax.axis_index("dp")
        self.me = self.row * parts + self.place
        self.shift = ndev >> LEVELS
        self.block = self.me // self.shift
        self.send_sems, self.recv_sems = send_sems, recv_sems
        self.used = 0
        self.started = []
        self.has_prev = self.place > 0
        self.has_next = self.place < parts - 1

    def partner(self, *flips):
        other = self.me
        for flip in flips:
            other = other + (1 - 2 * ((self.me // flip) % 2)) * flip
        return (other // self.parts, other % self.parts)

    def greet(self, flips, neighbours):
        barrier = pltpu.get_barrier_semaphore()

        def signal(device):
            pl.semaphore_signal(
                barrier, inc=1, device_id=device, device_id_type=pl.DeviceIdType.MESH
            )

        for flip in flips:
            signal(self.partner(*(flip if isinstance(flip, tuple) else (flip,))))
        if neighbours:

            @pl.when(self.has_prev)
            def _():
                signal((self.row, self.place - 1))

            @pl.when(self.has_next)
            def _():
                signal((self.row, self.place + 1))

        count = len(flips)
        if neighbours:
            count = count + jnp.minimum(self.place, 1)
            count = count + jnp.minimum(self.parts - 1 - self.place, 1)
        pl.semaphore_wait(barrier, count)

    def make(self, src, dst, device):
        n = self.used
        self.used += 1
        return pltpu.make_async_remote_copy(
            src_ref=src, dst_ref=dst, send_sem=self.send_sems.at[n],
            recv_sem=self.recv_sems.at[n], device_id=device,
            device_id_type=pl.DeviceIdType.MESH,
        )

    def exchange(self, src, dst, *flips):
        copy = self.make(src, dst, self.partner(*flips))
        copy.start()
        self.started.append(copy)
        return copy

    def finish(self):
        for copy in self.started:
            copy.wait_send()

    def neighbours(self, src, at_next, at_prev):
        ahead = self.make(src, at_next, (self.row, self.place + 1))
        back = self.make(src, at_prev, (self.row, self.place - 1))

        @pl.when(self.has_next)
        def _():
            ahead.start()

        @pl.when(self.has_prev)
        def _():
            back.start()

        return ahead, back

    def from_prev(self, pair):
        @pl.when(self.has_prev)
        def _():
            pair[0].wait_recv()

    def from_next(self, pair):
        @pl.when(self.has_next)
        def _():
            pair[1].wait_recv()

    def sent(self, pair):
        @pl.when(self.has_next)
        def _():
            pair[0].wait_send()

        @pl.when(self.has_prev)
        def _():
            pair[1].wait_send()


def both(a, b):
    return (a.astype(F32) + b.astype(F32)).astype(BF16)


class Chain:
    def __init__(self, links, buf, recv, order, step):
        self.links, self.buf, self.recv, self.order, self.step = links, buf, recv, order, step
        self.base = 0

    def position(self, c):
        at = 0
        for k, b in enumerate(self.order):
            mine, its = (self.links.block // (1 << b)) % 2, (c // (1 << b)) % 2
            at = at + (mine + its - 2 * mine * its) * (1 << (LEVELS - 1 - k))
        return at

    def send(self):
        self.half = (1 << LEVELS) >> (self.step + 1)
        self.copy = self.links.exchange(
            self.buf.at[pl.ds(self.half, self.half)],
            self.recv.at[pl.ds(self.base, self.half)],
            self.links.shift << self.order[self.step],
        )

    def receive(self):
        self.copy.wait_recv()
        self.base += self.half
        self.step += 1

    def add(self):
        base, half, buf, recv = self.base, self.half, self.buf, self.recv
        self.receive()
        if half > 1:

            @pl.loop(0, half)
            def _(i):
                buf[i] = both(buf[i], recv[base + i])

            self.send()

    def last(self):
        return self.buf[0].astype(F32) + self.recv[self.base - 1].astype(F32)


class Flat:
    def __init__(self, links, buf, recvs, bits, order, step, cols=None):
        self.links, self.buf, self.recvs = links, buf, list(recvs)
        self.bits, self.order, self.step = bits, order, step
        self.at = [slice(None)] * len(bits)
        self.rows = buf.shape[len(bits)]
        self.cols = slice(None) if cols is None else cols

    def view(self, lead, start, size):
        index = tuple(i if isinstance(i, int) else slice(None) for i in lead)
        return self.buf.at[index + (pl.ds(start, size), self.cols)]

    def send(self):
        bit = self.order[self.step]
        shift = self.links.shift
        self.recv = self.recvs.pop(0)
        if isinstance(bit, tuple):
            self.rows //= 4
            self.copies = [
                self.links.exchange(
                    self.view(self.at, n * self.rows, self.rows),
                    self.recv.at[n - 1],
                    *(shift << b for k, b in enumerate(bit) if (n >> (1 - k)) & 1),
                )
                for n in (1, 2, 3)
            ]
            return
        if bit in self.bits:
            lead = list(self.at)
            lead[self.bits.index(bit)] = 1
            src = self.view(lead, 0, self.rows)
            self.at[self.bits.index(bit)] = 0
        else:
            self.rows //= 2
            src = self.view(self.at, self.rows, self.rows)
        self.copies = [self.links.exchange(src, self.recv, shift << bit)]

    def add(self):
        for copy in self.copies:
            copy.wait_recv()
        self.step += 1
        if self.step == len(self.order):
            return
        leads = [()]
        for i in self.at:
            leads = [a + (b,) for a in leads for b in ((0, 1) if i != 0 else (0,))]
        free = [n for n, i in enumerate(self.at) if i != 0]
        buf, recv, cols = self.buf, self.recv, self.cols

        @pl.loop(0, self.rows // 16)
        def _(i):
            at = pl.ds(pl.multiple_of(i * 16, 16), 16)
            for lead in leads:
                from_ = tuple(lead[n] for n in free)
                to = lead + (at, cols)
                buf[to] = both(buf[to], recv[from_ + (at,)])

        self.send()

    def last(self):
        lead = (0,) * len(self.bits)
        total = self.buf[lead + (slice(0, self.rows), self.cols)].astype(F32)
        if isinstance(self.order[-1], tuple):
            for n in range(3):
                total = total + self.recv[n].astype(F32)
            return total
        return total + self.recv[...].astype(F32)


def flat_recvs(bits, order, step, cols, blocks_rows):
    lead, rows = len(bits), blocks_rows
    shapes = []
    for bit in order[step:]:
        if isinstance(bit, tuple):
            shapes.append((3, rows // 4, cols))
            continue
        if bit in bits:
            lead -= 1
        else:
            rows //= 2
        shapes.append((2,) * lead + (rows, cols))
    return shapes


def shuffle(links, width):
    short = width // BLOCKS
    col = lax.broadcasted_iota(jnp.int32, (8, width), 1)
    source = col
    for p in range(BLOCKS):
        c = 0
        for k, b in enumerate(FLAT):
            mine, its = (links.block // (1 << b)) % 2, (p >> (LEVELS - 1 - k)) & 1
            c = c + (mine + its - 2 * mine * its) * (1 << b)
        source = jnp.where(col >= p * short, col + (c - p) * short, source)
    row = lax.broadcasted_iota(jnp.int32, (width, width), 0)
    return (row == source[0:1]).astype(F32).astype(BF16)


FLAT = (0, 2, 1, 3, 4)
DN_ONE = (0, 2, 1, 3, 4)
DN_TWO = (0, 1, 2, 3, 4)
UP_ONE = (0, 2, 1, 3, 4)
UP_TWO = (0, 3, 2, 1, 4)
OUT_ORDER = (0, 2, 1, 3, 4)
LEFT_ORDER = (0, 2, 1, (3, 4))
RIGHT_ORDER = (0, 1, 2, (3, 4))
BLOCKS = 1 << LEVELS


def first_kernel(
    ndev, parts, x_ref, lengths, wq_hbm, bq, wk_hbm, wv_hbm, bv,
    q_hbm, k_hbm, v_hbm, onehot, qmask, bounds, mix, xp,
    halo, wq, wk, wv, q_ref, k_ref, v_ref, load_sems, store_sems, send_sems, recv_sems,
):
    rows, width = x_ref.shape
    count = rows * parts
    loads = [
        pltpu.make_async_copy(src, dst, load_sems.at[n])
        for n, (src, dst) in enumerate(((wq_hbm, wq), (wk_hbm, wk), (wv_hbm, wv)))
    ]
    for load in loads:
        load.start()
    links = Links(ndev, parts, send_sems, recv_sems)
    links.greet([], True)
    step = rows // 2
    pairs = [
        links.neighbours(
            x_ref.at[pl.ds(h * step, step)],
            halo.at[pl.ds(h * step, step)],
            halo.at[pl.ds(2 * rows + h * step, step)],
        )
        for h in range(2)
    ]

    @pl.when(jnp.logical_not(links.has_prev))
    def _():
        halo[0:rows, :] = jnp.zeros((rows, width), BF16)

    @pl.when(jnp.logical_not(links.has_next))
    def _():
        halo[2 * rows : 3 * rows, :] = jnp.zeros((rows, width), BF16)

    halo[rows : 2 * rows, :] = x_ref[...]

    for load in loads:
        load.wait()

    def stores(at, n):
        part = pl.ds(at, step)
        return [
            pltpu.make_async_copy(src.at[part], dst.at[part], store_sems.at[n, m])
            for m, (src, dst) in enumerate(((q_ref, q_hbm), (k_ref, k_hbm), (v_ref, v_hbm)))
        ]

    def chunk(t):
        return jnp.where(t < 2, 2 + t, (t % 2) * 4 + t // 2 - 1)

    def project(t):
        at = pl.multiple_of(chunk(t) * step, step)
        rows_at = pl.ds(at, step)
        x = halo[rows_at, :]
        q_ref[rows_at, :] = (nn(x, wq[...]) + line(bq)).astype(BF16)
        k_ref[rows_at, :] = nn(x, wk[...]).astype(BF16)
        v_ref[rows_at, :] = (nn(x, wv[...]) + line(bv)).astype(BF16)
        for copy in stores(at, t):
            copy.start()

    pl.loop(0, 2)(project)

    slots = lengths.shape[1]
    ends, total = [], jnp.int32(0)
    for n in range(slots):
        total = total + lengths[0, n]
        ends.append(total)
    start = (links.place - 1) * rows
    lane = lax.broadcasted_iota(jnp.int32, (BQ, PAIR), 1) % HEAD_DIM
    one, none, far = BF16(1.0), BF16(0.0), BF16(NEG)

    @pl.loop(0, 3 * rows // BQ)
    def _(i):
        at = start + i * BQ
        where = at + lax.broadcasted_iota(jnp.int32, (BQ, PAIR), 0)
        seg = jnp.zeros((BQ, PAIR), jnp.int32)
        for end in ends:
            seg = seg + (where >= end).astype(jnp.int32)
        outside = (where < 0) | (where >= count)
        seg = jnp.where(outside, slots, seg)
        match = (seg == lane).astype(F32)
        to = pl.ds(pl.multiple_of(i * BQ, BQ), BQ)
        onehot[to, :] = match.astype(BF16)
        qmask[to, :] = ((1.0 - match) * NEG).astype(BF16)

    mix[...] = shuffle(links, width)
    xp[...] = nn(x_ref[...], mix[...]).astype(BF16)

    for n in range(rows // BQ):
        near = links.place * rows + n * BQ
        far_row = near + BQ - 1
        lo, hi = jnp.int32(0), jnp.int32(count)
        for end in ends:
            lo = jnp.where(end <= near, jnp.maximum(lo, end), lo)
            hi = jnp.where(end > far_row, jnp.minimum(hi, end), hi)
        lo = jnp.maximum(lo - start, 0)
        hi = jnp.minimum(hi - start, 3 * rows)
        bounds[0, n] = lo // BK
        bounds[1, n] = (hi + BK - 1) // BK

    @pl.loop(2, 6)
    def _(t):
        for h in range(2):

            @pl.when(t == 2 + 2 * h)
            def _():
                links.from_prev(pairs[h])

            @pl.when(t == 3 + 2 * h)
            def _():
                links.from_next(pairs[h])

        project(t)

    for pair in pairs:
        links.sent(pair)

    @pl.loop(0, 6)
    def _(t):
        for copy in stores(pl.multiple_of(chunk(t) * step, step), t):
            copy.wait()


def first(ndev, parts, x, lengths, wq, bq, wk, wv, bv):
    rows, width = x.shape
    ext = jax.ShapeDtypeStruct((3 * rows, width), BF16)
    seg = jax.ShapeDtypeStruct((3 * rows, PAIR), BF16)
    smem = pl.BlockSpec(memory_space=pltpu.SMEM)
    return pl.pallas_call(
        functools.partial(first_kernel, ndev, parts),
        in_specs=[whole(), smem, hbm(), whole(), hbm(), hbm(), whole()],
        out_specs=[hbm()] * 3 + [whole()] * 2 + [smem] + [whole()] * 2,
        out_shape=[ext] * 3
        + [seg] * 2
        + [
            jax.ShapeDtypeStruct((2, rows // BQ), jnp.int32),
            jax.ShapeDtypeStruct((width, width), BF16),
            jax.ShapeDtypeStruct((rows, width), BF16),
        ],
        scratch_shapes=[
            pltpu.VMEM((3 * rows, width), BF16),
            pltpu.VMEM((width, width), BF16),
            pltpu.VMEM((width, width), BF16),
            pltpu.VMEM((width, width), BF16),
            pltpu.VMEM((3 * rows, width), BF16),
            pltpu.VMEM((3 * rows, width), BF16),
            pltpu.VMEM((3 * rows, width), BF16),
            pltpu.SemaphoreType.DMA((3,)),
            pltpu.SemaphoreType.DMA((6, 3)),
            pltpu.SemaphoreType.DMA((4,)),
            pltpu.SemaphoreType.DMA((4,)),
        ],
        compiler_params=remote_params(0, 26),
        cost_estimate=cost(15e9, 12 << 20),
        name="first",
    )(x, lengths, wq, bq, wk, wv, bv)


def lengths_of(rows):
    most = BQ // BK + 2 * -(-(rows - 1) // BK)
    return [n for n in range(3, most) if n <= 6 or n % 2 == 0] + [most]


def key_range(bounds, i, rows):
    lo, hi = bounds[0, i], bounds[1, i]
    sizes = lengths_of(rows)
    number = jnp.int32(sizes[-1])
    for n in reversed(sizes):
        number = jnp.where(hi - lo <= n, n, number)
    return jnp.minimum(lo, 3 * rows // BK - number), number


def forward_kernel(bounds, q_ref, k_ref, v_ref, onehot, qmask, ctx_ref, lse_ref, ka, kb):
    rows = ctx_ref.shape[0]
    low = low_lanes()
    key, hot = k_ref[...], onehot[...]
    ka[...] = jnp.where(low, key, hot)
    kb[...] = jnp.where(low, hot, key)

    @pl.loop(0, rows // BQ)
    def _(i):
        first_block, number = key_range(bounds, i, rows)
        base = pl.multiple_of(first_block * BK, BK)
        at = pl.ds(pl.multiple_of(i * BQ, BQ), BQ)
        own = pl.ds(pl.multiple_of(rows + i * BQ, BQ), BQ)
        for num in lengths_of(rows):

            @pl.when(number == num)
            def _():
                span = pl.ds(base, num * BK)
                query = q_ref[own, :] * BF16(HEAD_DIM**-0.5)
                mask = qmask[own, :]
                parts = []
                for head, keys in enumerate((ka, kb)):
                    pick = (query, mask) if head == 0 else (mask, query)
                    scores = nt(jnp.where(low, *pick), keys[span, :])
                    top = jnp.max(scores, axis=1, keepdims=True)
                    weights = jnp.exp(scores - top)
                    total = jnp.sum(weights, axis=1, keepdims=True)
                    acc = nn(weights.astype(BF16), v_ref[span, :])
                    parts.append((acc / total, top + jnp.log(total)))
                ctx_ref[at, :] = jnp.where(low, parts[0][0], parts[1][0])
                flip = jnp.where(low, parts[0][1], parts[1][1]).T
                lse_ref[0, 0:1, at] = flip[0:1]
                lse_ref[0, 1:2, at] = flip[HEAD_DIM : HEAD_DIM + 1]


def attend_forward(bounds, q, k, v, onehot, qmask):
    rows, width = q.shape[0] // 3, q.shape[1]
    pairs = width // PAIR
    ext = pl.BlockSpec((3 * rows, PAIR), lambda p, *_: (0, p))
    seg = pl.BlockSpec((3 * rows, PAIR), lambda p, *_: (0, 0))
    grid = pltpu.PrefetchScalarGridSpec(
        num_scalar_prefetch=1,
        grid=(pairs,),
        in_specs=[ext, ext, ext, seg, seg],
        out_specs=[
            pl.BlockSpec((rows, PAIR), lambda p, *_: (0, p)),
            pl.BlockSpec((1, 2, rows), lambda p, *_: (p, 0, 0)),
        ],
        scratch_shapes=[pltpu.VMEM((3 * rows, PAIR), BF16)] * 2,
    )
    return pl.pallas_call(
        forward_kernel,
        grid_spec=grid,
        out_shape=[
            jax.ShapeDtypeStruct((rows, width), F32),
            jax.ShapeDtypeStruct((pairs, 2, rows), F32),
        ],
        compiler_params=params(16 << 20),
        cost_estimate=cost(20e9, 24 * rows * width),
        name="attend_forward",
    )(bounds, q, k, v, onehot, qmask)


def backward_kernel(
    bounds, q_ref, k_ref, v_ref, g_ref, stat_ref, onehot, qmask,
    dq_ref, dk_ref, dv_ref, ka, kb, qa, qb, qs,
):
    rows = dq_ref.shape[0]
    low = low_lanes()
    zero = jnp.zeros((1, PAIR), BF16)
    scale = BF16(HEAD_DIM**-0.5)
    key, hot = k_ref[...], onehot[...]
    ka[...] = jnp.where(low, key, hot)
    kb[...] = jnp.where(low, hot, key)
    query, mask = q_ref[...] * scale, qmask[...]
    qa[...] = jnp.where(low, query, mask)
    qb[...] = jnp.where(low, mask, query)
    qs[...] = query

    @pl.loop(0, rows // BQ)
    def _(i):
        first_block, number = key_range(bounds, i, rows)
        base = pl.multiple_of(first_block * BK, BK)
        at = pl.ds(pl.multiple_of(i * BQ, BQ), BQ)
        own = pl.ds(pl.multiple_of(rows + i * BQ, BQ), BQ)
        for num in lengths_of(rows):

            @pl.when(number == num)
            def _():
                span = pl.ds(base, num * BK)

                def pick(head, value, other):
                    return jnp.where(low, value, other) if head == 0 else jnp.where(
                        low, other, value
                    )

                columns = stat_ref[0, :, own]
                columns = jnp.concatenate([columns, columns], axis=0).T
                out = []
                for head, keys in enumerate((ka, kb)):
                    queries = (qa, qb)[head][own, :]
                    grads = pick(head, g_ref[own, :], zero)
                    scores = nt(queries, keys[span, :])
                    prob_grad = nt(grads, v_ref[span, :])
                    probs = jnp.exp(scores - columns[:, head : head + 1])
                    delta = columns[:, 2 + head : 3 + head]
                    score_grad = (probs * (prob_grad - delta)).astype(BF16)
                    out.append(nn(score_grad, k_ref[span, :]))
                dq = jnp.where(low, out[0], out[1]) * F32(HEAD_DIM**-0.5)
                dq_ref[at, :] = dq.astype(BF16)
                out = []
                for head, queries in enumerate((qa, qb)):
                    keys = (ka, kb)[head][own, :]
                    vals = pick(head, v_ref[own, :], zero)
                    scores = nt(keys, queries[span, :])
                    prob_grad = nt(vals, g_ref[span, :])
                    probs = jnp.exp(scores - stat_ref[0, head : head + 1, span])
                    delta = stat_ref[0, 2 + head : 3 + head, span]
                    score_grad = (probs * (prob_grad - delta)).astype(BF16)
                    out.append((
                        nn(score_grad, qs[span, :]),
                        nn(probs.astype(BF16), g_ref[span, :]),
                    ))
                dk_ref[at, :] = jnp.where(low, out[0][0], out[1][0]).astype(BF16)
                dv_ref[at, :] = jnp.where(low, out[0][1], out[1][1]).astype(BF16)


def attend_backward(bounds, q, k, v, g, stat, onehot, qmask):
    rows, width = q.shape[0] // 3, q.shape[1]
    pairs = width // PAIR
    ext = pl.BlockSpec((3 * rows, PAIR), lambda p, *_: (0, p))
    own = pl.BlockSpec((rows, PAIR), lambda p, *_: (0, p))
    seg = pl.BlockSpec((3 * rows, PAIR), lambda p, *_: (0, 0))
    grid = pltpu.PrefetchScalarGridSpec(
        num_scalar_prefetch=1,
        grid=(pairs,),
        in_specs=[ext] * 4 + [pl.BlockSpec((1, 4, 3 * rows), lambda p, *_: (p, 0, 0)), seg, seg],
        out_specs=[own] * 3,
        scratch_shapes=[pltpu.VMEM((3 * rows, PAIR), BF16)] * 5,
    )
    return pl.pallas_call(
        backward_kernel,
        grid_spec=grid,
        out_shape=[jax.ShapeDtypeStruct((rows, width), BF16)] * 3,
        compiler_params=params(24 << 20),
        cost_estimate=cost(40e9, 40 * rows * width),
        name="attend_backward",
    )(bounds, q, k, v, g, stat, onehot, qmask)


def norm_forward(h):
    mean = jnp.mean(h, axis=-1, keepdims=True)
    centred = h - mean
    variance = jnp.mean(centred * centred, axis=-1, keepdims=True)
    inverse = lax.rsqrt(variance + layer_eps)
    return centred * inverse, inverse


def norm_backward(grad, gain, hat, inverse):
    g = grad * gain
    return inverse * (
        g - jnp.mean(g, axis=-1, keepdims=True) - hat * jnp.mean(g * hat, axis=-1, keepdims=True)
    )


def colsum(v):
    return jnp.sum(v, axis=0, keepdims=True)


def middle_kernel(
    ndev, parts,
    x_ref, ctx_ref, ct_ref, wo, bo, g1, s1, wup_hbm, bup, wdn_hbm, bdn, g2, s2, lse_ref, mix,
    result_hbm, fg_hbm, g_hbm, stat_ref, vec_ref, bup_ref,
    one_keep_hbm, one_send_hbm, two_keep_hbm, two_send_hbm, upa_keep_hbm, upa_send_hbm, upb_keep_hbm,
    upb_send_hbm, wo_keep_hbm, wo_send_hbm,
    wup, wdn, hid, nl, nlp, bg, cl, ag, slope, normed, inv, acc, grad_s,
    result_ref, fg_ref, g_ref,
    one_s, one_r, two_s, two_r, up_s, up_r, wo_s, wo_r,
    load_sems, store_sems, send_sems, recv_sems,
):
    stores = []

    def store(src, dst):
        copy = pltpu.make_async_copy(src, dst, store_sems.at[len(stores)])
        copy.start()
        stores.append(copy)

    rows, width = x_ref.shape
    ff = wup.shape[1]
    rc, fc = 256, 1024
    chunks, tiles = rows // rc, ff // fc
    tall, short = ff // BLOCKS, width // BLOCKS
    up_copy = pltpu.make_async_copy(wup_hbm, wup, load_sems.at[0])
    dn_copy = pltpu.make_async_copy(wdn_hbm, wdn, load_sems.at[1])
    up_copy.start()
    dn_copy.start()
    links = Links(ndev, parts, send_sems, recv_sems)
    links.greet([links.shift << DN_ONE[0], links.shift << DN_ONE[1]], True)
    one = Chain(links, one_s, one_r, DN_ONE, 0)
    two = Chain(links, two_s, two_r, DN_TWO, 0)
    @pl.loop(0, chunks)
    def _(r):
        at = pl.ds(pl.multiple_of(r * rc, rc), rc)
        c_low = ctx_ref[at, :].astype(BF16)
        cl[at, :] = nn(c_low, mix[...]).astype(BF16)
        h = x_ref[at, :].astype(F32) + (nn(c_low, wo[...]) + line(bo))
        xhat, inverse = norm_forward(h)
        res = xhat * line(g1) + line(s1)
        fg_ref[at, :] = xhat
        inv[at, :] = inverse
        normed[at, :] = res
        low = res.astype(BF16)
        nl[at, :] = low
        nlp[at, :] = nn(low, mix[...]).astype(BF16)

    up_copy.wait()
    dn_copy.wait()
    acc[...] = jnp.zeros_like(acc)

    @pl.loop(0, tiles)
    def _(j):
        cols = pl.ds(pl.multiple_of(j * fc, fc), fc)
        bias = bup[cols].reshape(1, fc)

        @pl.loop(0, chunks)
        def _(r):
            at = pl.ds(pl.multiple_of(r * rc, rc), rc)
            up = nn(nl[at, :], wup[:, cols]) + bias
            cdf = 0.5 * (1.0 + lax.erf(up * F32(0.5**0.5)))
            density = jnp.exp(-0.5 * up * up) * F32(0.3989422804014327)
            slope[at, cols] = cdf + up * density
            act = (up * cdf).astype(BF16)
            hid[at, cols] = act
            acc[at, :] = acc[at, :] + nn(act, wdn[cols, :])

    vec_ref[...] = jnp.zeros_like(vec_ref)

    @pl.loop(0, chunks)
    def _(r):
        at = pl.ds(pl.multiple_of(r * rc, rc), rc)
        xhat, inverse = norm_forward(normed[at, :] + (acc[at, :] + line(bdn)))
        result_ref[at, :] = (xhat * line(g2) + line(s2)).astype(BF16)
        ct = ct_ref[at, :].astype(F32)
        second = norm_backward(ct, line(g2), xhat, inverse)
        low = second.astype(BF16)
        bg[at, :] = low
        acc[at, :] = second
        vec_ref[0:1, :] = vec_ref[0:1, :] + colsum(ct * xhat)
        vec_ref[1:2, :] = vec_ref[1:2, :] + colsum(ct)
        vec_ref[2:3, :] = vec_ref[2:3, :] + colsum(low.astype(F32))

    store(result_ref, result_hbm)

    some = width // tall

    @pl.loop(0, ff // width)
    def _(j):
        grad_s[...] = tn(hid[:, pl.ds(pl.multiple_of(j * width, width), width)], bg[...])

        @pl.loop(0, some)
        def _(c):
            base = pl.multiple_of(c * tall, tall // 2)
            one_s[one.position(j * some + c)] = grad_s[pl.ds(base, tall // 2), :].astype(BF16)
            base = pl.multiple_of(c * tall + tall // 2, tall // 2)
            two_s[two.position(j * some + c)] = grad_s[pl.ds(base, tall // 2), :].astype(BF16)

    one.send()
    two.send()

    def back_tiles(lo, hi):
        @pl.loop(lo, hi)
        def _(j):
            cols = pl.ds(pl.multiple_of(j * fc, fc), fc)
            bup_ref[:, cols] = jnp.zeros((1, fc), F32)

            @pl.loop(0, chunks)
            def _(r):
                at = pl.ds(pl.multiple_of(r * rc, rc), rc)
                grad = (nt(bg[at, :], wdn[cols, :]) * slope[at, cols]).astype(BF16)
                hid[at, cols] = grad
                bup_ref[:, cols] = bup_ref[:, cols] + colsum(grad.astype(F32))
                acc[at, :] = acc[at, :] + nt(grad, wup[:, cols])

    back_tiles(0, tiles - 1)
    one.add()
    back_tiles(tiles - 1, tiles)

    zero_prev = pltpu.make_async_copy(
        result_ref, g_hbm.at[pl.ds(0, rows)], store_sems.at[store_sems.shape[0] - 2]
    )
    zero_next = pltpu.make_async_copy(
        result_ref, g_hbm.at[pl.ds(2 * rows, rows)], store_sems.at[store_sems.shape[0] - 1]
    )
    stores.pop().wait()
    result_ref[...] = jnp.zeros_like(result_ref)

    @pl.when(jnp.logical_not(links.has_prev))
    def _():
        zero_prev.start()
        stat_ref[:, :, 0:rows] = jnp.zeros((width // PAIR, 4, rows), F32)

    @pl.when(jnp.logical_not(links.has_next))
    def _():
        zero_next.start()
        stat_ref[:, :, 2 * rows : 3 * rows] = jnp.zeros((width // PAIR, 4, rows), F32)

    pairs = []
    for r in range(chunks):
        at = slice(r * rc, (r + 1) * rc)
        mid = slice(rows + r * rc, rows + (r + 1) * rc)
        total = acc[at, :]
        xhat = fg_ref[at, :]
        first_grad = norm_backward(total, line(g1), xhat, inv[at, :])
        fg_ref[at, :] = first_grad
        low = first_grad.astype(BF16)
        ag[at, :] = low
        vec_ref[3:4, :] = vec_ref[3:4, :] + colsum(total * xhat)
        vec_ref[4:5, :] = vec_ref[4:5, :] + colsum(total)
        vec_ref[5:6, :] = vec_ref[5:6, :] + colsum(low.astype(F32))
        cg = nt(low, wo[...]).astype(BF16)
        g_ref[at, :] = cg
        pairs.append(links.neighbours(
            g_ref.at[pl.ds(r * rc, rc)],
            g_hbm.at[pl.ds(r * rc, rc)],
            g_hbm.at[pl.ds(2 * rows + r * rc, rc)],
        ))
        prod = cg.astype(F32) * ctx_ref[at, :]
        for p in range(width // PAIR):
            flip = prod[:, p * PAIR : (p + 1) * PAIR].T
            stat_ref[p, 2:3, mid] = colsum(flip[:HEAD_DIM])
            stat_ref[p, 3:4, mid] = colsum(flip[HEAD_DIM:])
    store(g_ref, g_hbm.at[pl.ds(rows, rows)])
    store(fg_ref, fg_hbm)
    for p in range(width // PAIR):
        stat_ref[p, 0:2, rows : 2 * rows] = lse_ref[p]
    pairs.append(links.neighbours(
        stat_ref.at[:, :, pl.ds(rows, rows)],
        stat_ref.at[:, :, pl.ds(0, rows)],
        stat_ref.at[:, :, pl.ds(2 * rows, rows)],
    ))

    quarter = width // 8
    ups = []
    for n in range(2):

        @pl.loop(0, 2)
        def _(t):
            cols = pl.ds(pl.multiple_of(n * (ff // 2) + t * width, width), width)
            grad = tn(nlp[...], hid[:, cols])
            up_s[:, :, :, :, cols] = grad.astype(BF16).reshape(2, 2, 2, quarter, width)

        cols = pl.ds(n * (ff // 2), ff // 2)
        ups.append(links.exchange(
            up_s.at[1, :, :, :, cols], up_r.at[:, :, :, cols], links.shift << FLAT[0]
        ))

    wo_s[...] = tn(cl[...], ag[...]).astype(BF16).reshape(2, 2, 2, quarter, width)
    out = links.exchange(wo_s.at[1], wo_r, links.shift << FLAT[0])

    def settle(chain, keep, send):
        chain.receive()
        half, quarter = BLOCKS // 2, BLOCKS // 4

        @pl.loop(0, half)
        def _(i):
            chain.recv[i] = both(chain.buf[i], chain.recv[i])

        store(chain.recv.at[pl.ds(0, quarter)], keep)
        store(chain.recv.at[pl.ds(quarter, quarter)], send)

    settle(two, two_keep_hbm, two_send_hbm)

    def settle_flat(copy, mine, got, cols):
        copy.wait_recv()

        @pl.loop(0, quarter // 16)
        def _(i):
            at = pl.ds(pl.multiple_of(i * 16, 16), 16)
            for x_bit in range(2):
                for y_bit in range(2):
                    index = (x_bit, y_bit, at, cols)
                    got[index] = both(mine[(0,) + index], got[index])

    left, right = pl.ds(0, ff // 2), pl.ds(ff // 2, ff // 2)
    settle_flat(ups[0], up_s, up_r, left)
    store(up_r.at[0, :, :, left], upa_keep_hbm)
    store(up_r.at[1, :, :, left], upa_send_hbm)
    settle_flat(ups[1], up_s, up_r, right)
    store(up_r.at[:, :, pl.ds(0, quarter // 2), right], upb_keep_hbm)
    store(up_r.at[:, :, pl.ds(quarter // 2, quarter // 2), right], upb_send_hbm)
    settle_flat(out, wo_s, wo_r, slice(None))
    store(wo_r.at[0], wo_keep_hbm)
    store(wo_r.at[1], wo_send_hbm)
    one.receive()

    @pl.loop(0, BLOCKS // 4)
    def _(i):
        one_s[i] = both(one_s[i], one_r[BLOCKS // 2 + i])

    store(one_s.at[pl.ds(0, BLOCKS // 8)], one_keep_hbm)
    store(one_s.at[pl.ds(BLOCKS // 8, BLOCKS // 8)], one_send_hbm)
    for copy in stores:
        copy.wait()

    @pl.when(jnp.logical_not(links.has_prev))
    def _():
        zero_prev.wait()

    @pl.when(jnp.logical_not(links.has_next))
    def _():
        zero_next.wait()

    for pair in pairs:
        links.from_prev(pair)
        links.from_next(pair)
        links.sent(pair)
    links.finish()


def middle(ndev, parts, x, ctx, ct, wo, bo, g1, s1, wup, bup, wdn, bdn, g2, s2, lse, mix):
    rows, width = x.shape
    ff = wup.shape[1]
    pairs = width // PAIR
    tall, short = ff // BLOCKS, width // BLOCKS
    left = BLOCKS // 4

    def out(*shape, dtype=BF16):
        return jax.ShapeDtypeStruct(shape, dtype)

    shapes = [
        out(rows, width),
        out(rows, width, dtype=F32),
        out(3 * rows, width),
        out(pairs, 4, 3 * rows, dtype=F32),
        out(8, width, dtype=F32),
        out(1, ff, dtype=F32),
        out(left // 2, tall // 2, width),
        out(left // 2, tall // 2, width),
        out(left, tall // 2, width),
        out(left, tall // 2, width),
        out(2, width // 8, ff // 2),
        out(2, width // 8, ff // 2),
        out(2, 2, width // 16, ff // 2),
        out(2, 2, width // 16, ff // 2),
        out(2, width // 8, width),
        out(2, width // 8, width),
    ]

    def chain(*shape):
        return [pltpu.VMEM((BLOCKS,) + shape, BF16), pltpu.VMEM((BLOCKS // 2,) + shape, BF16)]

    dn_one = chain(tall // 2, width)
    dn_one[1] = pltpu.VMEM((3 * BLOCKS // 4, tall // 2, width), BF16)
    copies = 6 + 6
    return pl.pallas_call(
        functools.partial(middle_kernel, ndev, parts),
        in_specs=[whole()] * 7 + [hbm(), whole(), hbm()] + [whole()] * 5,
        out_specs=[hbm()] * 3 + [whole()] * 3 + [hbm()] * 10,
        out_shape=shapes,
        scratch_shapes=[
            pltpu.VMEM((width, ff), BF16),
            pltpu.VMEM((ff, width), BF16),
            pltpu.VMEM((rows, ff), BF16),
            pltpu.VMEM((rows, width), BF16),
            pltpu.VMEM((rows, width), BF16),
            pltpu.VMEM((rows, width), BF16),
            pltpu.VMEM((rows, width), BF16),
            pltpu.VMEM((rows, width), BF16),
            pltpu.VMEM((rows, ff), F32),
            pltpu.VMEM((rows, width), F32),
            pltpu.VMEM((rows, 1), F32),
            pltpu.VMEM((rows, width), F32),
            pltpu.VMEM((width, width), F32),
            pltpu.VMEM((rows, width), BF16),
            pltpu.VMEM((rows, width), F32),
            pltpu.VMEM((rows, width), BF16),
        ]
        + dn_one + chain(tall // 2, width)
        + [
            pltpu.VMEM((2, 2, 2, width // 8, ff), BF16),
            pltpu.VMEM((2, 2, width // 8, ff), BF16),
            pltpu.VMEM((2, 2, 2, width // 8, width), BF16),
            pltpu.VMEM((2, 2, width // 8, width), BF16),
        ]
        + [
            pltpu.SemaphoreType.DMA((2,)),
            pltpu.SemaphoreType.DMA((15,)),
            pltpu.SemaphoreType.DMA((copies,)),
            pltpu.SemaphoreType.DMA((copies,)),
        ],
        compiler_params=remote_params(1, 60),
        cost_estimate=cost(50e9, 30 << 20),
        name="middle",
    )(x, ctx, ct, wo, bo, g1, s1, wup, bup, wdn, bdn, g2, s2, lse, mix)


def tail_kernel(
    ndev, parts,
    xp, dq_hbm, dk_hbm, dv_hbm, wq, wk, wv, fg, one_keep, one_got, two_keep, two_got,
    upa_keep, upa_got, upb_keep, upb_got, wo_keep, wo_got, vec, bup,
    ig_ref, dn1_out, dn2_out, up1_out, up2_out, wo_out, q_out, k_out, v_out, vec_out, bup_out,
    one_s, one_r, two_s, two_r, grads, vec_s, vec_r, bup_s, bup_r,
    load_sems, send_sems, recv_sems, upa_s, upb_s, wo_s, qkv_s, *recvs,
):
    rows, width = xp.shape
    loads = []
    for n, src in enumerate((dq_hbm, dk_hbm, dv_hbm)):
        to = grads.at[:, pl.ds(n * width, width)]
        loads.append(pltpu.make_async_copy(src, to, load_sems.at[n]))
    for load in loads:
        load.start()
    links = Links(ndev, parts, send_sems, recv_sems)
    flips = [1 << n for n in range(ndev.bit_length() - 1)]
    links.greet(flips + [(links.shift << 3, links.shift << 4)], False)
    one = Chain(links, one_s, one_r, DN_ONE, 3)
    two = Chain(links, two_s, two_r, DN_TWO, 2)
    recvs = iter(recvs)
    half = 3 * width // 2

    def chain(n, buf, cols=None):
        _, bits, order, step, _, _ = FLATS[n]
        return Flat(links, buf, [next(recvs) for _ in order[step:]], bits, order, step, cols)

    upa, upb, out = (chain(n, buf) for n, buf in enumerate((upa_s, upb_s, wo_s)))
    left = chain(3, qkv_s, slice(0, half))
    right = chain(4, qkv_s, slice(half, 2 * half))

    def begin(chain, keep, got):
        @pl.loop(0, keep.shape[0])
        def _(i):
            chain.buf[i] = both(keep[i], got[i])

        chain.send()

    def begin_flat(chain, keep, got):
        leads = [()]
        for size in keep.shape[:-2]:
            leads = [a + (b,) for a in leads for b in range(size)]

        @pl.loop(0, keep.shape[-2] // 16)
        def _(i):
            at = pl.ds(pl.multiple_of(i * 16, 16), 16)
            for lead in leads:
                index = lead + (at, slice(None))
                chain.buf[index] = both(keep[index], got[index])

        chain.send()

    begin(two, two_keep, two_got)
    begin_flat(upa, upa_keep, upa_got)
    for load in loads:
        load.wait()
    tile = width // 2

    def weights(chain, first_tile):
        @pl.loop(first_tile, first_tile + 3)
        def _(n):
            cols = pl.ds(pl.multiple_of(n * tile, tile), tile)
            part = tn(xp[...], grads[:, cols])
            qkv_s[:, :, :, :, cols] = part.astype(BF16).reshape(2, 2, 2, width // 8, tile)

        chain.send()

    weights(left, 0)
    weights(right, 3)
    begin_flat(upb, upb_keep, upb_got)
    begin_flat(out, wo_keep, wo_got)
    begin(one, one_keep, one_got)
    vec_s[0] = vec[...]
    vec_s[0, 6:7, :] = colsum(grads[:, 0:width].astype(F32))
    vec_s[0, 7:8, :] = colsum(grads[:, 2 * width : 3 * width].astype(F32))
    bup_s[0] = bup[...]

    def vectors(n):
        if n >= len(flips):
            return None
        return [
            links.exchange(vec_s.at[n], vec_r.at[n], flips[n]),
            links.exchange(bup_s.at[n], bup_r.at[n], flips[n]),
        ]

    def add_vectors(n, copies):
        for c in copies:
            c.wait_recv()
        vec_s[n + 1] = vec_s[n] + vec_r[n]
        bup_s[n + 1] = bup_s[n] + bup_r[n]
        return vectors(n + 1)

    pending = vectors(0)
    left.add()
    right.add()

    @pl.loop(0, 2)
    def _(r):
        at = pl.ds(pl.multiple_of(r * (rows // 2), rows // 2), rows // 2)
        total = nt(grads[at, 0:width], wq[...]) + nt(grads[at, width : 2 * width], wk[...])
        total = total + nt(grads[at, 2 * width : 3 * width], wv[...])
        ig_ref[at, :] = (total + fg[at, :]).astype(BF16)

    pending = add_vectors(0, pending)
    two.add()
    upa.add()
    upb.add()
    out.add()
    one.add()
    pending = add_vectors(1, pending)
    left.add()
    right.add()
    pending = add_vectors(2, pending)
    two.add()
    upa.add()
    upb.add()
    out.add()
    one.add()
    left.add()
    right.add()
    pending = add_vectors(3, pending)
    two.add()
    upa.add()
    upb.add()
    out.add()
    dn1_out[...] = one.last()
    dn2_out[...] = two.last()
    up1_out[...] = upa.last()
    up2_out[...] = upb.last()
    wo_out[...] = out.last()
    for n in range(4, len(flips)):
        pending = add_vectors(n, pending)
    vec_out[...] = vec_s[len(flips)]
    bup_out[...] = bup_s[len(flips)]
    left.add()
    right.add()
    mine = left.last()
    q_out[...] = mine[:, 0:width]
    k_out[:, 0:tile] = mine[:, width:]
    mine = right.last()
    k_out[:, tile:] = mine[:, 0:tile]
    v_out[...] = mine[:, tile:]
    links.finish()


FLATS = (
    ("upa", (1,), UP_ONE, 2, 4, 1),
    ("upb", (2, 1), UP_TWO, 2, 4, 2),
    ("out", (1,), OUT_ORDER, 2, 2, 1),
    ("left", (0, 2, 1), LEFT_ORDER, 0, 3, 1),
    ("right", (0, 2, 1), RIGHT_ORDER, 0, 3, 1),
)


def tail(ndev, parts, xp, dq, dk, dv, wq, wk, wv, fg, one, two, upa, upb, wo, vec, bup):
    rows, width = xp.shape
    short = width // BLOCKS
    tall, ff = one[0].shape[1] * 2, upa[0].shape[2] * 2
    steps = ndev.bit_length() - 1

    def out(*shape):
        return jax.ShapeDtypeStruct(shape, F32)

    def chain(step, *shape):
        return [pltpu.VMEM((BLOCKS >> step,) + shape, BF16)] * 2

    flat, received = [], []
    for _, bits, order, step, wide, cut in FLATS:
        cols, tops = wide * width // 2, width // 8 // cut
        flat.append(pltpu.VMEM((2,) * len(bits) + (tops, cols), BF16))
        received += [pltpu.VMEM(u, BF16) for u in flat_recvs(bits, order, step, cols, tops)]
    flat = flat[:3] + [pltpu.VMEM((2, 2, 2, width // 8, 3 * width), BF16)]
    copies = 2 + 3 + 3 * 3 + 2 * 6 + 2 * steps
    return pl.pallas_call(
        functools.partial(tail_kernel, ndev, parts),
        in_specs=[whole()] + [hbm()] * 3 + [whole()] * 16,
        out_specs=[whole()] * 11,
        out_shape=[
            jax.ShapeDtypeStruct((rows, width), BF16),
            out(tall // 2, width), out(tall // 2, width), out(short, ff // 2), out(short, ff // 2),
            out(short, width), out(short, width), out(short, width), out(short, width),
            out(8, width), out(1, ff),
        ],
        scratch_shapes=chain(3, tall // 2, width)
        + chain(2, tall // 2, width)
        + [
            pltpu.VMEM((rows, 3 * width), BF16),
            pltpu.VMEM((steps + 1, 8, width), F32),
            pltpu.VMEM((steps, 8, width), F32),
            pltpu.VMEM((steps + 1, 1, ff), F32),
            pltpu.VMEM((steps, 1, ff), F32),
            pltpu.SemaphoreType.DMA((3,)),
            pltpu.SemaphoreType.DMA((copies,)),
            pltpu.SemaphoreType.DMA((copies,)),
        ] + flat + received,
        compiler_params=remote_params(2, 40),
        cost_estimate=cost(40e9, 16 << 20),
        name="tail",
    )(xp, dq, dk, dv, wq, wk, wv, fg, *one, *two, *upa, *upb, *wo, vec, bup)


def write_kernel(
    ndev, parts, ig, dn1, dn2, up1, up2, wo, q, k, v, vec, bup,
    ig_out, dn_out, up_out, wo_out, q_out, k_out, v_out,
    g2_out, s2_out, db_out, g1_out, s1_out, ob_out, qb_out, vb_out, ub_out,
):
    ig_out[...] = ig[...]
    me = lax.axis_index("dp") * parts + lax.axis_index("seq")
    half = dn1.shape[0]
    dn_out[0:half, :] = dn1[...]
    dn_out[half : 2 * half, :] = dn2[...]
    half = up1.shape[1]
    up_out[:, 0:half] = up1[...]
    up_out[:, half : 2 * half] = up2[...]
    wo_out[...] = wo[...]
    q_out[...] = q[...]
    k_out[...] = k[...]
    v_out[...] = v[...]
    width, ff = vec.shape[1], bup.shape[1]
    mine = width // ndev
    mid = pltpu.roll(vec[...], lax.rem(width - me * mine, width), 1)[:, :128]
    for n, ref in enumerate((g2_out, s2_out, db_out, g1_out, s1_out, ob_out, qb_out, vb_out)):
        ref[...] = mid[n, :mine]
    wide = jnp.broadcast_to(bup[...], (8, ff))
    wide = pltpu.roll(wide, lax.rem(ff - me * (ff // ndev), ff), 1)[:, :128]
    ub_out[...] = wide[0, : ff // ndev]


def write(ndev, parts, ig, dn1, dn2, up1, up2, wo, q, k, v, vec, bup):
    width, ff = vec.shape[1], bup.shape[1]

    def out(*shape):
        return jax.ShapeDtypeStruct(shape, F32)

    shapes = [
        jax.ShapeDtypeStruct(ig.shape, BF16),
        out(2 * dn1.shape[0], width), out(up1.shape[0], ff), out(*wo.shape), out(*q.shape),
        out(*k.shape), out(*v.shape),
    ] + [out(width // ndev)] * 8 + [out(ff // ndev)]
    return pl.pallas_call(
        functools.partial(write_kernel, ndev, parts),
        in_specs=[whole()] * 11,
        out_specs=[whole()] * 16,
        out_shape=shapes,
        compiler_params=params(16 << 20),
        name="write",
    )(ig, dn1, dn2, up1, up2, wo, q, k, v, vec, bup)


def finish(block, ndev):
    rest = ndev >> LEVELS
    if rest == 1:
        return block
    step = 1
    me = lax.axis_index("dp") * lax.axis_size("seq") + lax.axis_index("seq")
    arr = block.reshape(rest, block.shape[0] // rest, block.shape[1])
    flip = rest
    while flip > 1:
        flip //= 2
        bit = (me // flip) % 2
        half = arr.shape[0] // 2
        keep = lax.dynamic_slice_in_dim(arr, bit * half, half, 0)
        send = lax.dynamic_slice_in_dim(arr, (1 - bit) * half, half, 0)
        arr = keep + lax.ppermute(send, AXES, [(i, i ^ flip) for i in range(ndev)])
    return arr[0]


def shards(
    layer_input,
    query_weight,
    query_bias,
    key_weight,
    value_weight,
    value_bias,
    output_weight,
    output_bias,
    first_gain,
    first_shift,
    up_weight,
    up_bias,
    down_weight,
    down_bias,
    second_gain,
    second_shift,
    out_cotangent,
    passage_lengths,
):
    parts = lax.axis_size("seq")
    ndev = parts * lax.axis_size("dp")
    shift = ndev >> LEVELS
    q, k, v, onehot, qmask, bounds, mix, xp = first(
        ndev, parts, layer_input, passage_lengths, query_weight, query_bias, key_weight,
        value_weight, value_bias,
    )
    ctx, lse = attend_forward(bounds, q, k, v, onehot, qmask)
    (
        result, fg, grads, stat, vec, bup, one_keep, one_send, two_keep, two_send, upa_keep,
        upa_send, upb_keep, upb_send, wo_keep, wo_send,
    ) = middle(
        ndev, parts, layer_input, ctx, out_cotangent, output_weight, output_bias, first_gain,
        first_shift, up_weight, up_bias, down_weight, down_bias, second_gain, second_shift, lse, mix,
    )

    def swap(send, bit):
        flip = shift << bit
        return lax.ppermute(send, AXES, [(i, i ^ flip) for i in range(ndev)])

    two = (two_keep, swap(two_send, DN_TWO[1]))
    upa = (upa_keep, swap(upa_send, UP_ONE[1]))
    upb = (upb_keep, swap(upb_send, UP_TWO[1]))
    one = (one_keep, swap(one_send, DN_ONE[2]))
    wo = (wo_keep, swap(wo_send, OUT_ORDER[1]))
    dq, dk, dv = attend_backward(bounds, q, k, v, grads, stat, onehot, qmask)
    sums = tail(
        ndev, parts, xp, dq, dk, dv, query_weight, key_weight, value_weight, fg, one, two, upa,
        upb, wo, vec, bup,
    )
    ig, dn, up, wo, qg, kg, vg, g2g, s2g, db, g1g, s1g, ob, qb, vb, ub = write(ndev, parts, *sums)
    dn, up, wo, qg, kg, vg = (finish(u, ndev) for u in (dn, up, wo, qg, kg, vg))
    return (
        result, ig, qg, qb, kg, vg, vb, wo, ob, g1g, s1g, up, ub, dn, db, g2g, s2g,
    )


def solution(mesh):
    split = P(AXES, None)
    part = P(AXES)
    in_specs = (split,) + (P(),) * 15 + (split, P("dp", None))
    out_specs = (
        split, split, split, part, split, split, part, split, part, part, part,
        split, part, split, part, part, part,
    )
    return jax.shard_map(shards, mesh=mesh, in_specs=in_specs, out_specs=out_specs, check_vma=False)
```

```python
import functools

import jax
import jax.numpy as jnp
from jax import lax
from jax.experimental import pallas as pl
from jax.experimental.pallas import tpu as pltpu
from jax.sharding import PartitionSpec as P

HEAD_DIM = 64
PAIR = 2 * HEAD_DIM
AXES = ("dp", "seq")
NEG = -1e30
FLOOR = -3e38
BQ = 256
BK = 128
LEVELS = 5
layer_eps = 1e-12
F32 = jnp.float32
BF16 = jnp.bfloat16


def nn(a, b):
    return lax.dot_general(a, b, (((1,), (0,)), ((), ())), preferred_element_type=F32)


def nt(a, b):
    return lax.dot_general(a, b, (((1,), (1,)), ((), ())), preferred_element_type=F32)


def tn(a, b):
    return lax.dot_general(a, b, (((0,), (0,)), ((), ())), preferred_element_type=F32)


def cost(flops, nbytes, trans=0):
    return pl.CostEstimate(flops=int(flops), bytes_accessed=int(nbytes), transcendentals=int(trans))


def params(limit=56 << 20):
    return pltpu.CompilerParams(vmem_limit_bytes=limit)


def whole():
    return pl.BlockSpec(memory_space=pltpu.VMEM)


def hbm():
    return pl.BlockSpec(memory_space=pl.ANY)


def low_lanes():
    return lax.broadcasted_iota(jnp.int32, (1, PAIR), 1) < HEAD_DIM


def line(ref):
    return ref[...].reshape(1, -1)


def remote_params(number, mib=60):
    return pltpu.CompilerParams(
        vmem_limit_bytes=mib << 20, collective_id=number, has_side_effects=True
    )


class Links:
    def __init__(self, ndev, parts, send_sems, recv_sems):
        self.ndev, self.parts = ndev, parts
        self.place = lax.axis_index("seq")
        self.row = lax.axis_index("dp")
        self.me = self.row * parts + self.place
        self.shift = ndev >> LEVELS
        self.block = self.me // self.shift
        self.send_sems, self.recv_sems = send_sems, recv_sems
        self.used = 0
        self.started = []
        self.has_prev = self.place > 0
        self.has_next = self.place < parts - 1

    def partner(self, *flips):
        other = self.me
        for flip in flips:
            other = other + (1 - 2 * ((self.me // flip) % 2)) * flip
        return (other // self.parts, other % self.parts)

    def greet(self, flips, neighbours):
        barrier = pltpu.get_barrier_semaphore()

        def signal(device):
            pl.semaphore_signal(
                barrier, inc=1, device_id=device, device_id_type=pl.DeviceIdType.MESH
            )

        for flip in flips:
            signal(self.partner(*(flip if isinstance(flip, tuple) else (flip,))))
        if neighbours:

            @pl.when(self.has_prev)
            def _():
                signal((self.row, self.place - 1))

            @pl.when(self.has_next)
            def _():
                signal((self.row, self.place + 1))

        count = len(flips)
        if neighbours:
            count = count + jnp.minimum(self.place, 1)
            count = count + jnp.minimum(self.parts - 1 - self.place, 1)
        pl.semaphore_wait(barrier, count)

    def make(self, src, dst, device, n=None):
        if n is None:
            n = self.used
            self.used += 1
        return pltpu.make_async_remote_copy(
            src_ref=src, dst_ref=dst, send_sem=self.send_sems.at[n],
            recv_sem=self.recv_sems.at[n], device_id=device,
            device_id_type=pl.DeviceIdType.MESH,
        )

    def exchange(self, src, dst, *flips):
        copy = Copy(self, src, dst, flips)
        copy.now().start()
        self.started.append(copy)
        return copy

    def finish(self):
        for copy in self.started:
            copy.wait_send()

    def neighbours(self, src, at_next, at_prev):
        ahead = self.make(src, at_next, (self.row, self.place + 1))
        back = self.make(src, at_prev, (self.row, self.place - 1))

        @pl.when(self.has_next)
        def _():
            ahead.start()

        @pl.when(self.has_prev)
        def _():
            back.start()

        return ahead, back

    def from_prev(self, pair):
        @pl.when(self.has_prev)
        def _():
            pair[0].wait_recv()

    def from_next(self, pair):
        @pl.when(self.has_next)
        def _():
            pair[1].wait_recv()

    def sent(self, pair):
        @pl.when(self.has_next)
        def _():
            pair[0].wait_send()

        @pl.when(self.has_prev)
        def _():
            pair[1].wait_send()


class Copy:
    def __init__(self, links, src, dst, flips):
        self.links, self.src, self.dst, self.flips = links, src, dst, flips
        self.number = links.used
        links.used += 1

    def now(self):
        src = self.src() if callable(self.src) else self.src
        dst = self.dst() if callable(self.dst) else self.dst
        return self.links.make(src, dst, self.links.partner(*self.flips), self.number)

    def wait_recv(self):
        self.now().wait_recv()

    def wait_send(self):
        self.now().wait_send()


def both(a, b):
    return (a.astype(F32) + b.astype(F32)).astype(BF16)


class Chain:
    def __init__(self, links, buf, recv, order, step):
        self.links, self.buf, self.recv, self.order, self.step = links, buf, recv, order, step
        self.base = 0

    def position(self, c):
        at = 0
        for k, b in enumerate(self.order):
            mine, its = (self.links.block // (1 << b)) % 2, (c // (1 << b)) % 2
            at = at + (mine + its - 2 * mine * its) * (1 << (LEVELS - 1 - k))
        return at

    def send(self):
        self.half = (1 << LEVELS) >> (self.step + 1)
        half, base, buf, recv = self.half, self.base, self.buf, self.recv
        self.copy = self.links.exchange(
            lambda: buf.at[pl.ds(half, half)],
            lambda: recv.at[pl.ds(base, half)],
            self.links.shift << self.order[self.step],
        )

    def begin(self, src):
        self.half = (1 << LEVELS) >> (self.step + 1)
        half, recv = self.half, self.recv
        self.copy = self.links.exchange(
            src, lambda: recv.at[pl.ds(0, half)], self.links.shift << self.order[self.step]
        )

    def receive(self):
        self.copy.wait_recv()
        self.base += self.half
        self.step += 1

    def add(self):
        base, half, buf, recv = self.base, self.half, self.buf, self.recv
        self.receive()
        if half > 1:

            @pl.loop(0, half)
            def _(i):
                buf[i] = both(buf[i], recv[base + i])

            self.send()

    def last(self):
        return self.buf[0].astype(F32) + self.recv[self.base - 1].astype(F32)


class Flat:
    def __init__(self, links, buf, recvs, bits, order, step, cols=None, prefix=()):
        self.links, self.buf, self.recvs = links, buf, list(recvs)
        self.bits, self.order, self.step = bits, order, step
        self.at = [slice(None)] * len(bits)
        self.prefix = prefix
        self.rows = buf.shape[len(prefix) + len(bits)]
        self.cols = slice(None) if cols is None else cols

    def view(self, lead, start, size):
        index = tuple(i if isinstance(i, int) else slice(None) for i in lead)
        buf, index = self.buf, self.prefix + index
        return lambda: buf.at[index + (pl.ds(start, size), self.cols)]

    def send(self):
        bit = self.order[self.step]
        shift = self.links.shift
        self.recv = self.recvs.pop(0)
        if isinstance(bit, tuple):
            self.rows //= 4
            recv = self.recv
            self.copies = [
                self.links.exchange(
                    self.view(self.at, n * self.rows, self.rows),
                    functools.partial(lambda n: recv.at[n - 1], n),
                    *(shift << b for k, b in enumerate(bit) if (n >> (1 - k)) & 1),
                )
                for n in (1, 2, 3)
            ]
            return
        if bit in self.bits:
            lead = list(self.at)
            lead[self.bits.index(bit)] = 1
            src = self.view(lead, 0, self.rows)
            self.at[self.bits.index(bit)] = 0
        else:
            self.rows //= 2
            src = self.view(self.at, self.rows, self.rows)
        self.copies = [self.links.exchange(src, self.recv, shift << bit)]

    def begin(self, src):
        self.recv = self.recvs.pop(0)
        flip = self.links.shift << self.order[self.step]
        self.copies = [self.links.exchange(src, self.recv, flip)]

    def add(self):
        for copy in self.copies:
            copy.wait_recv()
        self.step += 1
        if self.step == len(self.order):
            return
        leads = [()]
        for i in self.at:
            leads = [a + (b,) for a in leads for b in ((0, 1) if i != 0 else (0,))]
        free = [n for n, i in enumerate(self.at) if i != 0]
        buf, recv, cols = self.buf, self.recv, self.cols

        @pl.loop(0, self.rows // 16)
        def _(i):
            at = pl.ds(pl.multiple_of(i * 16, 16), 16)
            for lead in leads:
                from_ = tuple(lead[n] for n in free)
                to = self.prefix + lead + (at, cols)
                buf[to] = both(buf[to], recv[from_ + (at,)])

        self.send()

    def last(self):
        lead = self.prefix + (0,) * len(self.bits)
        total = self.buf[lead + (slice(0, self.rows), self.cols)].astype(F32)
        if isinstance(self.order[-1], tuple):
            for n in range(3):
                total = total + self.recv[n].astype(F32)
            return total
        return total + self.recv[...].astype(F32)


def flat_recvs(bits, order, step, cols, blocks_rows):
    lead, rows = len(bits), blocks_rows
    shapes = []
    for bit in order[step:]:
        if isinstance(bit, tuple):
            shapes.append((3, rows // 4, cols))
            continue
        if bit in bits:
            lead -= 1
        else:
            rows //= 2
        shapes.append((2,) * lead + (rows, cols))
    return shapes


def shuffle(links, width):
    short = width // BLOCKS
    col = lax.broadcasted_iota(jnp.int32, (8, width), 1)
    source = col
    for p in range(BLOCKS):
        c = 0
        for k, b in enumerate(FLAT):
            mine, its = (links.block // (1 << b)) % 2, (p >> (LEVELS - 1 - k)) & 1
            c = c + (mine + its - 2 * mine * its) * (1 << b)
        source = jnp.where(col >= p * short, col + (c - p) * short, source)
    row = lax.broadcasted_iota(jnp.int32, (width, width), 0)
    return (row == source[0:1]).astype(F32).astype(BF16)


FLAT = (0, 2, 1, 3, 4)
DN_ONE = (0, 2, 1, 3, 4)
DN_TWO = (0, 1, 2, 3, 4)
UP_ONE = (0, 2, 1, 3, 4)
UP_TWO = (0, 3, 1, 2, 4)
OUT_ORDER = (0, 3, 2, 1, 4)
LEFT_ORDER = (0, 2, 1, (3, 4))
RIGHT_ORDER = (0, 1, 2, (3, 4))
BLOCKS = 1 << LEVELS


def first_kernel(
    ndev, parts, x_ref, lengths, wq_hbm, bq, wk_hbm, wv_hbm, bv,
    q_hbm, k_hbm, v_hbm, onehot, qmask, bounds, mix, xp,
    halo, wq, wk, wv, q_ref, k_ref, v_ref, load_sems, store_sems, send_sems, recv_sems,
):
    rows, width = x_ref.shape
    count = rows * parts
    loads = [
        pltpu.make_async_copy(src, dst, load_sems.at[n])
        for n, (src, dst) in enumerate(((wq_hbm, wq), (wk_hbm, wk), (wv_hbm, wv)))
    ]
    for load in loads:
        load.start()
    links = Links(ndev, parts, send_sems, recv_sems)
    links.greet([], True)
    pieces = 4
    step = rows // pieces
    pairs = [
        links.neighbours(
            x_ref.at[pl.ds(h * step, step)],
            halo.at[pl.ds(h * step, step)],
            halo.at[pl.ds(2 * rows + h * step, step)],
        )
        for h in range(pieces)
    ]

    @pl.when(jnp.logical_not(links.has_prev))
    def _():
        halo[0:rows, :] = jnp.zeros((rows, width), BF16)

    @pl.when(jnp.logical_not(links.has_next))
    def _():
        halo[2 * rows : 3 * rows, :] = jnp.zeros((rows, width), BF16)

    halo[rows : 2 * rows, :] = x_ref[...]

    for load in loads:
        load.wait()

    def stores(at, n):
        part = pl.ds(at, step)
        return [
            pltpu.make_async_copy(src.at[part], dst.at[part], store_sems.at[n, m])
            for m, (src, dst) in enumerate(((q_ref, q_hbm), (k_ref, k_hbm), (v_ref, v_hbm)))
        ]

    def chunk(t):
        return jnp.where(t < pieces, pieces + t, (t % 2) * 2 * pieces + (t - pieces) // 2)

    def project(t):
        at = pl.multiple_of(chunk(t) * step, step)
        rows_at = pl.ds(at, step)
        x = halo[rows_at, :]
        q_ref[rows_at, :] = (nn(x, wq[...]) + line(bq)).astype(BF16)
        k_ref[rows_at, :] = nn(x, wk[...]).astype(BF16)
        v_ref[rows_at, :] = (nn(x, wv[...]) + line(bv)).astype(BF16)
        for copy in stores(at, t):
            copy.start()

    pl.loop(0, pieces)(project)

    slots = lengths.shape[1]
    ends, total = [], jnp.int32(0)
    for n in range(slots):
        total = total + lengths[0, n]
        ends.append(total)
    start = (links.place - 1) * rows
    lane = lax.broadcasted_iota(jnp.int32, (BQ, PAIR), 1) % HEAD_DIM
    one, none, far = BF16(1.0), BF16(0.0), BF16(NEG)

    @pl.loop(0, 3 * rows // BQ)
    def _(i):
        at = start + i * BQ
        where = at + lax.broadcasted_iota(jnp.int32, (BQ, PAIR), 0)
        seg = jnp.zeros((BQ, PAIR), jnp.int32)
        for end in ends:
            seg = seg + (where >= end).astype(jnp.int32)
        outside = (where < 0) | (where >= count)
        seg = jnp.where(outside, slots, seg)
        match = (seg == lane).astype(F32)
        to = pl.ds(pl.multiple_of(i * BQ, BQ), BQ)
        onehot[to, :] = match.astype(BF16)
        qmask[to, :] = ((1.0 - match) * NEG).astype(BF16)

    mix[...] = shuffle(links, width)
    xp[...] = nn(x_ref[...], mix[...]).astype(BF16)

    for n in range(rows // BQ):
        near = links.place * rows + n * BQ
        far_row = near + BQ - 1
        lo, hi = jnp.int32(0), jnp.int32(count)
        for end in ends:
            lo = jnp.where(end <= near, jnp.maximum(lo, end), lo)
            hi = jnp.where(end > far_row, jnp.minimum(hi, end), hi)
        lo = jnp.maximum(lo - start, 0)
        hi = jnp.minimum(hi - start, 3 * rows)
        bounds[0, n] = lo // BK
        bounds[1, n] = (hi + BK - 1) // BK

    @pl.loop(pieces, 3 * pieces)
    def _(t):
        for h in range(pieces):

            @pl.when(t == pieces + 2 * h)
            def _():
                links.from_prev(pairs[h])

            @pl.when(t == pieces + 1 + 2 * h)
            def _():
                links.from_next(pairs[h])

        project(t)

    for pair in pairs:
        links.sent(pair)

    @pl.loop(0, 3 * pieces)
    def _(t):
        for copy in stores(pl.multiple_of(chunk(t) * step, step), t):
            copy.wait()


def first(ndev, parts, x, lengths, wq, bq, wk, wv, bv):
    rows, width = x.shape
    ext = jax.ShapeDtypeStruct((3 * rows, width), BF16)
    seg = jax.ShapeDtypeStruct((3 * rows, PAIR), BF16)
    smem = pl.BlockSpec(memory_space=pltpu.SMEM)
    return pl.pallas_call(
        functools.partial(first_kernel, ndev, parts),
        in_specs=[whole(), smem, hbm(), whole(), hbm(), hbm(), whole()],
        out_specs=[hbm()] * 3 + [whole()] * 2 + [smem] + [whole()] * 2,
        out_shape=[ext] * 3
        + [seg] * 2
        + [
            jax.ShapeDtypeStruct((2, rows // BQ), jnp.int32),
            jax.ShapeDtypeStruct((width, width), BF16),
            jax.ShapeDtypeStruct((rows, width), BF16),
        ],
        scratch_shapes=[
            pltpu.VMEM((3 * rows, width), BF16),
            pltpu.VMEM((width, width), BF16),
            pltpu.VMEM((width, width), BF16),
            pltpu.VMEM((width, width), BF16),
            pltpu.VMEM((3 * rows, width), BF16),
            pltpu.VMEM((3 * rows, width), BF16),
            pltpu.VMEM((3 * rows, width), BF16),
            pltpu.SemaphoreType.DMA((3,)),
            pltpu.SemaphoreType.DMA((12, 3)),
            pltpu.SemaphoreType.DMA((8,)),
            pltpu.SemaphoreType.DMA((8,)),
        ],
        compiler_params=remote_params(0),
        cost_estimate=cost(15e9, 12 << 20),
        name="first",
    )(x, lengths, wq, bq, wk, wv, bv)


def lengths_of(rows):
    most = BQ // BK + 2 * -(-(rows - 1) // BK)
    return [n for n in range(3, most) if n <= 6 or n % 2 == 0] + [most]


def key_range(bounds, i, rows):
    lo, hi = bounds[0, i], bounds[1, i]
    sizes = lengths_of(rows)
    number = jnp.int32(sizes[-1])
    for n in reversed(sizes):
        number = jnp.where(hi - lo <= n, n, number)
    return jnp.minimum(lo, 3 * rows // BK - number), number


def forward_kernel(bounds, q_ref, k_ref, v_ref, onehot, qmask, ctx_ref, lse_ref, ka, kb):
    rows = ctx_ref.shape[0]
    low = low_lanes()
    key, hot = k_ref[...], onehot[...]
    ka[...] = jnp.where(low, key, hot)
    kb[...] = jnp.where(low, hot, key)

    @pl.loop(0, rows // BQ)
    def _(i):
        first_block, number = key_range(bounds, i, rows)
        base = pl.multiple_of(first_block * BK, BK)
        at = pl.ds(pl.multiple_of(i * BQ, BQ), BQ)
        own = pl.ds(pl.multiple_of(rows + i * BQ, BQ), BQ)
        for num in lengths_of(rows):

            @pl.when(number == num)
            def _():
                span = pl.ds(base, num * BK)
                query = q_ref[own, :] * BF16(HEAD_DIM**-0.5)
                mask = qmask[own, :]
                parts = []
                for head, keys in enumerate((ka, kb)):
                    pick = (query, mask) if head == 0 else (mask, query)
                    scores = nt(jnp.where(low, *pick), keys[span, :])
                    top = jnp.max(scores, axis=1, keepdims=True)
                    weights = jnp.exp(scores - top)
                    total = jnp.sum(weights, axis=1, keepdims=True)
                    acc = nn(weights.astype(BF16), v_ref[span, :])
                    parts.append((acc / total, top + jnp.log(total)))
                ctx_ref[at, :] = jnp.where(low, parts[0][0], parts[1][0])
                flip = jnp.where(low, parts[0][1], parts[1][1]).T
                lse_ref[0, 0:1, at] = flip[0:1]
                lse_ref[0, 1:2, at] = flip[HEAD_DIM : HEAD_DIM + 1]


def attend_forward(bounds, q, k, v, onehot, qmask):
    rows, width = q.shape[0] // 3, q.shape[1]
    pairs = width // PAIR
    ext = pl.BlockSpec((3 * rows, PAIR), lambda p, *_: (0, p))
    seg = pl.BlockSpec((3 * rows, PAIR), lambda p, *_: (0, 0))
    grid = pltpu.PrefetchScalarGridSpec(
        num_scalar_prefetch=1,
        grid=(pairs,),
        in_specs=[ext, ext, ext, seg, seg],
        out_specs=[
            pl.BlockSpec((rows, PAIR), lambda p, *_: (0, p)),
            pl.BlockSpec((1, 2, rows), lambda p, *_: (p, 0, 0)),
        ],
        scratch_shapes=[pltpu.VMEM((3 * rows, PAIR), BF16)] * 2,
    )
    return pl.pallas_call(
        forward_kernel,
        grid_spec=grid,
        out_shape=[
            jax.ShapeDtypeStruct((rows, width), F32),
            jax.ShapeDtypeStruct((pairs, 2, rows), F32),
        ],
        compiler_params=params(),
        cost_estimate=cost(20e9, 24 * rows * width),
        name="attend_forward",
    )(bounds, q, k, v, onehot, qmask)


def norm_forward(h):
    mean = jnp.mean(h, axis=-1, keepdims=True)
    centred = h - mean
    variance = jnp.mean(centred * centred, axis=-1, keepdims=True)
    inverse = lax.rsqrt(variance + layer_eps)
    return centred * inverse, inverse


def norm_backward(grad, gain, hat, inverse):
    g = grad * gain
    return inverse * (
        g - jnp.mean(g, axis=-1, keepdims=True) - hat * jnp.mean(g * hat, axis=-1, keepdims=True)
    )


def colsum(v):
    return jnp.sum(v, axis=0, keepdims=True)


def middle_kernel(
    ndev, parts,
    x_ref, ctx_ref, ct_ref, wo, bo, g1, s1, wup_hbm, bup, wdn_hbm, bdn, g2, s2, lse_ref, mix,
    result_hbm, fg_hbm, g_hbm, stat_ref, vec_ref, bup_ref,
    one_keep_hbm, one_send_hbm, two_keep_hbm, two_send_hbm, upa_keep_hbm, upa_send_hbm, upb_keep_hbm,
    upb_send_hbm, wo_keep_hbm, wo_send_hbm,
    wup, wdn, hid, nl, nlp, bg, cl, ag, slope, normed, inv, acc, grad_s,
    result_ref, fg_ref, g_ref,
    one_s, one_r, two_s, two_r, up_s, up_r, wo_s, wo_r,
    load_sems, store_sems, send_sems, recv_sems,
):
    stores = []

    def store(src, dst):
        copy = pltpu.make_async_copy(src, dst, store_sems.at[len(stores)])
        copy.start()
        stores.append(copy)

    rows, width = x_ref.shape
    ff = wup.shape[1]
    rc, fc = 256, 1536
    chunks, tiles = rows // rc, ff // fc
    tall, short = ff // BLOCKS, width // BLOCKS
    up_copy = pltpu.make_async_copy(wup_hbm, wup, load_sems.at[0])
    dn_copy = pltpu.make_async_copy(wdn_hbm, wdn, load_sems.at[1])
    up_copy.start()
    dn_copy.start()
    links = Links(ndev, parts, send_sems, recv_sems)
    links.greet([links.shift << DN_ONE[0], links.shift << DN_ONE[1]], True)
    one = Chain(links, one_s, one_r, DN_ONE, 0)
    two = Chain(links, two_s, two_r, DN_TWO, 0)
    @pl.loop(0, chunks)
    def _(r):
        at = pl.ds(pl.multiple_of(r * rc, rc), rc)
        c_low = ctx_ref[at, :].astype(BF16)
        cl[at, :] = nn(c_low, mix[...]).astype(BF16)
        h = x_ref[at, :].astype(F32) + (nn(c_low, wo[...]) + line(bo))
        xhat, inverse = norm_forward(h)
        res = xhat * line(g1) + line(s1)
        fg_ref[at, :] = xhat
        inv[at, :] = inverse
        normed[at, :] = res
        low = res.astype(BF16)
        nl[at, :] = low
        nlp[at, :] = nn(low, mix[...]).astype(BF16)

    up_copy.wait()
    dn_copy.wait()
    acc[...] = jnp.zeros_like(acc)

    @pl.loop(0, tiles)
    def _(j):
        cols = pl.ds(pl.multiple_of(j * fc, fc), fc)
        bias = bup[cols].reshape(1, fc)

        @pl.loop(0, chunks)
        def _(r):
            at = pl.ds(pl.multiple_of(r * rc, rc), rc)
            up = nn(nl[at, :], wup[:, cols]) + bias
            cdf = 0.5 * (1.0 + lax.erf(up * F32(0.5**0.5)))
            density = jnp.exp(-0.5 * up * up) * F32(0.3989422804014327)
            slope[at, cols] = cdf + up * density
            act = (up * cdf).astype(BF16)
            hid[at, cols] = act
            acc[at, :] = acc[at, :] + nn(act, wdn[cols, :])

    vec_ref[...] = jnp.zeros_like(vec_ref)

    @pl.loop(0, chunks)
    def _(r):
        at = pl.ds(pl.multiple_of(r * rc, rc), rc)
        xhat, inverse = norm_forward(normed[at, :] + (acc[at, :] + line(bdn)))
        result_ref[at, :] = (xhat * line(g2) + line(s2)).astype(BF16)
        ct = ct_ref[at, :].astype(F32)
        second = norm_backward(ct, line(g2), xhat, inverse)
        low = second.astype(BF16)
        bg[at, :] = low
        acc[at, :] = second
        vec_ref[0:1, :] = vec_ref[0:1, :] + colsum(ct * xhat)
        vec_ref[1:2, :] = vec_ref[1:2, :] + colsum(ct)
        vec_ref[2:3, :] = vec_ref[2:3, :] + colsum(low.astype(F32))

    store(result_ref, result_hbm)

    some = width // tall

    @pl.loop(0, ff // width)
    def _(j):
        grad_s[...] = tn(hid[:, pl.ds(pl.multiple_of(j * width, width), width)], bg[...])

        @pl.loop(0, some)
        def _(c):
            base = pl.multiple_of(c * tall, tall // 2)
            one_s[one.position(j * some + c)] = grad_s[pl.ds(base, tall // 2), :].astype(BF16)
            base = pl.multiple_of(c * tall + tall // 2, tall // 2)
            two_s[two.position(j * some + c)] = grad_s[pl.ds(base, tall // 2), :].astype(BF16)

    one.send()
    two.send()

    def back_tiles(lo, hi):
        @pl.loop(lo, hi)
        def _(j):
            cols = pl.ds(pl.multiple_of(j * fc, fc), fc)
            bup_ref[:, cols] = jnp.zeros((1, fc), F32)

            @pl.loop(0, chunks)
            def _(r):
                at = pl.ds(pl.multiple_of(r * rc, rc), rc)
                grad = (nt(bg[at, :], wdn[cols, :]) * slope[at, cols]).astype(BF16)
                hid[at, cols] = grad
                bup_ref[:, cols] = bup_ref[:, cols] + colsum(grad.astype(F32))
                acc[at, :] = acc[at, :] + nt(grad, wup[:, cols])

    back_tiles(0, tiles - 1)
    one.add()
    back_tiles(tiles - 1, tiles)

    zero_prev = pltpu.make_async_copy(
        result_ref, g_hbm.at[pl.ds(0, rows)], store_sems.at[store_sems.shape[0] - 2]
    )
    zero_next = pltpu.make_async_copy(
        result_ref, g_hbm.at[pl.ds(2 * rows, rows)], store_sems.at[store_sems.shape[0] - 1]
    )
    stores.pop().wait()
    result_ref[...] = jnp.zeros_like(result_ref)

    @pl.when(jnp.logical_not(links.has_prev))
    def _():
        zero_prev.start()
        stat_ref[:, :, 0:rows] = jnp.zeros((width // PAIR, 4, rows), F32)

    @pl.when(jnp.logical_not(links.has_next))
    def _():
        zero_next.start()
        stat_ref[:, :, 2 * rows : 3 * rows] = jnp.zeros((width // PAIR, 4, rows), F32)

    pairs = []
    for r in range(chunks):
        at = slice(r * rc, (r + 1) * rc)
        mid = slice(rows + r * rc, rows + (r + 1) * rc)
        total = acc[at, :]
        xhat = fg_ref[at, :]
        first_grad = norm_backward(total, line(g1), xhat, inv[at, :])
        fg_ref[at, :] = first_grad
        low = first_grad.astype(BF16)
        ag[at, :] = low
        vec_ref[3:4, :] = vec_ref[3:4, :] + colsum(total * xhat)
        vec_ref[4:5, :] = vec_ref[4:5, :] + colsum(total)
        vec_ref[5:6, :] = vec_ref[5:6, :] + colsum(low.astype(F32))
        cg = nt(low, wo[...]).astype(BF16)
        g_ref[at, :] = cg
        pairs.append(links.neighbours(
            g_ref.at[pl.ds(r * rc, rc)],
            g_hbm.at[pl.ds(r * rc, rc)],
            g_hbm.at[pl.ds(2 * rows + r * rc, rc)],
        ))
        prod = cg.astype(F32) * ctx_ref[at, :]
        for p in range(width // PAIR):
            flip = prod[:, p * PAIR : (p + 1) * PAIR].T
            stat_ref[p, 2:3, mid] = colsum(flip[:HEAD_DIM])
            stat_ref[p, 3:4, mid] = colsum(flip[HEAD_DIM:])
    store(g_ref, g_hbm.at[pl.ds(rows, rows)])
    store(fg_ref, fg_hbm)
    for p in range(width // PAIR):
        stat_ref[p, 0:2, rows : 2 * rows] = lse_ref[p]
    pairs.append(links.neighbours(
        stat_ref.at[:, :, pl.ds(rows, rows)],
        stat_ref.at[:, :, pl.ds(0, rows)],
        stat_ref.at[:, :, pl.ds(2 * rows, rows)],
    ))

    quarter = width // 8
    ups = []
    for n in range(2):

        @pl.loop(0, 2)
        def _(t):
            cols = pl.ds(pl.multiple_of(n * (ff // 2) + t * width, width), width)
            grad = tn(nlp[...], hid[:, cols])
            up_s[:, :, :, :, cols] = grad.astype(BF16).reshape(2, 2, 2, quarter, width)

        cols = pl.ds(n * (ff // 2), ff // 2)
        ups.append(links.exchange(
            up_s.at[1, :, :, :, cols], up_r.at[:, :, :, cols], links.shift << FLAT[0]
        ))

    wo_s[...] = tn(cl[...], ag[...]).astype(BF16).reshape(2, 2, 2, quarter, width)
    out = links.exchange(wo_s.at[1], wo_r, links.shift << FLAT[0])

    def settle(chain, keep, send):
        chain.receive()
        half, quarter = BLOCKS // 2, BLOCKS // 4

        @pl.loop(0, half)
        def _(i):
            chain.recv[i] = both(chain.buf[i], chain.recv[i])

        store(chain.recv.at[pl.ds(0, quarter)], keep)
        store(chain.recv.at[pl.ds(quarter, quarter)], send)

    settle(two, two_keep_hbm, two_send_hbm)

    def settle_flat(copy, mine, got, cols):
        copy.wait_recv()

        @pl.loop(0, quarter // 16)
        def _(i):
            at = pl.ds(pl.multiple_of(i * 16, 16), 16)
            for x_bit in range(2):
                for y_bit in range(2):
                    index = (x_bit, y_bit, at, cols)
                    got[index] = both(mine[(0,) + index], got[index])

    left, right = pl.ds(0, ff // 2), pl.ds(ff // 2, ff // 2)
    settle_flat(ups[0], up_s, up_r, left)
    store(up_r.at[0, :, :, left], upa_keep_hbm)
    store(up_r.at[1, :, :, left], upa_send_hbm)
    settle_flat(ups[1], up_s, up_r, right)
    store(up_r.at[:, :, pl.ds(0, quarter // 2), right], upb_keep_hbm)
    store(up_r.at[:, :, pl.ds(quarter // 2, quarter // 2), right], upb_send_hbm)
    settle_flat(out, wo_s, wo_r, slice(None))
    store(wo_r.at[:, :, pl.ds(0, quarter // 2)], wo_keep_hbm)
    store(wo_r.at[:, :, pl.ds(quarter // 2, quarter // 2)], wo_send_hbm)
    one.receive()

    @pl.loop(0, BLOCKS // 4)
    def _(i):
        one_s[i] = both(one_s[i], one_r[BLOCKS // 2 + i])

    store(one_s.at[pl.ds(0, BLOCKS // 8)], one_keep_hbm)
    store(one_s.at[pl.ds(BLOCKS // 8, BLOCKS // 8)], one_send_hbm)
    for copy in stores:
        copy.wait()

    @pl.when(jnp.logical_not(links.has_prev))
    def _():
        zero_prev.wait()

    @pl.when(jnp.logical_not(links.has_next))
    def _():
        zero_next.wait()

    for pair in pairs:
        links.from_prev(pair)
        links.from_next(pair)
        links.sent(pair)
    links.finish()


def middle(ndev, parts, x, ctx, ct, wo, bo, g1, s1, wup, bup, wdn, bdn, g2, s2, lse, mix):
    rows, width = x.shape
    ff = wup.shape[1]
    pairs = width // PAIR
    tall, short = ff // BLOCKS, width // BLOCKS
    left = BLOCKS // 4

    def out(*shape, dtype=BF16):
        return jax.ShapeDtypeStruct(shape, dtype)

    shapes = [
        out(rows, width),
        out(rows, width, dtype=F32),
        out(3 * rows, width),
        out(pairs, 4, 3 * rows, dtype=F32),
        out(8, width, dtype=F32),
        out(1, ff, dtype=F32),
        out(left // 2, tall // 2, width),
        out(left // 2, tall // 2, width),
        out(left, tall // 2, width),
        out(left, tall // 2, width),
        out(2, width // 8, ff // 2),
        out(2, width // 8, ff // 2),
        out(2, 2, width // 16, ff // 2),
        out(2, 2, width // 16, ff // 2),
        out(2, 2, width // 16, width),
        out(2, 2, width // 16, width),
    ]

    def chain(*shape):
        return [pltpu.VMEM((BLOCKS,) + shape, BF16), pltpu.VMEM((BLOCKS // 2,) + shape, BF16)]

    dn_one = chain(tall // 2, width)
    dn_one[1] = pltpu.VMEM((3 * BLOCKS // 4, tall // 2, width), BF16)
    copies = 6 + 6
    return pl.pallas_call(
        functools.partial(middle_kernel, ndev, parts),
        in_specs=[whole()] * 7 + [hbm(), whole(), hbm()] + [whole()] * 5,
        out_specs=[hbm()] * 3 + [whole()] * 3 + [hbm()] * 10,
        out_shape=shapes,
        scratch_shapes=[
            pltpu.VMEM((width, ff), BF16),
            pltpu.VMEM((ff, width), BF16),
            pltpu.VMEM((rows, ff), BF16),
            pltpu.VMEM((rows, width), BF16),
            pltpu.VMEM((rows, width), BF16),
            pltpu.VMEM((rows, width), BF16),
            pltpu.VMEM((rows, width), BF16),
            pltpu.VMEM((rows, width), BF16),
            pltpu.VMEM((rows, ff), F32),
            pltpu.VMEM((rows, width), F32),
            pltpu.VMEM((rows, 1), F32),
            pltpu.VMEM((rows, width), F32),
            pltpu.VMEM((width, width), F32),
            pltpu.VMEM((rows, width), BF16),
            pltpu.VMEM((rows, width), F32),
            pltpu.VMEM((rows, width), BF16),
        ]
        + dn_one + chain(tall // 2, width)
        + [
            pltpu.VMEM((2, 2, 2, width // 8, ff), BF16),
            pltpu.VMEM((2, 2, width // 8, ff), BF16),
            pltpu.VMEM((2, 2, 2, width // 8, width), BF16),
            pltpu.VMEM((2, 2, width // 8, width), BF16),
        ]
        + [
            pltpu.SemaphoreType.DMA((2,)),
            pltpu.SemaphoreType.DMA((15,)),
            pltpu.SemaphoreType.DMA((copies,)),
            pltpu.SemaphoreType.DMA((copies,)),
        ],
        compiler_params=remote_params(1),
        cost_estimate=cost(50e9, 30 << 20),
        name="middle",
    )(x, ctx, ct, wo, bo, g1, s1, wup, bup, wdn, bdn, g2, s2, lse, mix)


GROUPS = 3


def last_kernel(
    ndev, parts,
    q_hbm, k_hbm, v_hbm, g_hbm, stat_hbm, onehot_hbm, qmask_hbm, xp_hbm, wq_hbm, wk_hbm, wv_hbm,
    fg_hbm,
    one_keep, one_send, two_keep, two_send, upa_keep, upa_send, upb_keep, upb_send, wo_keep,
    wo_send, vec, bup,
    ig_ref, dn1_out, dn2_out, up1_out, up2_out, wo_out, q_out, k_out, v_out, vec_out, bup_out,
    q_ref, k_ref, v_ref, g_ref, stat_ref, onehot, qmask, xp, keys, queries, grads, wq, wk, wv, fg,
    one_s, one_r, two_s, two_r, vec_s, vec_r, bup_s, bup_r,
    small_sems, ext_sems, load_sems, send_sems, recv_sems, upa_s, upb_s, wo_s, qkv_s, *recvs,
):
    rows, width = xp.shape
    wide = width // GROUPS
    pairs = wide // PAIR
    exts = ((q_hbm, q_ref), (k_hbm, k_ref), (v_hbm, v_ref), (g_hbm, g_ref))

    def ext_loads(t):
        cols = pl.ds(pl.multiple_of(t * wide, wide), wide)
        return [
            pltpu.make_async_copy(src.at[:, cols], dst.at[:, cols], ext_sems.at[t, n])
            for n, (src, dst) in enumerate(exts)
        ]

    small = [
        pltpu.make_async_copy(src, dst, small_sems.at[n])
        for n, (src, dst) in enumerate((
            (onehot_hbm, onehot), (qmask_hbm, qmask), (stat_hbm, stat_ref), (xp_hbm, xp)
        ))
    ]
    for load in small:
        load.start()
    for t in range(GROUPS):
        for load in ext_loads(t):
            load.start()
    links = Links(ndev, parts, send_sems, recv_sems)
    flips = [1 << n for n in range(ndev.bit_length() - 1)]
    links.greet(flips + [(links.shift << 3, links.shift << 4)], False)
    one = Chain(links, one_s, one_r, DN_ONE, 2)
    two = Chain(links, two_s, two_r, DN_TWO, 1)
    recvs = iter(recvs)
    half = width // 2

    def chain(n, buf, cols=None, prefix=()):
        _, bits, order, step, _, _ = FLATS[n]
        got = [next(recvs) for _ in order[step:]]
        return Flat(links, buf, got, bits, order, step, cols, prefix)

    upa, upb, out = (chain(n, buf) for n, buf in enumerate((upa_s, upb_s, wo_s)))
    left, right = [], []
    for t in range(GROUPS):
        left.append(chain(3, qkv_s, slice(0, half), (t,)))
        right.append(chain(4, qkv_s, slice(half, width), (t,)))
    loads = []
    for src, dst in (
        (two_keep, two_s), (upa_keep, upa_s), (upb_keep, upb_s), (wo_keep, wo_s),
        (one_keep, one_s), (wq_hbm, wq), (wk_hbm, wk), (wv_hbm, wv), (fg_hbm, fg),
    ):
        loads.append(pltpu.make_async_copy(src, dst, load_sems.at[len(loads)]))
        loads[-1].start()
    two.begin(two_send)
    upa.begin(upa_send)
    upb.begin(upb_send)
    out.begin(wo_send)
    one.begin(one_send)

    low = low_lanes()
    zero = jnp.zeros((1, PAIR), BF16)
    scale = BF16(HEAD_DIM**-0.5)
    window = BQ + 2 * BK * -(-(rows - 1) // BK)

    def pick(head, value, other):
        return jnp.where(low, value, other) if head == 0 else jnp.where(low, other, value)

    def attend(t, i):
        at = pl.ds(pl.multiple_of(i * BQ, BQ), BQ)
        own = pl.ds(pl.multiple_of(rows + i * BQ, BQ), BQ)
        span = pl.ds(pl.multiple_of(rows + BQ * i - (window - BQ) // 2, BK), window)
        for n in range(pairs):
            first_col = t * wide + n * PAIR
            cols = pl.ds(pl.multiple_of(first_col, PAIR), PAIR)

            @pl.when(i == 0)
            def _():
                for head in range(2):
                    keys[n, head] = pick(head, k_ref[:, cols], onehot[...])
                    queries[n, head] = pick(head, q_ref[:, cols] * scale, qmask[...])

            mine = stat_ref[t * pairs + n, :, own]
            columns = jnp.concatenate([mine, mine], axis=0).T
            dqs, dks, dvs = [], [], []
            for head in range(2):
                grad = pick(head, g_ref[own, cols], zero)
                scores = nt(queries[n, head, own, :], keys[n, head, span, :])
                prob_grad = nt(grad, v_ref[span, cols])
                probs = jnp.exp(scores - columns[:, head : head + 1])
                delta = columns[:, 2 + head : 3 + head]
                score_grad = (probs * (prob_grad - delta)).astype(BF16)
                dqs.append(nn(score_grad, k_ref[span, cols]))
            for head in range(2):
                val = pick(head, v_ref[own, cols], zero)
                scores = nt(keys[n, head, own, :], queries[n, head, span, :])
                prob_grad = nt(val, g_ref[span, cols])
                probs = jnp.exp(scores - stat_ref[t * pairs + n, head : head + 1, span])
                delta = stat_ref[t * pairs + n, 2 + head : 3 + head, span]
                score_grad = (probs * (prob_grad - delta)).astype(BF16)
                dks.append(nn(score_grad, q_ref[span, cols] * scale))
                dvs.append(nn(probs.astype(BF16), g_ref[span, cols]))
            dq = jnp.where(low, dqs[0], dqs[1]) * F32(HEAD_DIM**-0.5)
            grads[at, cols] = dq.astype(BF16)
            at_k = pl.ds(pl.multiple_of(width + first_col, PAIR), PAIR)
            grads[at, at_k] = jnp.where(low, dks[0], dks[1]).astype(BF16)
            at_v = pl.ds(pl.multiple_of(2 * width + first_col, PAIR), PAIR)
            grads[at, at_v] = jnp.where(low, dvs[0], dvs[1]).astype(BF16)

    def weights(t):
        for n in range(3):
            cols = pl.ds(pl.multiple_of(n * width + t * wide, wide), wide)
            part = tn(xp[...], grads[:, cols])
            part = part.astype(BF16).reshape(2, 2, 2, width // 8, wide)
            qkv_s[t, :, :, :, :, n * wide : (n + 1) * wide] = part

    def group_send(t):
        left[t].send()
        right[t].send()

    def group_add(t):
        left[t].add()
        right[t].add()

    def group_last(t):
        group_add(t)
        cols = slice(t * wide, (t + 1) * wide)
        mine = left[t].last()
        q_out[:, cols] = mine[:, 0:wide]
        k_out[:, t * wide : t * wide + half - wide] = mine[:, wide:]
        mine = right[t].last()
        k_out[:, t * wide + half - wide : (t + 1) * wide] = mine[:, 0 : 2 * wide - half]
        v_out[:, cols] = mine[:, 2 * wide - half :]

    sums = (two, upa, upb, out)

    def settle():
        for c in sums:
            c.add()

    def step_one():
        group_send(0)
        for load in loads[:5]:
            load.wait()
        one.add()

    def step_two():
        settle()
        one.add()
        group_add(0)

    def step_three():
        group_send(1)
        group_add(0)

    def step_four():
        settle()
        group_add(1)
        group_add(0)
        one.add()

    def step_five():
        group_send(2)
        settle()
        group_add(1)

    steps = {1: step_one, 2: step_two, 3: step_three, 4: step_four,
             5: step_five}

    for load in small:
        load.wait()

    @pl.loop(0, 2 * GROUPS)
    def _(u):
        t, i = u // 2, u % 2

        @pl.when(i == 0)
        def _():
            for load in ext_loads(t):
                load.wait()

        attend(t, i)

        @pl.when(i == 1)
        def _():
            weights(t)

        for n, work in steps.items():

            @pl.when(u == n)
            def _():
                work()

    vec_s[0] = vec[...]
    vec_s[0, 6:7, :] = colsum(grads[:, 0:width].astype(F32))
    vec_s[0, 7:8, :] = colsum(grads[:, 2 * width : 3 * width].astype(F32))
    bup_s[0] = bup[...]

    def vectors(n):
        if n >= len(flips):
            return None
        return [
            links.exchange(vec_s.at[n], vec_r.at[n], flips[n]),
            links.exchange(bup_s.at[n], bup_r.at[n], flips[n]),
        ]

    def add_vectors(n, copies):
        for c in copies:
            c.wait_recv()
        vec_s[n + 1] = vec_s[n] + vec_r[n]
        bup_s[n + 1] = bup_s[n] + bup_r[n]
        return vectors(n + 1)

    pending = vectors(0)
    group_add(2)
    for load in loads[5:]:
        load.wait()

    @pl.loop(0, 2)
    def _(r):
        at = pl.ds(pl.multiple_of(r * (rows // 2), rows // 2), rows // 2)
        total = nt(grads[at, 0:width], wq[...]) + nt(grads[at, width : 2 * width], wk[...])
        total = total + nt(grads[at, 2 * width : 3 * width], wv[...])
        ig_ref[at, :] = (total + fg[at, :]).astype(BF16)

    pending = add_vectors(0, pending)
    group_add(2)
    pending = add_vectors(1, pending)
    group_add(1)
    pending = add_vectors(2, pending)
    group_add(2)
    settle()
    group_last(0)
    dn1_out[...] = one.last()
    dn2_out[...] = two.last()
    up1_out[...] = upa.last()
    up2_out[...] = upb.last()
    wo_out[...] = out.last()
    pending = add_vectors(3, pending)
    group_last(1)
    for n in range(4, len(flips)):
        pending = add_vectors(n, pending)
    vec_out[...] = vec_s[len(flips)]
    bup_out[...] = bup_s[len(flips)]
    group_last(2)
    links.finish()


FLATS = (
    ("upa", (1,), UP_ONE, 1, 4, 1),
    ("upb", (2, 1), UP_TWO, 1, 4, 2),
    ("out", (2, 1), OUT_ORDER, 1, 2, 2),
    ("left", (0, 2, 1), LEFT_ORDER, 0, 1, 1),
    ("right", (0, 2, 1), RIGHT_ORDER, 0, 1, 1),
)


def last(
    ndev, parts, q, k, v, g, stat, onehot, qmask, xp, wq, wk, wv, fg, one, two, upa, upb, wo, vec,
    bup,
):
    rows, width = xp.shape
    short = width // BLOCKS
    wide = width // GROUPS
    tall, ff = one[0].shape[1] * 2, upa[0].shape[2] * 2
    steps = ndev.bit_length() - 1

    def out(*shape):
        return jax.ShapeDtypeStruct(shape, F32)

    def vmem(*shape, dtype=BF16):
        return pltpu.VMEM(shape, dtype)

    def chain(step, *shape):
        return [vmem(BLOCKS >> (step + 1), *shape), vmem(BLOCKS >> step, *shape)]

    flat, received = [], []
    for name, bits, order, step, cols, cut in FLATS:
        cols, tops = cols * width // 2, width // 8 // cut
        shape = (2,) * len(bits) + (tops, cols)
        if step:
            flat.append(vmem(*shape))
            received.append([vmem(*shape)])
        else:
            received.append([])
        more = order[1 if step else 0 :]
        if step:
            more = order[step + 1 :]
        received[-1] += [vmem(*u) for u in flat_recvs(bits, more, 0, cols, tops)]
    groups = received[:3] + received[3:] * GROUPS
    received = [u for group in groups for u in group]
    flat.append(vmem(GROUPS, 2, 2, 2, width // 8, width))
    copies = 3 + 4 + 3 * 4 + 2 * GROUPS * 6 + 2 * steps
    explicit = pl.BlockSpec(memory_space=pltpu.HBM)
    return pl.pallas_call(
        functools.partial(last_kernel, ndev, parts),
        in_specs=[explicit] * 22 + [whole()] * 2,
        out_specs=[whole()] * 11,
        out_shape=[
            jax.ShapeDtypeStruct((rows, width), BF16),
            out(tall // 2, width), out(tall // 2, width), out(short, ff // 2), out(short, ff // 2),
            out(short, width), out(short, width), out(short, width), out(short, width),
            out(8, width), out(1, ff),
        ],
        scratch_shapes=[vmem(3 * rows, width)] * 4
        + [vmem(width // PAIR, 4, 3 * rows, dtype=F32)]
        + [vmem(3 * rows, PAIR)] * 2
        + [vmem(rows, width)]
        + [vmem(wide // PAIR, 2, 3 * rows, PAIR)] * 2
        + [vmem(rows, 3 * width)]
        + [vmem(width, width)] * 3
        + [vmem(rows, width, dtype=F32)]
        + chain(2, tall // 2, width)
        + chain(1, tall // 2, width)
        + [
            vmem(steps + 1, 8, width, dtype=F32),
            vmem(steps, 8, width, dtype=F32),
            vmem(steps + 1, 1, ff, dtype=F32),
            vmem(steps, 1, ff, dtype=F32),
            pltpu.SemaphoreType.DMA((4,)),
            pltpu.SemaphoreType.DMA((GROUPS, 4)),
            pltpu.SemaphoreType.DMA((9,)),
            pltpu.SemaphoreType.DMA((copies,)),
            pltpu.SemaphoreType.DMA((copies,)),
        ] + flat + received,
        compiler_params=remote_params(2),
        cost_estimate=cost(60e9, 16 << 20),
        name="last",
    )(
        q, k, v, g, stat, onehot, qmask, xp, wq, wk, wv, fg, *one, *two, *upa, *upb, *wo, vec, bup
    )


def write_kernel(
    ndev, parts, ig, dn1, dn2, up1, up2, wo, q, k, v, vec, bup,
    ig_out, dn_out, up_out, wo_out, q_out, k_out, v_out,
    g2_out, s2_out, db_out, g1_out, s1_out, ob_out, qb_out, vb_out, ub_out,
):
    ig_out[...] = ig[...]
    me = lax.axis_index("dp") * parts + lax.axis_index("seq")
    half = dn1.shape[0]
    dn_out[0:half, :] = dn1[...]
    dn_out[half : 2 * half, :] = dn2[...]
    half = up1.shape[1]
    up_out[:, 0:half] = up1[...]
    up_out[:, half : 2 * half] = up2[...]
    wo_out[...] = wo[...]
    q_out[...] = q[...]
    k_out[...] = k[...]
    v_out[...] = v[...]
    width, ff = vec.shape[1], bup.shape[1]
    mine = width // ndev
    mid = pltpu.roll(vec[...], lax.rem(width - me * mine, width), 1)[:, :128]
    for n, ref in enumerate((g2_out, s2_out, db_out, g1_out, s1_out, ob_out, qb_out, vb_out)):
        ref[...] = mid[n, :mine]
    wide = jnp.broadcast_to(bup[...], (8, ff))
    wide = pltpu.roll(wide, lax.rem(ff - me * (ff // ndev), ff), 1)[:, :128]
    ub_out[...] = wide[0, : ff // ndev]


def write(ndev, parts, ig, dn1, dn2, up1, up2, wo, q, k, v, vec, bup):
    width, ff = vec.shape[1], bup.shape[1]

    def out(*shape):
        return jax.ShapeDtypeStruct(shape, F32)

    shapes = [
        jax.ShapeDtypeStruct(ig.shape, BF16),
        out(2 * dn1.shape[0], width), out(up1.shape[0], ff), out(*wo.shape), out(*q.shape),
        out(*k.shape), out(*v.shape),
    ] + [out(width // ndev)] * 8 + [out(ff // ndev)]
    return pl.pallas_call(
        functools.partial(write_kernel, ndev, parts),
        in_specs=[whole()] * 11,
        out_specs=[whole()] * 16,
        out_shape=shapes,
        compiler_params=params(),
        name="write",
    )(ig, dn1, dn2, up1, up2, wo, q, k, v, vec, bup)


def finish(block, ndev):
    rest = ndev >> LEVELS
    if rest == 1:
        return block
    step = 1
    me = lax.axis_index("dp") * lax.axis_size("seq") + lax.axis_index("seq")
    arr = block.reshape(rest, block.shape[0] // rest, block.shape[1])
    flip = rest
    while flip > 1:
        flip //= 2
        bit = (me // flip) % 2
        half = arr.shape[0] // 2
        keep = lax.dynamic_slice_in_dim(arr, bit * half, half, 0)
        send = lax.dynamic_slice_in_dim(arr, (1 - bit) * half, half, 0)
        arr = keep + lax.ppermute(send, AXES, [(i, i ^ flip) for i in range(ndev)])
    return arr[0]


def shards(
    layer_input,
    query_weight,
    query_bias,
    key_weight,
    value_weight,
    value_bias,
    output_weight,
    output_bias,
    first_gain,
    first_shift,
    up_weight,
    up_bias,
    down_weight,
    down_bias,
    second_gain,
    second_shift,
    out_cotangent,
    passage_lengths,
):
    parts = lax.axis_size("seq")
    ndev = parts * lax.axis_size("dp")
    q, k, v, onehot, qmask, bounds, mix, xp = first(
        ndev, parts, layer_input, passage_lengths, query_weight, query_bias, key_weight,
        value_weight, value_bias,
    )
    ctx, lse = attend_forward(bounds, q, k, v, onehot, qmask)
    (
        result, fg, grads, stat, vec, bup, one_keep, one_send, two_keep, two_send, upa_keep,
        upa_send, upb_keep, upb_send, wo_keep, wo_send,
    ) = middle(
        ndev, parts, layer_input, ctx, out_cotangent, output_weight, output_bias, first_gain,
        first_shift, up_weight, up_bias, down_weight, down_bias, second_gain, second_shift, lse, mix,
    )

    sums = last(
        ndev, parts, q, k, v, grads, stat, onehot, qmask, xp, query_weight, key_weight,
        value_weight, fg, (one_keep, one_send), (two_keep, two_send), (upa_keep, upa_send),
        (upb_keep, upb_send), (wo_keep, wo_send), vec, bup,
    )
    ig, dn, up, wo, qg, kg, vg, g2g, s2g, db, g1g, s1g, ob, qb, vb, ub = write(ndev, parts, *sums)
    dn, up, wo, qg, kg, vg = (finish(u, ndev) for u in (dn, up, wo, qg, kg, vg))
    return (
        result, ig, qg, qb, kg, vg, vb, wo, ob, g1g, s1g, up, ub, dn, db, g2g, s2g,
    )


def solution(mesh):
    split = P(AXES, None)
    part = P(AXES)
    in_specs = (split,) + (P(),) * 15 + (split, P("dp", None))
    out_specs = (
        split, split, split, part, split, split, part, split, part, part, part,
        split, part, split, part, part, part,
    )
    return jax.shard_map(shards, mesh=mesh, in_specs=in_specs, out_specs=out_specs, check_vma=False)
```
